32 devices in a mesh: dp: 2 (over core), head: 4 (over y, x), seq: 4 (over z).
Axes of the slice: x: 2, y: 2, z: 4, core: 2. Of those that a mesh axis runs over, the one named last changes fastest.
Arguments:
- layer_input: bfloat16 [2, 2048, 2048], P('dp', 'seq'), may hold values from -6 to 6
- head_values: bfloat16 [2, 2048, 2048], P('dp', 'seq', 'head'), may hold values from -6 to 6
- dt_raw: float32 [2, 32, 2048], P('dp', 'head', 'seq'), may hold values from -2 to 40
- w_bc: bfloat16 [2048, 128], replicated, may hold values from -0.015625 to 0.015625
- decay_rate: float32 [32], P('head'), may hold values from 0.0068359375 to 2
- dt_bias: float32 [32], P('head'), may hold values from -4.5 to -3.5
- skip_gain: float32 [32], P('head'), may hold values from 0.5 to 1.5
- grad_y: bfloat16 [2, 2048, 2048], P('dp', 'seq', 'head'), may hold values from -6 to 6
Outputs:
- y_out: bfloat16 [2, 2048, 2048], P('dp', 'seq', 'head')
- grad_values: bfloat16 [2, 2048, 2048], P('dp', 'seq', 'head')
- grad_input: bfloat16 [2, 2048, 2048], P('dp', 'seq')
- grad_w_bc: float32 [2048, 128], P(('dp', 'seq'))
The draws below stay inside these ranges and needn't reach their ends.
All inputs are finite; a program needn't handle non-finite values.
Results may differ from the reference program's by a relative error of at most 0.013.
Values may be sent and summed in bfloat16 or wider, within the bound.
No kernel may reach another device: no remote copies, remote signals or barrier semaphores. Data moves between devices by JAX's collectives and lax.ppermute only.
A program may use at most 320 MiB of HBM per device.

```python
import jax
import jax.numpy as jnp
from jax import lax

D = 2048
H = 32
P_SIZE = 64
N = 64
TOK_DEV = 512
DOCUMENT_COUNT = 2
DOCUMENT_LENGTH = 2048
N_HEAD = 4
N_SEQ = 4


def draw_dt_raw(key, part):
    key_level, key_rough, key_location = jax.random.split(key, 3)
    block_count = DOCUMENT_LENGTH // TOK_DEV
    block_level = jax.random.uniform(key_level, (DOCUMENT_COUNT, H, block_count, 1), jnp.float32, -1.0, 1.0)
    token_rough = jnp.clip(0.5 * jax.random.normal(key_rough, (DOCUMENT_COUNT, H, block_count, TOK_DEV), jnp.float32), -1.0, 1.0)
    filled_value = (block_level + token_rough).reshape(DOCUMENT_COUNT, H, DOCUMENT_LENGTH)
    spike_locations = jax.random.randint(key_location, (DOCUMENT_COUNT, 1, 1, 2), 0, DOCUMENT_LENGTH)
    position_index = jnp.arange(DOCUMENT_LENGTH)[None, None, :, None]
    spike_flags = jnp.any(position_index == spike_locations, axis=-1)
    spike_magnitude = jnp.float32(DOCUMENT_LENGTH // 56 + 4)
    return jnp.where(spike_flags, spike_magnitude, filled_value)


def head_kinds(key):
    slow_share = 0.5
    slow_kind = jax.random.bernoulli(jax.random.fold_in(key, 101), slow_share, (H,))
    medium_kind = jax.random.bernoulli(jax.random.fold_in(key, 102), 0.7, (H,))
    return (slow_kind, medium_kind)


def draw_decay_rate(key, part):
    slow_kind, medium_kind = head_kinds(key)
    slow_rate = jax.random.uniform(jax.random.fold_in(key, 103), (H,), jnp.float32, 14.0, 28.0) / DOCUMENT_LENGTH
    medium_rate = jax.random.uniform(jax.random.fold_in(key, 104), (H,), jnp.float32, 70.0, 160.0) / TOK_DEV
    fast_rate = jax.random.uniform(jax.random.fold_in(key, 105), (H,), jnp.float32, 1.0, 2.0)
    return jnp.where(slow_kind, slow_rate, jnp.where(medium_kind, medium_rate, fast_rate))


def value_field(key, salt):
    slow_kind, medium_kind = head_kinds(key)
    slow_scale = jnp.minimum(1.0, 96.0 / jnp.sqrt(0.7 * N * DOCUMENT_LENGTH))
    head_scale = jnp.where(slow_kind, slow_scale, 1.0).astype(jnp.float32)
    noise_key = jax.random.fold_in(key, salt)
    noise = jnp.clip(jax.random.normal(noise_key, (DOCUMENT_COUNT, DOCUMENT_LENGTH, H, P_SIZE), jnp.float32), -6.0, 6.0)
    scaled = noise * head_scale[None, None, :, None]
    return scaled.reshape(DOCUMENT_COUNT, DOCUMENT_LENGTH, H * P_SIZE)


def draw_head_values(key, part):
    return value_field(key, 201).astype(jnp.bfloat16)


def draw_grad_y(key, part):
    return value_field(key, 202).astype(jnp.bfloat16)


def with_spikes(result, key, source, target, shards_of, factor):
    def block_of(position):
        return (jnp.arange(result.shape[position]) // (result.shape[position] // shards_of)).reshape((-1,) + (1,) * (result.ndim - 1 - position))

    near = jax.random.permutation(key, shards_of)[block_of(target)]
    second = (block_of(target) + shards_of // 2) % shards_of
    return jnp.where((block_of(source) == near) | (block_of(source) == second), factor * result, result)


def shard_levels(key, dims, cuts, smallest, largest):
    def one(position, parts):
        heights = jax.random.uniform(jax.random.fold_in(jax.random.fold_in(key, 6), position), (parts,), jnp.float32, smallest / len(cuts), largest / len(cuts))
        return jnp.repeat(jnp.exp(heights), dims[position] // parts).reshape((-1,) + (1,) * (len(dims) - position - 1))

    gain = one(*cuts[0])
    for cut in cuts[1:]:
        gain = gain * one(*cut)
    return gain


def centred(own_key, extent, spread, bound, cuts=(), kind=jnp.bfloat16):
    factor_of = shard_levels(own_key, extent, cuts, -0.22, 0.18) if cuts else 1.0
    drawn = jax.random.normal(own_key, extent, jnp.float32) * spread * factor_of
    return jnp.minimum(jnp.maximum(drawn, -bound), bound).astype(kind)


def noise_with(rng, extent, width, most, cuts, heavy, held_as=jnp.bfloat16):
    values = width * jax.random.normal(rng, extent, jnp.float32)
    if cuts:
        values = values * shard_levels(rng, extent, cuts, -0.22, 0.18)
    return jnp.clip(with_spikes(values, jax.random.fold_in(rng, 3), *heavy), -most, most).astype(held_as)


def setup_inputs(seed: int = 0) -> dict:
    streams_of = jax.random.split(jax.random.key(seed), 9)
    return {
        "layer_input": noise_with(streams_of[0], (DOCUMENT_COUNT, DOCUMENT_LENGTH, D), 1.0, 6.0, ((0, 2), (1, 4)), (1, 2, 4, 2.0)),
        "head_values": draw_head_values(jax.random.fold_in(streams_of[8], 71), 0),
        "dt_raw": draw_dt_raw(jax.random.fold_in(streams_of[8], 71), 0),
        "w_bc": centred(streams_of[3], (D, 2 * N), (64 * D) ** -0.5, 0.015625),
        "decay_rate": draw_decay_rate(jax.random.fold_in(streams_of[8], 71), 0),
        "dt_bias": jnp.clip(-4.5 + 1.0 * jax.random.uniform(streams_of[5], (H,), jnp.float32) ** shard_levels(streams_of[5], (H,), ((0, 4),), -0.2, 0.2), -4.5, -3.5),
        "skip_gain": jnp.clip(0.5 + 1.0 * jax.random.uniform(streams_of[6], (H,), jnp.float32) ** shard_levels(streams_of[6], (H,), ((0, 4),), -0.2, 0.2), 0.5, 1.5),
        "grad_y": draw_grad_y(jax.random.fold_in(streams_of[8], 71), 0),
    }


maximum_level = lax.Precision.HIGHEST


def block_terms(queries, keys_in, values, forward_logarithm, backward_logarithm, final_logarithm):
    count_rows = queries.shape[0]
    scores = jnp.einsum("thd,shd->hts", queries.astype(jnp.float32), keys_in.astype(jnp.float32), precision=maximum_level)
    row_index = jnp.arange(count_rows)[:, None]
    col_index = jnp.arange(count_rows)[None, :]
    diff_fwd = forward_logarithm[:, :, None] - forward_logarithm[:, None, :]
    diff_bwd = backward_logarithm[:, None, :] - backward_logarithm[:, :, None]
    kernel = jnp.where(col_index < row_index, jnp.exp(jnp.minimum(diff_fwd, 0.0)), 0.0)
    kernel = kernel + jnp.where(col_index > row_index, jnp.exp(jnp.minimum(diff_bwd, 0.0)), 0.0)
    rounded = (scores * kernel).astype(jnp.bfloat16)
    weights = lax.optimization_barrier(rounded).astype(jnp.float32)
    widened_values = values.astype(jnp.float32)
    local_part = jnp.einsum("hts,shv->thv", weights, widened_values, precision=maximum_level)
    keys_wide = keys_in.astype(jnp.float32)
    heading_following = keys_wide * jnp.exp(final_logarithm[:, None] - forward_logarithm).T[:, :, None]
    heading_preceding = keys_wide * jnp.exp(backward_logarithm).T[:, :, None]
    following_state = jnp.einsum("qgz,qgn->gzn", heading_following, widened_values, precision=maximum_level)
    preceding_state = jnp.einsum("qgz,qgn->gzn", heading_preceding, widened_values, precision=maximum_level)
    return local_part, following_state, preceding_state


def carry_terms(queries, forward_logarithm, backward_logarithm, final_logarithm, contribution_earlier, contribution_later):
    widened_queries = queries.astype(jnp.float32)
    preceding_portion = jnp.einsum("caz,azp->cap", widened_queries, contribution_earlier, precision=maximum_level) * jnp.exp(forward_logarithm).T[:, :, None]
    following_portion = jnp.einsum("caz,azp->cap", widened_queries, contribution_later, precision=maximum_level) * jnp.exp(final_logarithm[:, None] - backward_logarithm).T[:, :, None]
    return preceding_portion + following_portion


def mixer(queries, keys_in, values, forward_logarithm, backward_logarithm, final_logarithm):
    def blocked(array):
        return array.reshape((N_SEQ, TOK_DEV) + array.shape[1:])

    block_q = blocked(queries)
    block_k = blocked(keys_in)
    block_v = blocked(values)

    def one_block(inputs):
        return block_terms(inputs[0], inputs[1], inputs[2], inputs[3], inputs[4], inputs[5])

    local_part, following_state, preceding_state = lax.map(one_block, (block_q, block_k, block_v, forward_logarithm, backward_logarithm, final_logarithm))
    decay_total = jnp.exp(final_logarithm)

    def carry_step(carry_state, inputs):
        return inputs[0][:, None, None] * carry_state + inputs[1], carry_state

    zero_state = jnp.zeros(following_state.shape[1:], jnp.float32)
    _, contribution_earlier = lax.scan(carry_step, zero_state, (decay_total, following_state))
    _, contribution_later = lax.scan(carry_step, zero_state, (decay_total, preceding_state), reverse=True)

    def apply_block(inputs):
        return carry_terms(inputs[0], inputs[1], inputs[2], inputs[3], inputs[4], inputs[5])

    carried = lax.map(apply_block, (block_q, forward_logarithm, backward_logarithm, final_logarithm, contribution_earlier, contribution_later))
    total = local_part + carried
    return total.reshape((DOCUMENT_LENGTH,) + total.shape[2:])


def decay_logs(dt_doc, decay_rate, dt_bias):
    log_step = -decay_rate[:, None] * jax.nn.softplus(dt_doc + dt_bias[:, None])
    blocked_step = log_step.reshape(log_step.shape[0], N_SEQ, TOK_DEV).transpose(1, 0, 2)
    cum_log = jnp.cumsum(blocked_step, axis=2)
    return cum_log, cum_log - blocked_step, cum_log[:, :, -1]


def group_heads(per_head):
    grouped = per_head.reshape(DOCUMENT_LENGTH, N_HEAD, H // N_HEAD, per_head.shape[2])
    return jnp.sum(grouped, axis=2)


def reference(layer_input, head_values, dt_raw, w_bc, decay_rate, dt_bias, skip_gain, grad_y):
    output_list = []
    grad_value_list = []
    grad_input_list = []
    weight_total = jnp.zeros(w_bc.shape, jnp.float32)
    for doc_index in range(DOCUMENT_COUNT):
        tokens = layer_input[doc_index]
        projected = jnp.dot(tokens, w_bc, preferred_element_type=jnp.float32).astype(jnp.bfloat16)
        b_heads = jnp.broadcast_to(projected[:, None, :N], (DOCUMENT_LENGTH, H, N))
        c_heads = jnp.broadcast_to(projected[:, None, N:], (DOCUMENT_LENGTH, H, N))
        values_x = head_values[doc_index].reshape(DOCUMENT_LENGTH, H, P_SIZE)
        cotangent = grad_y[doc_index].reshape(DOCUMENT_LENGTH, H, P_SIZE)
        cum_log, prev_log, final_logarithm = decay_logs(dt_raw[doc_index], decay_rate, dt_bias)
        mixed = mixer(c_heads, b_heads, values_x, cum_log, prev_log, final_logarithm)
        output_list.append((mixed + skip_gain[None, :, None] * values_x.astype(jnp.float32)).astype(jnp.bfloat16))
        back_mixed = mixer(b_heads, c_heads, cotangent, prev_log, cum_log, final_logarithm)
        grad_value_list.append((back_mixed + skip_gain[None, :, None] * cotangent.astype(jnp.float32)).astype(jnp.bfloat16))
        grad_c = group_heads(mixer(cotangent, values_x, b_heads, cum_log, prev_log, final_logarithm))
        grad_b = group_heads(mixer(values_x, cotangent, c_heads, prev_log, cum_log, final_logarithm))
        group_bc = jnp.concatenate([grad_b, grad_c], axis=2).astype(jnp.bfloat16)
        group_wide = lax.optimization_barrier(group_bc).astype(jnp.float32)
        grad_bc = jnp.sum(group_wide, axis=1).astype(jnp.bfloat16)
        grad_input_list.append(jnp.dot(grad_bc, w_bc.T, preferred_element_type=jnp.float32).astype(jnp.bfloat16))
        weight_total = weight_total + jnp.dot(tokens.T, grad_bc, preferred_element_type=jnp.float32)
    y_out = jnp.stack(output_list).reshape(DOCUMENT_COUNT, DOCUMENT_LENGTH, H * P_SIZE)
    grad_values = jnp.stack(grad_value_list).reshape(DOCUMENT_COUNT, DOCUMENT_LENGTH, H * P_SIZE)
    grad_input = jnp.stack(grad_input_list)
    return (y_out, grad_values, grad_input, weight_total / (DOCUMENT_COUNT * DOCUMENT_LENGTH))
```

```python
import functools

import jax
import jax.numpy as jnp
from jax import lax
from jax.experimental import pallas as pl
from jax.experimental.pallas import tpu as pltpu
from jax.sharding import PartitionSpec as P

F32 = jnp.float32
BF16 = jnp.bfloat16
VMEM_SPEC = pl.BlockSpec(memory_space=pltpu.VMEM)
SMEM_SPEC = pl.BlockSpec(memory_space=pltpu.SMEM)
EXTRA = 16


def mm(a, b):
    return jnp.dot(a, b, preferred_element_type=F32)


def mm_t(a, b):
    return lax.dot_general(a, b, (((1,), (1,)), ((), ())), preferred_element_type=F32)


def split2(v):
    high = v.astype(BF16)
    return high, (v - high.astype(F32)).astype(BF16)


def spread_matrix(heads, width):
    rows = 8 * heads
    row = lax.broadcasted_iota(jnp.int32, (rows, 4 * width), 0)
    col = lax.broadcasted_iota(jnp.int32, (rows, 4 * width), 1)
    per_head = width // heads
    kind_ok = (row // (2 * heads)) == (col // width)
    head_ok = (row % heads) == ((col % width) // per_head)
    return jnp.where(kind_ok & head_ok, 1.0, 0.0).astype(BF16)


def states_kernel(
    n_seq, steps, tokens_ref, x_ref, g_ref, dt_ref, w_ref, rate_ref, bias_ref,
    bc_ref, cb_ref, rows_ref, cols_ref, decs_ref, pay1_ref, pay2_ref, pay3_ref, acc_ref, spread_ref, last_ref,
):
    step = pl.program_id(0)
    heads, length = dt_ref.shape
    chunk = tokens_ref.shape[0]
    width = x_ref.shape[1]

    @pl.when(step == 0)
    def _():
        sub = lax.broadcasted_iota(jnp.int32, (heads, 1), 0)
        rate = jnp.zeros((heads, 1), F32)
        bias = jnp.zeros((heads, 1), F32)
        for h in range(heads):
            rate = jnp.where(sub == h, rate_ref[h], rate)
            bias = jnp.where(sub == h, bias_ref[h], bias)
        v = dt_ref[...] + bias
        log_step = -rate * (jnp.maximum(v, 0.0) + jnp.log1p(jnp.exp(-jnp.abs(v))))
        lane = lax.broadcasted_iota(jnp.int32, (heads, length), 1)
        cum = log_step
        shift = 1
        while shift < length:
            cum = cum + jnp.where(lane >= shift, pltpu.roll(cum, shift, 1), 0.0)
            shift *= 2
        prev = cum - log_step
        final = cum[:, length - 1 : length]
        kinds = (jnp.exp(cum), jnp.exp(final - prev), jnp.exp(prev), jnp.exp(final - cum))
        parts = []
        for k in kinds:
            high = k.astype(BF16).astype(F32)
            parts += [high, k - high]
        decs_ref[...] = jnp.concatenate(parts, axis=0).astype(BF16)
        for p in range(heads // 2):
            block = jnp.concatenate(
                [cum[2 * p : 2 * p + 1], prev[2 * p : 2 * p + 1], cum[2 * p + 1 : 2 * p + 2], prev[2 * p + 1 : 2 * p + 2]]
                + [jnp.zeros((4, length), F32)],
                axis=0,
            )
            rows_ref[p] = block
            cols_ref[p] = block.T
        spread_ref[...] = spread_matrix(heads, width)
        head_of = lax.broadcasted_iota(jnp.int32, (heads, width), 1) // (width // heads)
        head_row = lax.broadcasted_iota(jnp.int32, (heads, width), 0)
        decay = jnp.sum(jnp.where(head_of == head_row, jnp.exp(final), 0.0), axis=0, keepdims=True)
        high = decay.astype(BF16).astype(F32)
        row16 = lax.broadcasted_iota(jnp.int32, (EXTRA, width), 0)
        last_ref[...] = jnp.where(row16 == 0, high, jnp.where(row16 == 1, decay - high, 0.0))
        acc_ref[...] = jnp.zeros_like(acc_ref)

    projected = mm(tokens_ref[...], w_ref[...])
    half = projected.shape[1] // 2
    bc = projected.astype(BF16)
    bc_ref[...] = bc
    turned = pltpu.roll(projected, half, 1)
    cb = turned.astype(BF16)
    cb_ref[...] = cb
    cb_t = turned.T.astype(BF16)
    start = pl.multiple_of(step * chunk, chunk)
    decs = decs_ref[:, pl.ds(start, chunk)].astype(F32).T.astype(BF16)
    e = mm(decs, spread_ref[...])
    x = x_ref[...].astype(F32)
    g = g_ref[...].astype(F32)
    g_up = (g * e[:, :width]).astype(BF16)
    g_down = (g * e[:, width : 2 * width]).astype(BF16)
    x_up = (x * e[:, 2 * width : 3 * width]).astype(BF16)
    x_down = (x * e[:, 3 * width :]).astype(BF16)
    acc_ref[0, :half] += mm(cb_t[:half], g_down)
    acc_ref[0, half:] += mm(cb_t[half:], x_down)
    acc_ref[1, :half] += mm(cb_t[:half], g_up)
    acc_ref[1, half:] += mm(cb_t[half:], x_up)

    @pl.when(step == steps - 1)
    def _():
        onward = acc_ref[0].astype(BF16)
        backward = acc_ref[1].astype(BF16)
        last = last_ref[...].astype(BF16)
        for k, ref in ((1, pay1_ref), (2, pay2_ref), (3, pay3_ref)):
            ref[2 * half :] = last
            if n_seq == 4:
                here = lax.axis_index("seq")
                up = (here ^ k) > here

                @pl.when(up)
                def _():
                    ref[: 2 * half] = onward

                @pl.when(jnp.logical_not(up))
                def _():
                    ref[: 2 * half] = backward
            else:
                ref[: 2 * half] = onward if k == 1 else backward


def block_states(n_seq, tokens, x, g, dt, w, rate, bias):
    _, length, depth = tokens.shape
    width = x.shape[2]
    heads = dt.shape[1]
    two_n = w.shape[1]
    steps = 2
    chunk = length // steps
    pay = jax.ShapeDtypeStruct((two_n + EXTRA, width), BF16)
    whole = lambda *shape: pl.BlockSpec(shape, lambda i: (0,) * len(shape))
    return pl.pallas_call(
        functools.partial(states_kernel, n_seq, steps),
        name="block_states",
        grid=(steps,),
        in_specs=[
            pl.BlockSpec((None, chunk, depth), lambda i: (0, i, 0)),
            pl.BlockSpec((None, chunk, width), lambda i: (0, i, 0)),
            pl.BlockSpec((None, chunk, width), lambda i: (0, i, 0)),
            pl.BlockSpec((None, heads, length), lambda i: (0, 0, 0)),
            whole(depth, two_n),
            SMEM_SPEC,
            SMEM_SPEC,
        ],
        out_specs=[
            pl.BlockSpec((chunk, two_n), lambda i: (i, 0)),
            pl.BlockSpec((chunk, two_n), lambda i: (i, 0)),
            whole(heads // 2, 8, length),
            whole(heads // 2, length, 8),
            whole(8 * heads, length),
            whole(two_n + EXTRA, width),
            whole(two_n + EXTRA, width),
            whole(two_n + EXTRA, width),
        ],
        out_shape=[
            jax.ShapeDtypeStruct((length, two_n), BF16),
            jax.ShapeDtypeStruct((length, two_n), BF16),
            jax.ShapeDtypeStruct((heads // 2, 8, length), F32),
            jax.ShapeDtypeStruct((heads // 2, length, 8), F32),
            jax.ShapeDtypeStruct((8 * heads, length), BF16),
            pay,
            pay,
            pay,
        ],
        scratch_shapes=[
            pltpu.VMEM((2, two_n, width), F32),
            pltpu.VMEM((8 * heads, 4 * width), BF16),
            pltpu.VMEM((EXTRA, width), F32),
        ],
        cost_estimate=pl.CostEstimate(flops=2 * length * depth * two_n, bytes_accessed=5 << 20, transcendentals=0),
    )(tokens, x, g, dt, w, rate, bias)


def local_kernel(
    n_t, n_pair, x_ref, g_ref, bc_ref, cb_ref, rows_ref, cols_ref, skip_ref,
    y_ref, gv_ref, gbc_ref, xm_ref, scores_ref, total_ref, gvt_ref, gbt_ref, gc_ref,
):
    tb = pl.program_id(0)
    pair = pl.program_id(1)
    length = x_ref.shape[0]
    tile = length // n_t
    lanes = 128
    t0 = pl.multiple_of(tb * tile, tile)
    p0 = pl.multiple_of(pair * lanes, lanes)
    first_half = lax.broadcasted_iota(jnp.int32, (1, lanes), 1) < lanes // 2
    zero = jnp.zeros((), BF16)

    @pl.when(tb == 0)
    def _():
        xp = x_ref[:, pl.ds(p0, lanes)]
        xm_ref[pair, :length] = jnp.where(first_half, xp, zero)
        xm_ref[pair, length:] = jnp.where(first_half, zero, xp)
        gvt_ref[pair] = jnp.zeros((lanes, length), F32)

    cb_t = cb_ref[pl.ds(t0, tile), :]

    @pl.when(pair == 0)
    def _():
        scores_ref[...] = mm_t(jnp.where(first_half, cb_t, zero), bc_ref[...])

    g_t = g_ref[pl.ds(t0, tile), pl.ds(p0, lanes)]
    g_s = g_t.astype(F32)
    row = t0 + lax.broadcasted_iota(jnp.int32, (tile, length), 0)
    col = lax.broadcasted_iota(jnp.int32, (tile, length), 1)
    below = col < row
    same = col == row
    xm = xm_ref[pair]
    grams = mm_t(g_t, xm)
    cols = cols_ref[pair, pl.ds(t0, tile), :]
    scores = scores_ref[...]
    mains = []
    grad = None
    for k in range(2):
        cum_t, prev_t = cols[:, 2 * k : 2 * k + 1], cols[:, 2 * k + 1 : 2 * k + 2]
        cum_s, prev_s = rows_ref[pair, 2 * k : 2 * k + 1], rows_ref[pair, 2 * k + 1 : 2 * k + 2]
        diff = jnp.minimum(jnp.where(below, cum_t - cum_s, prev_s - prev_t), 0.0)
        kern = jnp.where(same, 0.0, jnp.exp(diff))
        mains.append((scores * kern).astype(BF16))
        term = grams[:, k * length : (k + 1) * length] * kern
        grad = term if grad is None else grad + term

    y = mm(mains[0], xm[:length]) + mm(mains[1], xm[length:])
    sk = jnp.where(first_half, skip_ref[2 * pair], skip_ref[2 * pair + 1])
    y_ref[...] = y + sk * x_ref[pl.ds(t0, tile), pl.ds(p0, lanes)].astype(F32)
    gt = g_s.T.astype(BF16)
    upper = lax.broadcasted_iota(jnp.int32, (lanes, 1), 0) < lanes // 2
    gvt_ref[pair] += mm(jnp.where(upper, gt, zero), mains[0]) + mm(jnp.where(upper, zero, gt), mains[1])

    @pl.when(pair == 0)
    def _():
        total_ref[...] = grad

    @pl.when(pair > 0)
    def _():
        total_ref[...] += grad

    @pl.when(pair == n_pair - 1)
    def _():
        total = total_ref[...].astype(BF16)
        gc_ref[pl.ds(t0, tile), :] = mm(total, cb_ref[...])
        gbt = mm(cb_t.astype(F32).T.astype(BF16), total)

        @pl.when(tb == 0)
        def _():
            gbt_ref[...] = gbt

        @pl.when(tb > 0)
        def _():
            gbt_ref[...] += gbt

    @pl.when(tb == n_t - 1)
    def _():
        gv_ref[:, pl.ds(p0, lanes)] = gvt_ref[pair].T + sk * g_ref[:, pl.ds(p0, lanes)].astype(F32)

        @pl.when(pair == n_pair - 1)
        def _():
            gbc_ref[...] = jnp.where(first_half, gbt_ref[...].T, gc_ref[...])


def inside_block(x, g, bc, cb, rows, cols, skip):
    _, length, width = x.shape
    n_pair = width // 128
    n_t = 4
    tile = length // n_t
    full = lambda *shape: pl.BlockSpec(shape, lambda t, p: (0,) * len(shape))
    return pl.pallas_call(
        functools.partial(local_kernel, n_t, n_pair),
        name="inside_block",
        grid=(n_t, n_pair),
        in_specs=[
            pl.BlockSpec((None, length, width), lambda t, p: (0, 0, 0)),
            pl.BlockSpec((None, length, width), lambda t, p: (0, 0, 0)),
            full(length, 128),
            full(length, 128),
            full(n_pair, 8, length),
            full(n_pair, length, 8),
            SMEM_SPEC,
        ],
        out_specs=[
            pl.BlockSpec((tile, 128), lambda t, p: (t, p)),
            full(length, width),
            full(length, 128),
        ],
        out_shape=[
            jax.ShapeDtypeStruct((length, width), F32),
            jax.ShapeDtypeStruct((length, width), F32),
            jax.ShapeDtypeStruct((length, 128), F32),
        ],
        scratch_shapes=[
            pltpu.VMEM((n_pair, 2 * length, 128), BF16),
            pltpu.VMEM((tile, length), F32),
            pltpu.VMEM((tile, length), F32),
            pltpu.VMEM((n_pair, 128, length), F32),
            pltpu.VMEM((128, length), F32),
            pltpu.VMEM((length, 128), F32),
        ],
        cost_estimate=pl.CostEstimate(
            flops=6 * length * length * width, bytes_accessed=4 << 20, transcendentals=2 * n_pair * length * length
        ),
    )(x, g, bc, cb, rows, cols, skip)


def carry_kernel(
    direct, r1_ref, r2_ref, r3_ref, x_ref, g_ref, bc_ref, decs_ref, y_ref, gv_ref, gbc_ref,
    yo_ref, gvo_ref, group_ref, before_ref, after_ref, spread_ref,
):
    step = pl.program_id(0)
    two_n, width = before_ref.shape
    heads = decs_ref.shape[0] // 8
    chunk = x_ref.shape[0]

    @pl.when(step == 0)
    def _():
        spread_ref[...] = spread_matrix(heads, width)
        if direct:
            here = lax.axis_index("seq")
            refs = (r1_ref, r2_ref, r3_ref)
            decays = [r[two_n : two_n + 1].astype(F32) + r[two_n + 1 : two_n + 2].astype(F32) for r in refs]
            before = jnp.zeros((two_n, width), F32)
            after = jnp.zeros((two_n, width), F32)
            for k in (1, 2, 3):
                there = here ^ k
                low, high = jnp.minimum(here, there), jnp.maximum(here, there)
                factor = jnp.ones((1, width), F32)
                for m in (1, 2, 3):
                    if m != k:
                        mid = here ^ m
                        inside = jnp.logical_and(mid > low, mid < high)
                        factor = factor * jnp.where(inside, decays[m - 1], 1.0)
                part = refs[k - 1][:two_n].astype(F32)
                earlier = there < here
                before = before + part * jnp.where(earlier, factor, 0.0)
                after = after + part * jnp.where(earlier, 0.0, factor)
            before_ref[...] = before.astype(BF16)
            after_ref[...] = after.astype(BF16)
        else:
            before_ref[...] = r1_ref[:two_n]
            after_ref[...] = r2_ref[:two_n]

    before = before_ref[...]
    after = after_ref[...]
    half = two_n // 2
    top = lax.broadcasted_iota(jnp.int32, (two_n, 1), 0) < half
    zero = jnp.zeros((), BF16)
    start = pl.multiple_of(step * chunk, chunk)
    decs = decs_ref[:, pl.ds(start, chunk)].astype(F32).T.astype(BF16)
    e = mm(decs, spread_ref[...])
    g_up, g_down = e[:, :width], e[:, width : 2 * width]
    x_up, x_down = e[:, 2 * width : 3 * width], e[:, 3 * width :]
    bc = bc_ref[...]
    lower_b, lower_a = jnp.where(top, zero, before), jnp.where(top, zero, after)
    upper_b, upper_a = jnp.where(top, before, zero), jnp.where(top, after, zero)
    yo_ref[...] = (y_ref[...] + g_up * mm(bc, lower_b) + g_down * mm(bc, lower_a)).astype(BF16)
    gvo_ref[...] = (gv_ref[...] + x_up * mm(bc, upper_b) + x_down * mm(bc, upper_a)).astype(BF16)
    x = x_ref[...].astype(F32)
    g = g_ref[...].astype(F32)
    from_x = mm_t((x * x_up).astype(BF16), before) + mm_t((x * x_down).astype(BF16), after)
    from_g = mm_t((g * g_up).astype(BF16), before) + mm_t((g * g_down).astype(BF16), after)
    left = lax.broadcasted_iota(jnp.int32, (1, two_n), 1) < half
    group_ref[...] = (gbc_ref[...] + jnp.where(left, from_x, from_g)).astype(BF16)


def add_carries(direct, r1, r2, r3, x, g, bc, decs, y, gv, gbc):
    _, length, width = x.shape
    two_n = bc.shape[1]
    steps = 2
    chunk = length // steps
    whole = lambda a: pl.BlockSpec(a.shape, lambda i: (0, 0))
    part = lambda w: pl.BlockSpec((chunk, w), lambda i: (i, 0))
    part3 = lambda w: pl.BlockSpec((None, chunk, w), lambda i: (0, i, 0))
    return pl.pallas_call(
        functools.partial(carry_kernel, direct),
        name="add_carries",
        grid=(steps,),
        in_specs=[
            whole(r1), whole(r2), whole(r3), part3(width), part3(width), part(two_n), whole(decs),
            part(width), part(width), part(two_n),
        ],
        out_specs=[part3(width), part3(width), part(two_n)],
        out_shape=[
            jax.ShapeDtypeStruct((1, length, width), BF16),
            jax.ShapeDtypeStruct((1, length, width), BF16),
            jax.ShapeDtypeStruct((length, two_n), BF16),
        ],
        scratch_shapes=[
            pltpu.VMEM((two_n, width), BF16),
            pltpu.VMEM((two_n, width), BF16),
            pltpu.VMEM((decs.shape[0], 4 * width), BF16),
        ],
        cost_estimate=pl.CostEstimate(flops=16 * length * two_n * width, bytes_accessed=5 << 20, transcendentals=0),
    )(r1, r2, r3, x, g, bc, decs, y, gv, gbc)


def scanned_generic(onward, backward, two_n):
    size, here = lax.axis_size("seq"), lax.axis_index("seq")

    def total(payload, reverse):
        every = lax.all_gather(payload, "seq")

        def step(k, before):
            at = size - 1 - k if reverse else k
            one = every[at].astype(F32)
            new = before * (one[two_n : two_n + 1] + one[two_n + 1 : two_n + 2]) + one[:two_n]
            return jnp.where(at > here if reverse else at < here, new, before)

        return lax.fori_loop(0, size, step, jnp.zeros((two_n, payload.shape[1]), F32))

    pad = lambda v: jnp.pad(v.astype(BF16), ((0, EXTRA), (0, 0)))
    return pad(total(onward, False)), pad(total(backward, True))


def weight_kernel(a0_ref, a1_ref, a2_ref, a3_ref, tokens_ref, grad_ref, send_ref, keep_ref):
    total = a0_ref[...].astype(F32) + a1_ref[...].astype(F32) + a2_ref[...].astype(F32) + a3_ref[...].astype(F32)
    grad = total.astype(BF16)
    grad_ref[...] = grad
    grad_t = grad.astype(F32).T.astype(BF16)
    here = lax.axis_index("dp")
    n_seq, _, cols = keep_ref.shape
    for s in range(n_seq):
        away = pl.multiple_of(((1 - here) * n_seq + s) * cols, cols)
        send_ref[s] = mm(grad_t, tokens_ref[:, pl.ds(away, cols)]).astype(BF16)
    for s in range(n_seq):
        home = pl.multiple_of((here * n_seq + s) * cols, cols)
        keep_ref[s] = mm(grad_t, tokens_ref[:, pl.ds(home, cols)])


def weight_parts(n_seq, groups, tokens):
    _, length, depth = tokens.shape
    two_n = groups[0].shape[1]
    cols = depth // (2 * n_seq)
    return pl.pallas_call(
        weight_kernel,
        name="weight_parts",
        grid=(1,),
        in_specs=[pl.BlockSpec((length, two_n), lambda i: (0, 0))] * 4
        + [pl.BlockSpec((None, length, depth), lambda i: (0, 0, 0))],
        out_specs=[
            pl.BlockSpec((length, two_n), lambda i: (0, 0)),
            pl.BlockSpec((n_seq, two_n, cols), lambda i: (0, 0, 0)),
            pl.BlockSpec((n_seq, two_n, cols), lambda i: (0, 0, 0)),
        ],
        out_shape=[
            jax.ShapeDtypeStruct((length, two_n), BF16),
            jax.ShapeDtypeStruct((n_seq, two_n, cols), BF16),
            jax.ShapeDtypeStruct((n_seq, two_n, cols), F32),
        ],
        cost_estimate=pl.CostEstimate(flops=2 * length * two_n * depth, bytes_accessed=4 << 20, transcendentals=0),
    )(*groups, tokens)


def pair_kernel(keep_ref, got_ref, own_ref, s1_ref, s2_ref, s3_ref):
    here = lax.axis_index("seq")
    own_ref[...] = keep_ref[here] + got_ref[here].astype(F32)
    for k, ref in ((1, s1_ref), (2, s2_ref), (3, s3_ref)):
        at = here ^ k
        ref[...] = (keep_ref[at] + got_ref[at].astype(F32)).astype(BF16)


def pair_sum(keep, got):
    _, two_n, cols = keep.shape
    small = jax.ShapeDtypeStruct((two_n, cols), BF16)
    return pl.pallas_call(
        pair_kernel,
        name="pair_sum",
        in_specs=[VMEM_SPEC, VMEM_SPEC],
        out_specs=[VMEM_SPEC] * 4,
        out_shape=[jax.ShapeDtypeStruct((two_n, cols), F32), small, small, small],
    )(keep, got)


def final_kernel(scale, own_ref, r1_ref, r2_ref, r3_ref, out_ref):
    total = own_ref[...] + r1_ref[...].astype(F32) + r2_ref[...].astype(F32) + r3_ref[...].astype(F32)
    out_ref[...] = total.T * scale


def final_sum(scale, own, r1, r2, r3):
    two_n, cols = own.shape
    return pl.pallas_call(
        functools.partial(final_kernel, scale),
        name="final_sum",
        in_specs=[VMEM_SPEC] * 4,
        out_specs=VMEM_SPEC,
        out_shape=jax.ShapeDtypeStruct((cols, two_n), F32),
    )(own, r1, r2, r3)


def input_kernel(grad_ref, w_ref, out_ref):
    out_ref[...] = mm_t(grad_ref[...], w_ref[...]).astype(BF16)


def input_grad(grad, w):
    length, two_n = grad.shape
    depth = w.shape[0]
    steps = 4
    chunk = length // steps
    return pl.pallas_call(
        input_kernel,
        name="input_grad",
        grid=(steps,),
        in_specs=[pl.BlockSpec((chunk, two_n), lambda i: (i, 0)), pl.BlockSpec((depth, two_n), lambda i: (0, 0))],
        out_specs=pl.BlockSpec((None, chunk, depth), lambda i: (0, i, 0)),
        out_shape=jax.ShapeDtypeStruct((1, length, depth), BF16),
        cost_estimate=pl.CostEstimate(flops=2 * length * two_n * depth, bytes_accessed=3 << 20, transcendentals=0),
    )(grad, w)


def swap(value, axis, k):
    return lax.ppermute(value, axis, [(i, i ^ k) for i in range(lax.axis_size(axis))])


def per_device(layer_input, head_values, dt_raw, w_bc, decay_rate, dt_bias, skip_gain, grad_y):
    n_seq, n_head, n_dp = lax.axis_size("seq"), lax.axis_size("head"), lax.axis_size("dp")
    length = layer_input.shape[1]
    two_n = w_bc.shape[1]
    bc, cb, rows, cols, decs, pay1, pay2, pay3 = block_states(
        n_seq, layer_input, head_values, grad_y, dt_raw, w_bc, decay_rate, dt_bias
    )
    direct = n_seq == 4
    if direct:
        r1, r2, r3 = swap(pay1, "seq", 1), swap(pay2, "seq", 2), swap(pay3, "seq", 3)
    else:
        r1, r2 = scanned_generic(pay1, pay2, two_n)
        r3 = r2
    y_local, gv_local, gbc_local = inside_block(head_values, grad_y, bc, cb, rows, cols, skip_gain)
    y_out, grad_values, group = add_carries(
        direct, r1, r2, r3, head_values, grad_y, bc, decs, y_local, gv_local, gbc_local
    )
    total_tokens = n_dp * n_seq * length
    if direct and n_dp == 2 and n_head == 4:
        groups = [group] + [swap(group, "head", k) for k in (1, 2, 3)]
        grad_bc, send, keep = weight_parts(n_seq, groups, layer_input)
        got = swap(send, "dp", 1)
        own, s1, s2, s3 = pair_sum(keep, got)
        grad_w_bc = final_sum(1.0 / total_tokens, own, swap(s1, "seq", 1), swap(s2, "seq", 2), swap(s3, "seq", 3))
    else:
        grad_bc = lax.psum(group.astype(F32), "head").astype(BF16)
        part = jnp.einsum("td,tk->dk", layer_input[0], grad_bc, preferred_element_type=F32)
        grad_w_bc = lax.psum_scatter(part, ("dp", "seq"), scatter_dimension=0, tiled=True) / total_tokens
    grad_input = input_grad(grad_bc, w_bc)
    return y_out, grad_values, grad_input, grad_w_bc


def solution(mesh):
    in_specs = (
        P("dp", "seq", None),
        P("dp", "seq", "head"),
        P("dp", "head", "seq"),
        P(),
        P("head"),
        P("head"),
        P("head"),
        P("dp", "seq", "head"),
    )
    out_specs = (
        P("dp", "seq", "head"),
        P("dp", "seq", "head"),
        P("dp", "seq", None),
        P(("dp", "seq"), None),
    )
    return jax.shard_map(per_device, mesh=mesh, in_specs=in_specs, out_specs=out_specs, check_vma=False)
```

```python
import functools

import jax
import jax.numpy as jnp
from jax import lax
from jax.experimental import pallas as pl
from jax.experimental.pallas import tpu as pltpu
from jax.sharding import PartitionSpec as P

F32 = jnp.float32
BF16 = jnp.bfloat16
VMEM_SPEC = pl.BlockSpec(memory_space=pltpu.VMEM)
SMEM_SPEC = pl.BlockSpec(memory_space=pltpu.SMEM)
EXTRA = 16


def mm(a, b):
    return jnp.dot(a, b, preferred_element_type=F32)


def mm_t(a, b):
    return lax.dot_general(a, b, (((1,), (1,)), ((), ())), preferred_element_type=F32)


LIMIT = pltpu.CompilerParams(vmem_limit_bytes=20 << 20)
HBM_SPEC = pl.BlockSpec(memory_space=pltpu.HBM)
CHUNKS = 2


def log2(n):
    return n.bit_length() - 1


def spread_matrix(heads, width):
    rows = 8 * heads
    row = lax.broadcasted_iota(jnp.int32, (rows, 4 * width), 0)
    col = lax.broadcasted_iota(jnp.int32, (rows, 4 * width), 1)
    kind_ok = (row >> log2(2 * heads)) == (col >> log2(width))
    head_ok = (row & (heads - 1)) == ((col & (width - 1)) >> log2(width // heads))
    return jnp.where(kind_ok & head_ok, 1.0, 0.0).astype(BF16)


def states_kernel(
    n_seq, tokens_hbm, x_hbm, g_hbm, dt_hbm, w_hbm, rate_hbm, bias_hbm,
    bc_ref, cb_ref, rows_ref, decs_ref, spread_ref, scaled_ref, near_ref, coef_ref, pay1_ref, pay2_ref, pay3_ref,
    tok_ref, x_ref, g_ref, dt_ref, w_ref, rate_ref, bias_ref, sems,
):
    heads, length = dt_ref.shape
    chunk = length // CHUNKS
    width = x_ref.shape[1]
    copies = [
        pltpu.make_async_copy(dt_hbm.at[0], dt_ref, sems.at[0]),
        pltpu.make_async_copy(rate_hbm, rate_ref, sems.at[1]),
        pltpu.make_async_copy(bias_hbm, bias_ref, sems.at[2]),
        pltpu.make_async_copy(w_hbm, w_ref, sems.at[3]),
        pltpu.make_async_copy(tokens_hbm.at[0, :chunk], tok_ref.at[:chunk], sems.at[4]),
        pltpu.make_async_copy(x_hbm.at[0], x_ref, sems.at[5]),
        pltpu.make_async_copy(g_hbm.at[0], g_ref, sems.at[6]),
        pltpu.make_async_copy(tokens_hbm.at[0, chunk:], tok_ref.at[chunk:], sems.at[7]),
    ]
    for c in copies:
        c.start()
    spread = spread_matrix(heads, width)
    spread_ref[...] = spread
    for c in copies[:3]:
        c.wait()
    sub = lax.broadcasted_iota(jnp.int32, (heads, 1), 0)
    rate = jnp.zeros((heads, 1), F32)
    bias = jnp.zeros((heads, 1), F32)
    for h in range(heads):
        rate = jnp.where(sub == h, rate_ref[h], rate)
        bias = jnp.where(sub == h, bias_ref[h], bias)
    v = dt_ref[...] + bias
    log_step = -rate * (jnp.maximum(v, 0.0) + jnp.log1p(jnp.exp(-jnp.abs(v))))
    lane = lax.broadcasted_iota(jnp.int32, (heads, length), 1)
    cum = log_step
    shift = 1
    while shift < length:
        cum = cum + jnp.where(lane >= shift, pltpu.roll(cum, shift, 1), 0.0)
        shift *= 2
    prev = cum - log_step
    middle = cum[:, chunk - 1 : chunk]
    final = cum[:, length - 1 : length]
    second = lane >= chunk
    begin = jnp.where(second, middle, 0.0)
    end = jnp.where(second, final, middle)
    kinds = (jnp.exp(cum - begin), jnp.exp(end - prev), jnp.exp(jnp.minimum(prev - begin, 0.0)), jnp.exp(end - cum))
    parts = []
    for k in kinds:
        high = k.astype(BF16).astype(F32)
        parts += [high, k - high]
    decs = jnp.concatenate(parts, axis=0)
    decs_ref[...] = decs.astype(BF16)
    for p in range(heads // 2):
        rows_ref[p] = jnp.concatenate(
            [cum[2 * p : 2 * p + 1], prev[2 * p : 2 * p + 1], cum[2 * p + 1 : 2 * p + 2], prev[2 * p + 1 : 2 * p + 2]]
            + [jnp.zeros((4, length), F32)],
            axis=0,
        )
    head_of = lax.broadcasted_iota(jnp.int32, (heads, width), 1) >> log2(width // heads)
    mine = head_of == lax.broadcasted_iota(jnp.int32, (heads, width), 0)
    to_lanes = lambda col: jnp.sum(jnp.where(mine, col, 0.0), axis=0, keepdims=True)
    decay = to_lanes(jnp.exp(final))
    first_decay = to_lanes(jnp.exp(middle))
    second_decay = to_lanes(jnp.exp(final - middle))
    row8 = lax.broadcasted_iota(jnp.int32, (8, width), 0)
    coef_ref[...] = jnp.where(row8 == 0, first_decay, jnp.where(row8 == 1, second_decay, 0.0))
    high = decay.astype(BF16).astype(F32)
    row16 = lax.broadcasted_iota(jnp.int32, (EXTRA, width), 0)
    last = jnp.where(row16 == 0, high, jnp.where(row16 == 1, decay - high, 0.0)).astype(BF16)

    onward, backward = [], []
    for q in range(CHUNKS):
        at = slice(q * chunk, (q + 1) * chunk)
        e = mm(decs[:, at].T.astype(BF16), spread)
        if q == 0:
            copies[3].wait()
            copies[4].wait()
        else:
            copies[7].wait()
        projected = mm(tok_ref[at], w_ref[...])
        half = projected.shape[1] // 2
        bc_ref[at] = projected.astype(BF16)
        turned = pltpu.roll(projected, half, 1)
        cb_ref[at] = turned.astype(BF16)
        cb_t = turned.T.astype(BF16)
        if q == 0:
            copies[5].wait()
            copies[6].wait()
        x = x_ref[at].astype(F32)
        g = g_ref[at].astype(F32)
        g_up = (g * e[:, :width]).astype(BF16)
        g_down = (g * e[:, width : 2 * width]).astype(BF16)
        x_up = (x * e[:, 2 * width : 3 * width]).astype(BF16)
        x_down = (x * e[:, 3 * width :]).astype(BF16)
        scaled_ref[at, :width] = g_up
        scaled_ref[at, width : 2 * width] = g_down
        scaled_ref[at, 2 * width : 3 * width] = x_up
        scaled_ref[at, 3 * width :] = x_down
        onward.append(jnp.concatenate([mm(cb_t[:half], g_down), mm(cb_t[half:], x_down)], axis=0))
        backward.append(jnp.concatenate([mm(cb_t[:half], g_up), mm(cb_t[half:], x_up)], axis=0))

    near_ref[0] = onward[0]
    near_ref[1] = backward[1]
    next_total = (onward[0] * second_decay + onward[1]).astype(BF16)
    prior_total = (backward[0] + first_decay * backward[1]).astype(BF16)
    rows = next_total.shape[0]
    for k, ref in ((1, pay1_ref), (2, pay2_ref), (3, pay3_ref)):
        ref[rows:] = last
        if n_seq == 4:
            here = lax.axis_index("seq")
            up = (here ^ k) > here

            @pl.when(up)
            def _():
                ref[:rows] = next_total

            @pl.when(jnp.logical_not(up))
            def _():
                ref[:rows] = prior_total
        else:
            ref[:rows] = next_total if k == 1 else prior_total


def block_states(n_seq, tokens, x, g, dt, w, rate, bias):
    _, length, depth = tokens.shape
    width = x.shape[2]
    heads = dt.shape[1]
    two_n = w.shape[1]
    pay = jax.ShapeDtypeStruct((two_n + EXTRA, width), BF16)
    return pl.pallas_call(
        functools.partial(states_kernel, n_seq),
        name="block_states",
        in_specs=[HBM_SPEC] * 7,
        out_specs=[VMEM_SPEC] * 11,
        out_shape=[
            jax.ShapeDtypeStruct((length, two_n), BF16),
            jax.ShapeDtypeStruct((length, two_n), BF16),
            jax.ShapeDtypeStruct((heads // 2, 8, length), F32),
            jax.ShapeDtypeStruct((8 * heads, length), BF16),
            jax.ShapeDtypeStruct((8 * heads, 4 * width), BF16),
            jax.ShapeDtypeStruct((length, 4 * width), BF16),
            jax.ShapeDtypeStruct((2, two_n, width), F32),
            jax.ShapeDtypeStruct((8, width), F32),
            pay,
            pay,
            pay,
        ],
        scratch_shapes=[
            pltpu.VMEM((length, depth), BF16),
            pltpu.VMEM((length, width), BF16),
            pltpu.VMEM((length, width), BF16),
            pltpu.VMEM((heads, length), F32),
            pltpu.VMEM((depth, two_n), BF16),
            pltpu.SMEM((heads,), F32),
            pltpu.SMEM((heads,), F32),
            pltpu.SemaphoreType.DMA((8,)),
        ],
        compiler_params=LIMIT,
        cost_estimate=pl.CostEstimate(flops=2 * length * depth * two_n, bytes_accessed=5 << 20, transcendentals=0),
    )(*[pltpu.with_memory_space_constraint(a, pltpu.HBM) for a in (tokens, x, g, dt, w, rate, bias)])


def local_kernel(
    x_ref, g_ref, bc_ref, cb_ref, rows_ref, decs_ref, spread_ref, skip_ref,
    y_ref, gv_ref, gbc_ref, queries_ref, gvt_ref, gbt_ref, gc_ref,
):
    length, width = x_ref.shape[1:]
    lanes = 128
    n_pair = width // lanes
    chunk = length // CHUNKS
    tile = 128
    first_half = lax.broadcasted_iota(jnp.int32, (1, lanes), 1) < lanes // 2
    upper = lax.broadcasted_iota(jnp.int32, (lanes, 1), 0) < lanes // 2
    zero = jnp.zeros((), BF16)

    @pl.loop(0, CHUNKS)
    def _(q):
        s0 = pl.multiple_of(q * chunk, chunk)
        bc_s = bc_ref[pl.ds(s0, chunk), :]
        for tb in range(chunk // tile):
            t0 = pl.multiple_of(s0 + tb * tile, tile)
            cb_t = cb_ref[pl.ds(t0, tile), :]
            scores = mm_t(jnp.where(first_half, cb_t, zero), bc_s)
            row = tb * tile + lax.broadcasted_iota(jnp.int32, (tile, chunk), 0)
            col = lax.broadcasted_iota(jnp.int32, (tile, chunk), 1)
            below = col < row
            same = col == row
            total = None
            for p in range(n_pair):
                at = slice(p * lanes, (p + 1) * lanes)
                xp = x_ref[0, pl.ds(s0, chunk), at]
                x1, x2 = jnp.where(first_half, xp, zero), jnp.where(first_half, zero, xp)
                g_t = g_ref[0, pl.ds(t0, tile), at]
                gt = g_t.astype(F32).T.astype(BF16)
                cols = rows_ref[p, :, pl.ds(t0, tile)].T
                mains = []
                for k, xk in ((0, x1), (1, x2)):
                    gram = mm_t(g_t, xk)
                    cum_t, prev_t = cols[:, 2 * k : 2 * k + 1], cols[:, 2 * k + 1 : 2 * k + 2]
                    cum_s = rows_ref[p, 2 * k : 2 * k + 1, pl.ds(s0, chunk)]
                    prev_s = rows_ref[p, 2 * k + 1 : 2 * k + 2, pl.ds(s0, chunk)]
                    diff = jnp.minimum(jnp.where(below, cum_t - cum_s, prev_s - prev_t), 0.0)
                    kern = jnp.where(same, 0.0, jnp.exp(diff))
                    mains.append((scores * kern).astype(BF16))
                    term = gram * kern
                    total = term if total is None else total + term
                sk = jnp.where(first_half, skip_ref[2 * p], skip_ref[2 * p + 1])
                y = mm(mains[0], x1) + mm(mains[1], x2)
                y_ref[pl.ds(t0, tile), at] = y + sk * x_ref[0, pl.ds(t0, tile), at].astype(F32)
                gvt = mm(jnp.where(upper, gt, zero), mains[0]) + mm(jnp.where(upper, zero, gt), mains[1])
                if tb == 0:
                    gvt_ref[p] = gvt
                elif tb < chunk // tile - 1:
                    gvt_ref[p] += gvt
                else:
                    gs = g_ref[0, pl.ds(s0, chunk), at].astype(F32)
                    gv_ref[pl.ds(s0, chunk), at] = (gvt_ref[p] + gvt).T + sk * gs
            total = total.astype(BF16)
            gc_ref[tb * tile : (tb + 1) * tile] = mm(total, cb_ref[pl.ds(s0, chunk), :])
            gbt = mm(cb_t.astype(F32).T.astype(BF16), total)
            if tb == 0:
                gbt_ref[...] = gbt
            else:
                gbt_ref[...] += gbt
        gbc_ref[pl.ds(s0, chunk), :] = jnp.where(first_half, gbt_ref[...].T, gc_ref[...])

        e = mm(decs_ref[:, pl.ds(s0, chunk)].astype(F32).T.astype(BF16), spread_ref[...])
        bc = bc_s.astype(F32)
        cb = cb_ref[pl.ds(s0, chunk), :].astype(F32)
        cc, bb = jnp.where(first_half, cb, bc), jnp.where(first_half, bc, cb)
        for j, (query, kind) in enumerate(((cc, 0), (cc, 1), (bb, 2), (bb, 3))):
            for p in range(n_pair):
                value = query * e[:, kind * width + p * lanes : kind * width + (p + 1) * lanes]
                to = (j // 2) * 2 * width + p * 2 * lanes + (j % 2) * lanes
                queries_ref[pl.ds(s0, chunk), to : to + lanes] = value.astype(BF16)


def inside_chunks(x, g, bc, cb, rows, decs, spread, skip):
    _, length, width = x.shape
    n_pair = width // 128
    chunk = length // CHUNKS
    return pl.pallas_call(
        local_kernel,
        name="inside_chunks",
        in_specs=[VMEM_SPEC] * 7 + [SMEM_SPEC],
        out_specs=[VMEM_SPEC] * 4,
        out_shape=[
            jax.ShapeDtypeStruct((length, width), F32),
            jax.ShapeDtypeStruct((length, width), F32),
            jax.ShapeDtypeStruct((length, 128), F32),
            jax.ShapeDtypeStruct((length, 4 * width), BF16),
        ],
        scratch_shapes=[
            pltpu.VMEM((n_pair, 128, chunk), F32),
            pltpu.VMEM((128, chunk), F32),
            pltpu.VMEM((chunk, 128), F32),
        ],
        compiler_params=LIMIT,
        cost_estimate=pl.CostEstimate(
            flops=6 * length * length * width, bytes_accessed=4 << 20, transcendentals=2 * n_pair * length * length
        ),
    )(x, g, bc, cb, rows, decs, spread, skip)


def carry_kernel(
    direct, r1_ref, r2_ref, r3_ref, near_ref, coef_ref, queries_ref, scaled_ref, y_ref, gv_ref, gbc_ref,
    yo_ref, gvo_ref, group_ref, before_ref, after_ref,
):
    step = pl.program_id(0)
    _, two_n, width = before_ref.shape
    chunk = group_ref.shape[0]
    lanes = 128
    half = two_n // 2

    @pl.when(step == 0)
    def _():
        if direct:
            here = lax.axis_index("seq")
            refs = (r1_ref, r2_ref, r3_ref)
            decays = [r[two_n : two_n + 1].astype(F32) + r[two_n + 1 : two_n + 2].astype(F32) for r in refs]
            before = jnp.zeros((two_n, width), F32)
            after = jnp.zeros((two_n, width), F32)
            for k in (1, 2, 3):
                there = here ^ k
                low, high = jnp.minimum(here, there), jnp.maximum(here, there)
                factor = jnp.ones((1, width), F32)
                for m in (1, 2, 3):
                    if m != k:
                        mid = here ^ m
                        inside = jnp.logical_and(mid > low, mid < high)
                        factor = factor * jnp.where(inside, decays[m - 1], 1.0)
                part = refs[k - 1][:two_n].astype(F32)
                earlier = there < here
                before = before + part * jnp.where(earlier, factor, 0.0)
                after = after + part * jnp.where(earlier, 0.0, factor)
        else:
            before = r1_ref[:two_n].astype(F32)
            after = r2_ref[:two_n].astype(F32)
        before_ref[0] = before.astype(BF16)
        before_ref[1] = (near_ref[0] + coef_ref[0:1] * before).astype(BF16)
        after_ref[0] = (near_ref[1] + coef_ref[1:2] * after).astype(BF16)
        after_ref[1] = after.astype(BF16)

    before = before_ref[step]
    after = after_ref[step]
    first_half = lax.broadcasted_iota(jnp.int32, (1, lanes), 1) < lanes // 2
    zero = jnp.zeros((), BF16)
    s0 = pl.multiple_of(step * chunk, chunk)

    def apart(v):
        return [jnp.where(first_half, v, zero), jnp.where(first_half, zero, v)]

    for p in range(width // lanes):
        at = slice(p * lanes, (p + 1) * lanes)
        main = jnp.concatenate(apart(before[half:, at]) + apart(after[half:, at]), axis=0)
        back = jnp.concatenate(apart(before[:half, at]) + apart(after[:half, at]), axis=0)
        wide = slice(2 * p * lanes, 2 * (p + 1) * lanes)
        wide2 = slice(2 * width + 2 * p * lanes, 2 * width + 2 * (p + 1) * lanes)
        yo_ref[:, at] = (y_ref[pl.ds(s0, chunk), at] + mm(queries_ref[pl.ds(s0, chunk), wide], main)).astype(BF16)
        gvo_ref[:, at] = (gv_ref[pl.ds(s0, chunk), at] + mm(queries_ref[pl.ds(s0, chunk), wide2], back)).astype(BF16)
    both = jnp.concatenate([before, after], axis=1)
    from_g = mm_t(scaled_ref[pl.ds(s0, chunk), : 2 * width], both)
    from_x = mm_t(scaled_ref[pl.ds(s0, chunk), 2 * width :], both)
    group_ref[...] = (gbc_ref[pl.ds(s0, chunk), :] + jnp.where(first_half, from_x, from_g)).astype(BF16)


def add_carries(direct, r1, r2, r3, near, coef, queries, scaled, y, gv, gbc):
    length, width = y.shape
    two_n = gbc.shape[1]
    chunk = length // CHUNKS
    part3 = pl.BlockSpec((None, chunk, width), lambda i: (0, i, 0))
    return pl.pallas_call(
        functools.partial(carry_kernel, direct),
        name="add_carries",
        grid=(CHUNKS,),
        in_specs=[VMEM_SPEC] * 10,
        out_specs=[part3, part3, pl.BlockSpec((chunk, two_n), lambda i: (i, 0))],
        out_shape=[
            jax.ShapeDtypeStruct((1, length, width), BF16),
            jax.ShapeDtypeStruct((1, length, width), BF16),
            jax.ShapeDtypeStruct((length, two_n), BF16),
        ],
        scratch_shapes=[
            pltpu.VMEM((CHUNKS, two_n, width), BF16),
            pltpu.VMEM((CHUNKS, two_n, width), BF16),
        ],
        compiler_params=LIMIT,
        cost_estimate=pl.CostEstimate(flops=16 * length * two_n * width, bytes_accessed=5 << 20, transcendentals=0),
    )(r1, r2, r3, near, coef, queries, scaled, y, gv, gbc)


def scanned_generic(onward, backward, two_n):
    size, here = lax.axis_size("seq"), lax.axis_index("seq")

    def total(payload, reverse):
        every = lax.all_gather(payload, "seq")

        def step(k, before):
            at = size - 1 - k if reverse else k
            one = every[at].astype(F32)
            new = before * (one[two_n : two_n + 1] + one[two_n + 1 : two_n + 2]) + one[:two_n]
            return jnp.where(at > here if reverse else at < here, new, before)

        return lax.fori_loop(0, size, step, jnp.zeros((two_n, payload.shape[1]), F32))

    pad = lambda v: jnp.pad(v.astype(BF16), ((0, EXTRA), (0, 0)))
    return pad(total(onward, False)), pad(total(backward, True))


def weight_kernel(a0_ref, a1_ref, a2_ref, a3_ref, tokens_ref, grad_ref, send_ref, keep_ref):
    total = a0_ref[...].astype(F32) + a1_ref[...].astype(F32) + a2_ref[...].astype(F32) + a3_ref[...].astype(F32)
    grad = total.astype(BF16)
    grad_ref[...] = grad
    grad_t = grad.astype(F32).T.astype(BF16)
    here = lax.axis_index("dp")
    n_seq, _, cols = keep_ref.shape
    for s in range(n_seq):
        away = pl.multiple_of(((1 - here) * n_seq + s) * cols, cols)
        send_ref[s] = mm(grad_t, tokens_ref[:, pl.ds(away, cols)]).astype(BF16)
    for s in range(n_seq):
        home = pl.multiple_of((here * n_seq + s) * cols, cols)
        keep_ref[s] = mm(grad_t, tokens_ref[:, pl.ds(home, cols)])


def weight_parts(n_seq, groups, tokens):
    _, length, depth = tokens.shape
    two_n = groups[0].shape[1]
    cols = depth // (2 * n_seq)
    return pl.pallas_call(
        weight_kernel,
        name="weight_parts",
        grid=(1,),
        in_specs=[pl.BlockSpec((length, two_n), lambda i: (0, 0))] * 4
        + [pl.BlockSpec((None, length, depth), lambda i: (0, 0, 0))],
        out_specs=[
            pl.BlockSpec((length, two_n), lambda i: (0, 0)),
            pl.BlockSpec((n_seq, two_n, cols), lambda i: (0, 0, 0)),
            pl.BlockSpec((n_seq, two_n, cols), lambda i: (0, 0, 0)),
        ],
        out_shape=[
            jax.ShapeDtypeStruct((length, two_n), BF16),
            jax.ShapeDtypeStruct((n_seq, two_n, cols), BF16),
            jax.ShapeDtypeStruct((n_seq, two_n, cols), F32),
        ],
        compiler_params=LIMIT,
        cost_estimate=pl.CostEstimate(flops=2 * length * two_n * depth, bytes_accessed=4 << 20, transcendentals=0),
    )(*groups, tokens)


def pair_kernel(keep_ref, got_ref, own_ref, s1_ref, s2_ref, s3_ref):
    here = lax.axis_index("seq")
    own_ref[...] = keep_ref[here] + got_ref[here].astype(F32)
    for k, ref in ((1, s1_ref), (2, s2_ref), (3, s3_ref)):
        at = here ^ k
        ref[...] = (keep_ref[at] + got_ref[at].astype(F32)).astype(BF16)


def pair_sum(keep, got):
    _, two_n, cols = keep.shape
    small = jax.ShapeDtypeStruct((two_n, cols), BF16)
    return pl.pallas_call(
        pair_kernel,
        name="pair_sum",
        compiler_params=LIMIT,
        in_specs=[VMEM_SPEC, VMEM_SPEC],
        out_specs=[VMEM_SPEC] * 4,
        out_shape=[jax.ShapeDtypeStruct((two_n, cols), F32), small, small, small],
    )(keep, got)


def final_kernel(scale, own_ref, r1_ref, r2_ref, r3_ref, out_ref):
    total = own_ref[...] + r1_ref[...].astype(F32) + r2_ref[...].astype(F32) + r3_ref[...].astype(F32)
    out_ref[...] = total.T * scale


def final_sum(scale, own, r1, r2, r3):
    two_n, cols = own.shape
    return pl.pallas_call(
        functools.partial(final_kernel, scale),
        name="final_sum",
        compiler_params=LIMIT,
        in_specs=[VMEM_SPEC] * 4,
        out_specs=VMEM_SPEC,
        out_shape=jax.ShapeDtypeStruct((cols, two_n), F32),
    )(own, r1, r2, r3)


def input_kernel(grad_ref, w_ref, out_ref):
    out_ref[...] = mm_t(grad_ref[...], w_ref[...]).astype(BF16)


def input_grad(grad, w):
    length, two_n = grad.shape
    depth = w.shape[0]
    steps = 4
    chunk = length // steps
    return pl.pallas_call(
        input_kernel,
        name="input_grad",
        grid=(steps,),
        in_specs=[pl.BlockSpec((chunk, two_n), lambda i: (i, 0)), pl.BlockSpec((depth, two_n), lambda i: (0, 0))],
        out_specs=pl.BlockSpec((None, chunk, depth), lambda i: (0, i, 0)),
        out_shape=jax.ShapeDtypeStruct((1, length, depth), BF16),
        compiler_params=LIMIT,
        cost_estimate=pl.CostEstimate(flops=2 * length * two_n * depth, bytes_accessed=3 << 20, transcendentals=0),
    )(grad, w)


def swap(value, axis, k):
    return lax.ppermute(value, axis, [(i, i ^ k) for i in range(lax.axis_size(axis))])


def per_device(layer_input, head_values, dt_raw, w_bc, decay_rate, dt_bias, skip_gain, grad_y):
    n_seq, n_head, n_dp = lax.axis_size("seq"), lax.axis_size("head"), lax.axis_size("dp")
    length = layer_input.shape[1]
    two_n = w_bc.shape[1]
    bc, cb, rows, decs, spread, scaled, near, coef, pay1, pay2, pay3 = block_states(
        n_seq, layer_input, head_values, grad_y, dt_raw, w_bc, decay_rate, dt_bias
    )
    direct = n_seq == 4
    if direct:
        r1, r2, r3 = swap(pay1, "seq", 1), swap(pay2, "seq", 2), swap(pay3, "seq", 3)
    else:
        r1, r2 = scanned_generic(pay1, pay2, two_n)
        r3 = r2
    y_local, gv_local, gbc_local, queries = inside_chunks(
        head_values, grad_y, bc, cb, rows, decs, spread, skip_gain
    )
    y_out, grad_values, group = add_carries(
        direct, r1, r2, r3, near, coef, queries, scaled, y_local, gv_local, gbc_local
    )
    total_tokens = n_dp * n_seq * length
    if direct and n_dp == 2 and n_head == 4:
        groups = [group] + [swap(group, "head", k) for k in (1, 2, 3)]
        grad_bc, send, keep = weight_parts(n_seq, groups, layer_input)
        got = swap(send, "dp", 1)
        own, s1, s2, s3 = pair_sum(keep, got)
        grad_w_bc = final_sum(1.0 / total_tokens, own, swap(s1, "seq", 1), swap(s2, "seq", 2), swap(s3, "seq", 3))
    else:
        grad_bc = lax.psum(group.astype(F32), "head").astype(BF16)
        part = jnp.einsum("td,tk->dk", layer_input[0], grad_bc, preferred_element_type=F32)
        grad_w_bc = lax.psum_scatter(part, ("dp", "seq"), scatter_dimension=0, tiled=True) / total_tokens
    grad_input = input_grad(grad_bc, w_bc)
    return y_out, grad_values, grad_input, grad_w_bc


def solution(mesh):
    in_specs = (
        P("dp", "seq", None),
        P("dp", "seq", "head"),
        P("dp", "head", "seq"),
        P(),
        P("head"),
        P("head"),
        P("head"),
        P("dp", "seq", "head"),
    )
    out_specs = (
        P("dp", "seq", "head"),
        P("dp", "seq", "head"),
        P("dp", "seq", None),
        P(("dp", "seq"), None),
    )
    return jax.shard_map(per_device, mesh=mesh, in_specs=in_specs, out_specs=out_specs, check_vma=False)
```

```python
import functools

import jax
import jax.numpy as jnp
from jax import lax
from jax.experimental import pallas as pl
from jax.experimental.pallas import tpu as pltpu
from jax.sharding import PartitionSpec as P

F32 = jnp.float32
BF16 = jnp.bfloat16
VMEM_SPEC = pl.BlockSpec(memory_space=pltpu.VMEM)
SMEM_SPEC = pl.BlockSpec(memory_space=pltpu.SMEM)
EXTRA = 8


def mm(a, b):
    return jnp.dot(a, b, preferred_element_type=F32)


def mm_t(a, b):
    return lax.dot_general(a, b, (((1,), (1,)), ((), ())), preferred_element_type=F32)


LIMIT = pltpu.CompilerParams(vmem_limit_bytes=20 << 20)
HBM_SPEC = pl.BlockSpec(memory_space=pltpu.HBM)
CHUNKS = 2


def log2(n):
    return n.bit_length() - 1


def spread_matrix(heads, width):
    rows = 8 * heads
    row = lax.broadcasted_iota(jnp.int32, (rows, 4 * width), 0)
    col = lax.broadcasted_iota(jnp.int32, (rows, 4 * width), 1)
    kind_ok = (row >> log2(2 * heads)) == (col >> log2(width))
    head_ok = (row & (heads - 1)) == ((col & (width - 1)) >> log2(width // heads))
    return jnp.where(kind_ok & head_ok, 1.0, 0.0).astype(BF16)


def states_kernel(
    n_seq, tokens_hbm, x_hbm, g_hbm, dt_hbm, w_hbm, rate_hbm, bias_hbm,
    bc_ref, cb_ref, rows_ref, decs_ref, spread_ref, scaled_ref, near_ref, coef_ref, pay1_ref, pay2_ref, pay3_ref,
    tok_ref, x_ref, g_ref, dt_ref, w_ref, rate_ref, bias_ref, sems,
):
    heads, length = dt_ref.shape
    chunk = length // CHUNKS
    width = x_ref.shape[1]
    copies = [
        pltpu.make_async_copy(dt_hbm.at[0], dt_ref, sems.at[0]),
        pltpu.make_async_copy(rate_hbm, rate_ref, sems.at[1]),
        pltpu.make_async_copy(bias_hbm, bias_ref, sems.at[2]),
        pltpu.make_async_copy(g_hbm.at[0], g_ref, sems.at[3]),
        pltpu.make_async_copy(x_hbm.at[0], x_ref, sems.at[4]),
        pltpu.make_async_copy(w_hbm, w_ref, sems.at[5]),
        pltpu.make_async_copy(tokens_hbm.at[0, :chunk], tok_ref.at[:chunk], sems.at[6]),
        pltpu.make_async_copy(tokens_hbm.at[0, chunk:], tok_ref.at[chunk:], sems.at[7]),
    ]
    for c in copies:
        c.start()
    spread = spread_matrix(heads, width)
    spread_ref[...] = spread
    for c in copies[:3]:
        c.wait()
    sub = lax.broadcasted_iota(jnp.int32, (heads, 1), 0)
    rate = jnp.zeros((heads, 1), F32)
    bias = jnp.zeros((heads, 1), F32)
    for h in range(heads):
        rate = jnp.where(sub == h, rate_ref[h], rate)
        bias = jnp.where(sub == h, bias_ref[h], bias)
    v = dt_ref[...] + bias
    log_step = -rate * (jnp.maximum(v, 0.0) + jnp.log1p(jnp.exp(-jnp.abs(v))))
    lane = lax.broadcasted_iota(jnp.int32, (heads, length), 1)
    cum = log_step
    shift = 1
    while shift < length:
        cum = cum + jnp.where(lane >= shift, pltpu.roll(cum, shift, 1), 0.0)
        shift *= 2
    prev = cum - log_step
    middle = cum[:, chunk - 1 : chunk]
    final = cum[:, length - 1 : length]
    second = lane >= chunk
    begin = jnp.where(second, middle, 0.0)
    end = jnp.where(second, final, middle)
    kinds = (jnp.exp(cum - begin), jnp.exp(end - prev), jnp.exp(jnp.minimum(prev - begin, 0.0)), jnp.exp(end - cum))
    parts = []
    for k in kinds:
        high = k.astype(BF16).astype(F32)
        parts += [high, k - high]
    decs = jnp.concatenate(parts, axis=0)
    decs_ref[...] = decs.astype(BF16)
    for p in range(heads // 2):
        rows_ref[p] = jnp.concatenate(
            [cum[2 * p : 2 * p + 1], prev[2 * p : 2 * p + 1], cum[2 * p + 1 : 2 * p + 2], prev[2 * p + 1 : 2 * p + 2]]
            + [jnp.zeros((4, length), F32)],
            axis=0,
        )
    head_of = lax.broadcasted_iota(jnp.int32, (heads, width), 1) >> log2(width // heads)
    mine = head_of == lax.broadcasted_iota(jnp.int32, (heads, width), 0)
    to_lanes = lambda col: jnp.sum(jnp.where(mine, col, 0.0), axis=0, keepdims=True)
    decay = to_lanes(jnp.exp(final))
    first_decay = to_lanes(jnp.exp(middle))
    second_decay = to_lanes(jnp.exp(final - middle))
    row8 = lax.broadcasted_iota(jnp.int32, (8, width), 0)
    coef_ref[...] = jnp.where(row8 == 0, first_decay, jnp.where(row8 == 1, second_decay, 0.0))
    high = decay.astype(BF16).astype(F32)
    row_e = lax.broadcasted_iota(jnp.int32, (EXTRA, width), 0)
    last = jnp.where(row_e == 0, high, jnp.where(row_e == 1, decay - high, 0.0)).astype(BF16)

    copies[3].wait()
    copies[4].wait()
    for q in range(CHUNKS):
        at = slice(q * chunk, (q + 1) * chunk)
        spread_decs = decs[:, at].T.astype(BF16)
        for j, (ref, kind) in enumerate(((g_ref, 0), (g_ref, 1), (x_ref, 2), (x_ref, 3))):
            to = slice(j * width, (j + 1) * width)
            scaled_ref[at, to] = (ref[at].astype(F32) * mm(spread_decs, spread[:, to])).astype(BF16)
    copies[5].wait()
    onward, backward = [], []
    for q in range(CHUNKS):
        at = slice(q * chunk, (q + 1) * chunk)
        copies[6 + q].wait()
        projected = mm(tok_ref[at], w_ref[...])
        half = projected.shape[1] // 2
        bc_ref[at] = projected.astype(BF16)
        turned = pltpu.roll(projected, half, 1)
        cb_ref[at] = turned.astype(BF16)
        cb_t = turned.T.astype(BF16)
        parts = [scaled_ref[at, j * width : (j + 1) * width] for j in range(4)]
        onward.append(jnp.concatenate([mm(cb_t[:half], parts[1]), mm(cb_t[half:], parts[3])], axis=0))
        backward.append(jnp.concatenate([mm(cb_t[:half], parts[0]), mm(cb_t[half:], parts[2])], axis=0))

    near_ref[0] = onward[0]
    near_ref[1] = backward[1]
    next_total = (onward[0] * second_decay + onward[1]).astype(BF16)
    prior_total = (backward[0] + first_decay * backward[1]).astype(BF16)
    rows = next_total.shape[0]
    for k, ref in ((1, pay1_ref), (2, pay2_ref), (3, pay3_ref)):
        ref[rows:] = last
        if n_seq == 4:
            here = lax.axis_index("seq")
            up = (here ^ k) > here

            @pl.when(up)
            def _():
                ref[:rows] = next_total

            @pl.when(jnp.logical_not(up))
            def _():
                ref[:rows] = prior_total
        else:
            ref[:rows] = next_total if k == 1 else prior_total


def block_states(n_seq, tokens, x, g, dt, w, rate, bias):
    _, length, depth = tokens.shape
    width = x.shape[2]
    heads = dt.shape[1]
    two_n = w.shape[1]
    pay = jax.ShapeDtypeStruct((two_n + EXTRA, width), BF16)
    return pl.pallas_call(
        functools.partial(states_kernel, n_seq),
        name="block_states",
        in_specs=[HBM_SPEC] * 7,
        out_specs=[VMEM_SPEC] * 11,
        out_shape=[
            jax.ShapeDtypeStruct((length, two_n), BF16),
            jax.ShapeDtypeStruct((length, two_n), BF16),
            jax.ShapeDtypeStruct((heads // 2, 8, length), F32),
            jax.ShapeDtypeStruct((8 * heads, length), BF16),
            jax.ShapeDtypeStruct((8 * heads, 4 * width), BF16),
            jax.ShapeDtypeStruct((length, 4 * width), BF16),
            jax.ShapeDtypeStruct((2, two_n, width), F32),
            jax.ShapeDtypeStruct((8, width), F32),
            pay,
            pay,
            pay,
        ],
        scratch_shapes=[
            pltpu.VMEM((length, depth), BF16),
            pltpu.VMEM((length, width), BF16),
            pltpu.VMEM((length, width), BF16),
            pltpu.VMEM((heads, length), F32),
            pltpu.VMEM((depth, two_n), BF16),
            pltpu.SMEM((heads,), F32),
            pltpu.SMEM((heads,), F32),
            pltpu.SemaphoreType.DMA((8,)),
        ],
        compiler_params=LIMIT,
        cost_estimate=pl.CostEstimate(flops=2 * length * depth * two_n, bytes_accessed=5 << 20, transcendentals=0),
    )(*[pltpu.with_memory_space_constraint(a, pltpu.HBM) for a in (tokens, x, g, dt, w, rate, bias)])


def local_kernel(
    x_ref, g_ref, bc_ref, cb_ref, rows_ref, decs_ref, spread_ref, skip_ref,
    y_ref, gv_ref, gbc_ref, queries_ref, gvt_ref, gbt_ref, gc_ref,
):
    length, width = x_ref.shape[1:]
    lanes = 128
    n_pair = width // lanes
    chunk = length // CHUNKS
    tile = 128
    first_half = lax.broadcasted_iota(jnp.int32, (1, lanes), 1) < lanes // 2
    upper = lax.broadcasted_iota(jnp.int32, (lanes, 1), 0) < lanes // 2
    zero = jnp.zeros((), BF16)

    @pl.loop(0, CHUNKS)
    def _(q):
        s0 = pl.multiple_of(q * chunk, chunk)
        bc_s = bc_ref[pl.ds(s0, chunk), :]
        for tb in range(chunk // tile):
            t0 = pl.multiple_of(s0 + tb * tile, tile)
            cb_t = cb_ref[pl.ds(t0, tile), :]
            scores = mm_t(jnp.where(first_half, cb_t, zero), bc_s)
            row = tb * tile + lax.broadcasted_iota(jnp.int32, (tile, chunk), 0)
            col = lax.broadcasted_iota(jnp.int32, (tile, chunk), 1)
            below = col < row
            same = col == row
            total = None
            for p in range(n_pair):
                at = slice(p * lanes, (p + 1) * lanes)
                xp = x_ref[0, pl.ds(s0, chunk), at]
                x1, x2 = jnp.where(first_half, xp, zero), jnp.where(first_half, zero, xp)
                g_t = g_ref[0, pl.ds(t0, tile), at]
                gt = g_t.astype(F32).T.astype(BF16)
                cols = rows_ref[p, :, pl.ds(t0, tile)].T
                mains = []
                for k, xk in ((0, x1), (1, x2)):
                    gram = mm_t(g_t, xk)
                    cum_t, prev_t = cols[:, 2 * k : 2 * k + 1], cols[:, 2 * k + 1 : 2 * k + 2]
                    cum_s = rows_ref[p, 2 * k : 2 * k + 1, pl.ds(s0, chunk)]
                    prev_s = rows_ref[p, 2 * k + 1 : 2 * k + 2, pl.ds(s0, chunk)]
                    diff = jnp.minimum(jnp.where(below, cum_t - cum_s, prev_s - prev_t), 0.0)
                    kern = jnp.where(same, 0.0, jnp.exp(diff))
                    mains.append((scores * kern).astype(BF16))
                    term = gram * kern
                    total = term if total is None else total + term
                sk = jnp.where(first_half, skip_ref[2 * p], skip_ref[2 * p + 1])
                y = mm(mains[0], x1) + mm(mains[1], x2)
                y_ref[pl.ds(t0, tile), at] = y + sk * x_ref[0, pl.ds(t0, tile), at].astype(F32)
                gvt = mm(jnp.where(upper, gt, zero), mains[0]) + mm(jnp.where(upper, zero, gt), mains[1])
                if tb == 0:
                    gvt_ref[p] = gvt
                elif tb < chunk // tile - 1:
                    gvt_ref[p] += gvt
                else:
                    gs = g_ref[0, pl.ds(s0, chunk), at].astype(F32)
                    gv_ref[pl.ds(s0, chunk), at] = (gvt_ref[p] + gvt).T + sk * gs
            total = total.astype(BF16)
            gc_ref[tb * tile : (tb + 1) * tile] = mm(total, cb_ref[pl.ds(s0, chunk), :])
            gbt = mm(cb_t.astype(F32).T.astype(BF16), total)
            if tb == 0:
                gbt_ref[...] = gbt
            else:
                gbt_ref[...] += gbt
        gbc_ref[pl.ds(s0, chunk), :] = jnp.where(first_half, gbt_ref[...].T, gc_ref[...])

        e = mm(decs_ref[:, pl.ds(s0, chunk)].astype(F32).T.astype(BF16), spread_ref[...])
        bc = bc_s.astype(F32)
        cb = cb_ref[pl.ds(s0, chunk), :].astype(F32)
        cc, bb = jnp.where(first_half, cb, bc), jnp.where(first_half, bc, cb)
        for j, (query, kind) in enumerate(((cc, 0), (cc, 1), (bb, 2), (bb, 3))):
            for p in range(n_pair):
                value = query * e[:, kind * width + p * lanes : kind * width + (p + 1) * lanes]
                to = (j // 2) * 2 * width + p * 2 * lanes + (j % 2) * lanes
                queries_ref[pl.ds(s0, chunk), to : to + lanes] = value.astype(BF16)


def inside_chunks(x, g, bc, cb, rows, decs, spread, skip):
    _, length, width = x.shape
    n_pair = width // 128
    chunk = length // CHUNKS
    return pl.pallas_call(
        local_kernel,
        name="inside_chunks",
        in_specs=[VMEM_SPEC] * 7 + [SMEM_SPEC],
        out_specs=[VMEM_SPEC] * 4,
        out_shape=[
            jax.ShapeDtypeStruct((length, width), F32),
            jax.ShapeDtypeStruct((length, width), F32),
            jax.ShapeDtypeStruct((length, 128), F32),
            jax.ShapeDtypeStruct((length, 4 * width), BF16),
        ],
        scratch_shapes=[
            pltpu.VMEM((n_pair, 128, chunk), F32),
            pltpu.VMEM((128, chunk), F32),
            pltpu.VMEM((chunk, 128), F32),
        ],
        compiler_params=LIMIT,
        cost_estimate=pl.CostEstimate(
            flops=6 * length * length * width, bytes_accessed=4 << 20, transcendentals=2 * n_pair * length * length
        ),
    )(x, g, bc, cb, rows, decs, spread, skip)


def combine_received(direct, refs, two_n):
    if not direct:
        return refs[0][:two_n].astype(F32), refs[1][:two_n].astype(F32)
    here = lax.axis_index("seq")
    width = refs[0].shape[1]
    decays = [r[two_n : two_n + 1].astype(F32) + r[two_n + 1 : two_n + 2].astype(F32) for r in refs]
    before = jnp.zeros((two_n, width), F32)
    after = jnp.zeros((two_n, width), F32)
    for k in (1, 2, 3):
        there = here ^ k
        low, high = jnp.minimum(here, there), jnp.maximum(here, there)
        factor = jnp.ones((1, width), F32)
        for m in (1, 2, 3):
            if m != k:
                mid = here ^ m
                inside = jnp.logical_and(mid > low, mid < high)
                factor = factor * jnp.where(inside, decays[m - 1], 1.0)
        part = refs[k - 1][:two_n].astype(F32)
        earlier = there < here
        before = before + part * jnp.where(earlier, factor, 0.0)
        after = after + part * jnp.where(earlier, 0.0, factor)
    return before, after


def group_kernel(
    direct, r3_ref, r2_ref, r1_ref, near_ref, coef_ref, scaled_ref, gbc_ref, group_ref, before_ref, after_ref
):
    length, two_n = group_ref.shape
    width = coef_ref.shape[1]
    chunk = length // CHUNKS
    before, after = combine_received(direct, (r1_ref, r2_ref, r3_ref), two_n)
    befores = [before.astype(BF16), (near_ref[0] + coef_ref[0:1] * before).astype(BF16)]
    afters = [(near_ref[1] + coef_ref[1:2] * after).astype(BF16), after.astype(BF16)]
    left = lax.broadcasted_iota(jnp.int32, (1, two_n), 1) < two_n // 2
    for q in range(CHUNKS):
        at = slice(q * chunk, (q + 1) * chunk)
        before_ref[q] = befores[q]
        after_ref[q] = afters[q]
        both = jnp.concatenate([befores[q], afters[q]], axis=1)
        from_g = mm_t(scaled_ref[at, : 2 * width], both)
        from_x = mm_t(scaled_ref[at, 2 * width :], both)
        group_ref[at] = (gbc_ref[at] + jnp.where(left, from_x, from_g)).astype(BF16)


def group_sums(direct, r3, r2, r1, near, coef, scaled, gbc):
    length, two_n = gbc.shape
    width = coef.shape[1]
    state = jax.ShapeDtypeStruct((CHUNKS, two_n, width), BF16)
    return pl.pallas_call(
        functools.partial(group_kernel, direct),
        name="group_sums",
        in_specs=[VMEM_SPEC] * 7,
        out_specs=[VMEM_SPEC] * 3,
        out_shape=[jax.ShapeDtypeStruct((length, two_n), BF16), state, state],
        compiler_params=LIMIT,
        cost_estimate=pl.CostEstimate(flops=8 * length * two_n * width, bytes_accessed=3 << 20, transcendentals=0),
    )(r3, r2, r1, near, coef, scaled, gbc)


def carry_kernel(before_ref, after_ref, queries_ref, y_ref, gv_ref, yo_ref, gvo_ref):
    step = pl.program_id(0)
    _, two_n, width = before_ref.shape
    chunk = yo_ref.shape[0]
    lanes = 128
    half = two_n // 2
    before = before_ref[step]
    after = after_ref[step]
    first_half = lax.broadcasted_iota(jnp.int32, (1, lanes), 1) < lanes // 2
    zero = jnp.zeros((), BF16)
    s0 = pl.multiple_of(step * chunk, chunk)

    def apart(v):
        return [jnp.where(first_half, v, zero), jnp.where(first_half, zero, v)]

    for p in range(width // lanes):
        at = slice(p * lanes, (p + 1) * lanes)
        main = jnp.concatenate(apart(before[half:, at]) + apart(after[half:, at]), axis=0)
        back = jnp.concatenate(apart(before[:half, at]) + apart(after[:half, at]), axis=0)
        wide = slice(2 * p * lanes, 2 * (p + 1) * lanes)
        wide2 = slice(2 * width + 2 * p * lanes, 2 * width + 2 * (p + 1) * lanes)
        yo_ref[:, at] = (y_ref[pl.ds(s0, chunk), at] + mm(queries_ref[pl.ds(s0, chunk), wide], main)).astype(BF16)
        gvo_ref[:, at] = (gv_ref[pl.ds(s0, chunk), at] + mm(queries_ref[pl.ds(s0, chunk), wide2], back)).astype(BF16)


def add_carries(before, after, queries, y, gv):
    length, width = y.shape
    two_n = before.shape[1]
    chunk = length // CHUNKS
    part3 = pl.BlockSpec((None, chunk, width), lambda i: (0, i, 0))
    out = jax.ShapeDtypeStruct((1, length, width), BF16)
    return pl.pallas_call(
        carry_kernel,
        name="add_carries",
        grid=(CHUNKS,),
        in_specs=[VMEM_SPEC] * 5,
        out_specs=[part3, part3],
        out_shape=[out, out],
        compiler_params=LIMIT,
        cost_estimate=pl.CostEstimate(flops=8 * length * two_n * width, bytes_accessed=5 << 20, transcendentals=0),
    )(before, after, queries, y, gv)


def scanned_generic(onward, backward, two_n):
    size, here = lax.axis_size("seq"), lax.axis_index("seq")

    def total(payload, reverse):
        every = lax.all_gather(payload, "seq")

        def step(k, before):
            at = size - 1 - k if reverse else k
            one = every[at].astype(F32)
            new = before * (one[two_n : two_n + 1] + one[two_n + 1 : two_n + 2]) + one[:two_n]
            return jnp.where(at > here if reverse else at < here, new, before)

        return lax.fori_loop(0, size, step, jnp.zeros((two_n, payload.shape[1]), F32))

    pad = lambda v: jnp.pad(v.astype(BF16), ((0, EXTRA), (0, 0)))
    return pad(total(onward, False)), pad(total(backward, True))


def away_kernel(a0_ref, a1_ref, a2_ref, a3_ref, tokens_ref, grad_ref, grad_t_ref, send_ref):
    total = a0_ref[...].astype(F32) + a1_ref[...].astype(F32) + a2_ref[...].astype(F32) + a3_ref[...].astype(F32)
    grad = total.astype(BF16)
    grad_ref[...] = grad
    grad_t = grad.astype(F32).T.astype(BF16)
    grad_t_ref[...] = grad_t
    here = lax.axis_index("dp")
    n_seq, _, cols = send_ref.shape
    for s in range(n_seq):
        away = pl.multiple_of(((1 - here) * n_seq + s) * cols, cols)
        send_ref[s] = mm(grad_t, tokens_ref[0, :, pl.ds(away, cols)]).astype(BF16)


def home_kernel(grad_t_ref, tokens_ref, keep_ref):
    here = lax.axis_index("dp")
    n_seq, _, cols = keep_ref.shape
    for s in range(n_seq):
        home = pl.multiple_of((here * n_seq + s) * cols, cols)
        keep_ref[s] = mm(grad_t_ref[...], tokens_ref[0, :, pl.ds(home, cols)])


def weight_away(n_seq, groups, tokens):
    _, length, depth = tokens.shape
    two_n = groups[0].shape[1]
    cols = depth // (2 * n_seq)
    return pl.pallas_call(
        away_kernel,
        name="weight_away",
        in_specs=[VMEM_SPEC] * 5,
        out_specs=[VMEM_SPEC] * 3,
        out_shape=[
            jax.ShapeDtypeStruct((length, two_n), BF16),
            jax.ShapeDtypeStruct((two_n, length), BF16),
            jax.ShapeDtypeStruct((n_seq, two_n, cols), BF16),
        ],
        compiler_params=LIMIT,
        cost_estimate=pl.CostEstimate(flops=length * two_n * depth, bytes_accessed=2 << 20, transcendentals=0),
    )(*groups, tokens)


def weight_home(n_seq, grad_t, tokens):
    _, length, depth = tokens.shape
    two_n = grad_t.shape[0]
    cols = depth // (2 * n_seq)
    return pl.pallas_call(
        home_kernel,
        name="weight_home",
        in_specs=[VMEM_SPEC] * 2,
        out_specs=VMEM_SPEC,
        out_shape=jax.ShapeDtypeStruct((n_seq, two_n, cols), F32),
        compiler_params=LIMIT,
        cost_estimate=pl.CostEstimate(flops=length * two_n * depth, bytes_accessed=2 << 20, transcendentals=0),
    )(grad_t, tokens)


def pair_kernel(keep_ref, got_ref, own_ref, s1_ref, s2_ref, s3_ref):
    here = lax.axis_index("seq")
    own_ref[...] = keep_ref[here] + got_ref[here].astype(F32)
    for k, ref in ((1, s1_ref), (2, s2_ref), (3, s3_ref)):
        at = here ^ k
        ref[...] = (keep_ref[at] + got_ref[at].astype(F32)).astype(BF16)


def pair_sum(keep, got):
    _, two_n, cols = keep.shape
    small = jax.ShapeDtypeStruct((two_n, cols), BF16)
    return pl.pallas_call(
        pair_kernel,
        name="pair_sum",
        compiler_params=LIMIT,
        in_specs=[VMEM_SPEC, VMEM_SPEC],
        out_specs=[VMEM_SPEC] * 4,
        out_shape=[jax.ShapeDtypeStruct((two_n, cols), F32), small, small, small],
    )(keep, got)


def final_kernel(scale, own_ref, r3_ref, r2_ref, r1_ref, out_ref):
    total = own_ref[...] + r1_ref[...].astype(F32) + r2_ref[...].astype(F32) + r3_ref[...].astype(F32)
    out_ref[...] = total.T * scale


def final_sum(scale, own, r3, r2, r1):
    two_n, cols = own.shape
    return pl.pallas_call(
        functools.partial(final_kernel, scale),
        name="final_sum",
        compiler_params=LIMIT,
        in_specs=[VMEM_SPEC] * 4,
        out_specs=VMEM_SPEC,
        out_shape=jax.ShapeDtypeStruct((cols, two_n), F32),
    )(own, r3, r2, r1)


def input_kernel(grad_ref, w_ref, out_ref):
    out_ref[...] = mm_t(grad_ref[...], w_ref[...]).astype(BF16)


def input_grad(grad, w):
    length, two_n = grad.shape
    depth = w.shape[0]
    steps = 4
    chunk = length // steps
    return pl.pallas_call(
        input_kernel,
        name="input_grad",
        grid=(steps,),
        in_specs=[pl.BlockSpec((chunk, two_n), lambda i: (i, 0)), pl.BlockSpec((depth, two_n), lambda i: (0, 0))],
        out_specs=pl.BlockSpec((None, chunk, depth), lambda i: (0, i, 0)),
        out_shape=jax.ShapeDtypeStruct((1, length, depth), BF16),
        compiler_params=LIMIT,
        cost_estimate=pl.CostEstimate(flops=2 * length * two_n * depth, bytes_accessed=3 << 20, transcendentals=0),
    )(grad, w)


def swap(value, axis, k):
    return lax.ppermute(value, axis, [(i, i ^ k) for i in range(lax.axis_size(axis))])


def per_device(layer_input, head_values, dt_raw, w_bc, decay_rate, dt_bias, skip_gain, grad_y):
    n_seq, n_head, n_dp = lax.axis_size("seq"), lax.axis_size("head"), lax.axis_size("dp")
    length = layer_input.shape[1]
    two_n = w_bc.shape[1]
    bc, cb, rows, decs, spread, scaled, near, coef, pay1, pay2, pay3 = block_states(
        n_seq, layer_input, head_values, grad_y, dt_raw, w_bc, decay_rate, dt_bias
    )
    direct = n_seq == 4
    if direct:
        r3, r2, r1 = swap(pay3, "seq", 3), swap(pay2, "seq", 2), swap(pay1, "seq", 1)
    else:
        r1, r2 = scanned_generic(pay1, pay2, two_n)
        r3 = r2
    y_local, gv_local, gbc_local, queries = inside_chunks(
        head_values, grad_y, bc, cb, rows, decs, spread, skip_gain
    )
    group, before, after = group_sums(direct, r3, r2, r1, near, coef, scaled, gbc_local)
    total_tokens = n_dp * n_seq * length
    if direct and n_dp == 2 and n_head == 4:
        groups = [group] + [swap(group, "head", k) for k in (1, 2, 3)]
        y_out, grad_values = add_carries(before, after, queries, y_local, gv_local)
        grad_bc, grad_t, send = weight_away(n_seq, groups, layer_input)
        got = swap(send, "dp", 1)
        keep = weight_home(n_seq, grad_t, layer_input)
        own, s1, s2, s3 = pair_sum(keep, got)
        t3, t2, t1 = swap(s3, "seq", 3), swap(s2, "seq", 2), swap(s1, "seq", 1)
        grad_w_bc = final_sum(1.0 / total_tokens, own, t3, t2, t1)
    else:
        y_out, grad_values = add_carries(before, after, queries, y_local, gv_local)
        grad_bc = lax.psum(group.astype(F32), "head").astype(BF16)
        part = jnp.einsum("td,tk->dk", layer_input[0], grad_bc, preferred_element_type=F32)
        grad_w_bc = lax.psum_scatter(part, ("dp", "seq"), scatter_dimension=0, tiled=True) / total_tokens
    grad_input = input_grad(grad_bc, w_bc)
    return y_out, grad_values, grad_input, grad_w_bc


def solution(mesh):
    in_specs = (
        P("dp", "seq", None),
        P("dp", "seq", "head"),
        P("dp", "head", "seq"),
        P(),
        P("head"),
        P("head"),
        P("head"),
        P("dp", "seq", "head"),
    )
    out_specs = (
        P("dp", "seq", "head"),
        P("dp", "seq", "head"),
        P("dp", "seq", None),
        P(("dp", "seq"), None),
    )
    return jax.shard_map(per_device, mesh=mesh, in_specs=in_specs, out_specs=out_specs, check_vma=False)
```

```python
import functools

import jax
import jax.numpy as jnp
from jax import lax
from jax.experimental import pallas as pl
from jax.experimental.pallas import tpu as pltpu
from jax.sharding import PartitionSpec as P

F32 = jnp.float32
BF16 = jnp.bfloat16
VMEM_SPEC = pl.BlockSpec(memory_space=pltpu.VMEM)
SMEM_SPEC = pl.BlockSpec(memory_space=pltpu.SMEM)
LANES = 128
ORDER_A = (3, 2, 1)
ORDER_B = (3, 2, 1)
ORDER_C = (3, 2, 1)


def mm(a, b):
    return jnp.dot(a, b, preferred_element_type=F32)


def mm_t(a, b):
    return lax.dot_general(a, b, (((1,), (1,)), ((), ())), preferred_element_type=F32)


LIMIT = pltpu.CompilerParams(vmem_limit_bytes=20 << 20)
HBM_SPEC = pl.BlockSpec(memory_space=pltpu.HBM)
CHUNKS = 2


def log2(n):
    return n.bit_length() - 1


def spread_matrix(heads, width):
    rows = 8 * heads
    row = lax.broadcasted_iota(jnp.int32, (rows, 4 * width), 0)
    col = lax.broadcasted_iota(jnp.int32, (rows, 4 * width), 1)
    kind_ok = (row >> log2(2 * heads)) == (col >> log2(width))
    head_ok = (row & (heads - 1)) == ((col & (width - 1)) >> log2(width // heads))
    return jnp.where(kind_ok & head_ok, 1.0, 0.0).astype(BF16)


def pack(ref, state, decay):
    rows, width = state.shape
    blocks = width // LANES
    high = decay.astype(BF16).astype(F32)
    for p in range(blocks):
        ref[p * rows : (p + 1) * rows] = state[:, p * LANES : (p + 1) * LANES].astype(BF16)
    parts = [v[:, p * LANES : (p + 1) * LANES] for v in (high, decay - high) for p in range(blocks)]
    ref[blocks * rows :] = jnp.concatenate(parts, axis=0).astype(BF16)


def unpack(payload, rows):
    blocks = payload.shape[0] // (rows + 2)
    state = jnp.concatenate([payload[p * rows : (p + 1) * rows] for p in range(blocks)], axis=1).astype(F32)
    tail = payload[blocks * rows :].astype(F32)
    decay = jnp.concatenate([tail[p : p + 1] + tail[blocks + p : blocks + p + 1] for p in range(blocks)], axis=1)
    return state, decay


def states_kernel(
    n_seq, tokens_hbm, x_hbm, g_hbm, dt_hbm, w_hbm, rate_hbm, bias_hbm,
    bc_ref, cb_ref, rows_ref, decs_ref, spread_ref, scaled_ref, near_ref, coef_ref, pay1_ref, pay2_ref, pay3_ref,
    tok_ref, x_ref, g_ref, dt_ref, w_ref, rate_ref, bias_ref, sems,
):
    heads, length = dt_ref.shape
    chunk = length // CHUNKS
    width = x_ref.shape[1]
    copies = [
        pltpu.make_async_copy(dt_hbm.at[0], dt_ref, sems.at[0]),
        pltpu.make_async_copy(rate_hbm, rate_ref, sems.at[1]),
        pltpu.make_async_copy(bias_hbm, bias_ref, sems.at[2]),
        pltpu.make_async_copy(g_hbm.at[0], g_ref, sems.at[3]),
        pltpu.make_async_copy(x_hbm.at[0], x_ref, sems.at[4]),
        pltpu.make_async_copy(w_hbm, w_ref, sems.at[5]),
        pltpu.make_async_copy(tokens_hbm.at[0, :chunk], tok_ref.at[:chunk], sems.at[6]),
        pltpu.make_async_copy(tokens_hbm.at[0, chunk:], tok_ref.at[chunk:], sems.at[7]),
    ]
    for c in copies:
        c.start()
    spread = spread_matrix(heads, width)
    spread_ref[...] = spread
    for c in copies[:3]:
        c.wait()
    sub = lax.broadcasted_iota(jnp.int32, (heads, 1), 0)
    rate = jnp.zeros((heads, 1), F32)
    bias = jnp.zeros((heads, 1), F32)
    for h in range(heads):
        rate = jnp.where(sub == h, rate_ref[h], rate)
        bias = jnp.where(sub == h, bias_ref[h], bias)
    v = dt_ref[...] + bias
    log_step = -rate * (jnp.maximum(v, 0.0) + jnp.log1p(jnp.exp(-jnp.abs(v))))
    lane = lax.broadcasted_iota(jnp.int32, (heads, length), 1)
    cum = log_step
    shift = 1
    while shift < length:
        cum = cum + jnp.where(lane >= shift, pltpu.roll(cum, shift, 1), 0.0)
        shift *= 2
    prev = cum - log_step
    middle = cum[:, chunk - 1 : chunk]
    final = cum[:, length - 1 : length]
    second = lane >= chunk
    begin = jnp.where(second, middle, 0.0)
    end = jnp.where(second, final, middle)
    kinds = (jnp.exp(cum - begin), jnp.exp(end - prev), jnp.exp(jnp.minimum(prev - begin, 0.0)), jnp.exp(end - cum))
    parts = []
    for k in kinds:
        high = k.astype(BF16).astype(F32)
        parts += [high, k - high]
    decs = jnp.concatenate(parts, axis=0)
    decs_ref[...] = decs.astype(BF16)
    for p in range(heads // 2):
        rows_ref[p] = jnp.concatenate(
            [cum[2 * p : 2 * p + 1], prev[2 * p : 2 * p + 1], cum[2 * p + 1 : 2 * p + 2], prev[2 * p + 1 : 2 * p + 2]]
            + [jnp.zeros((4, length), F32)],
            axis=0,
        )
    head_of = lax.broadcasted_iota(jnp.int32, (heads, width), 1) >> log2(width // heads)
    mine = head_of == lax.broadcasted_iota(jnp.int32, (heads, width), 0)
    to_lanes = lambda col: jnp.sum(jnp.where(mine, col, 0.0), axis=0, keepdims=True)
    decay = to_lanes(jnp.exp(final))
    first_decay = to_lanes(jnp.exp(middle))
    second_decay = to_lanes(jnp.exp(final - middle))
    row8 = lax.broadcasted_iota(jnp.int32, (8, width), 0)
    coef_ref[...] = jnp.where(row8 == 0, first_decay, jnp.where(row8 == 1, second_decay, 0.0))
    copies[3].wait()
    copies[4].wait()
    for q in range(CHUNKS):
        at = slice(q * chunk, (q + 1) * chunk)
        spread_decs = decs[:, at].T.astype(BF16)
        for j, (ref, kind) in enumerate(((g_ref, 0), (g_ref, 1), (x_ref, 2), (x_ref, 3))):
            to = slice(j * width, (j + 1) * width)
            scaled_ref[at, to] = (ref[at].astype(F32) * mm(spread_decs, spread[:, to])).astype(BF16)
    copies[5].wait()
    onward, backward = [], []
    for q in range(CHUNKS):
        at = slice(q * chunk, (q + 1) * chunk)
        copies[6 + q].wait()
        projected = mm(tok_ref[at], w_ref[...])
        half = projected.shape[1] // 2
        bc_ref[at] = projected.astype(BF16)
        turned = pltpu.roll(projected, half, 1)
        cb_ref[at] = turned.astype(BF16)
        cb_t = turned.T.astype(BF16)
        parts = [scaled_ref[at, j * width : (j + 1) * width] for j in range(4)]
        onward.append(jnp.concatenate([mm(cb_t[:half], parts[1]), mm(cb_t[half:], parts[3])], axis=0))
        backward.append(jnp.concatenate([mm(cb_t[:half], parts[0]), mm(cb_t[half:], parts[2])], axis=0))

    near_ref[0] = onward[0]
    near_ref[1] = backward[1]
    next_total = onward[0] * second_decay + onward[1]
    prior_total = backward[0] + first_decay * backward[1]
    if n_seq == 4:
        here = lax.axis_index("seq")
        for k, ref in ((1, pay1_ref), (2, pay2_ref), (3, pay3_ref)):
            up = (here ^ k) > here

            @pl.when(up)
            def _():
                pack(ref, next_total, decay)

            @pl.when(jnp.logical_not(up))
            def _():
                pack(ref, prior_total, decay)
    else:
        pack(pay1_ref, next_total, decay)
        pack(pay2_ref, prior_total, decay)
        pack(pay3_ref, prior_total, decay)


def block_states(n_seq, tokens, x, g, dt, w, rate, bias):
    _, length, depth = tokens.shape
    width = x.shape[2]
    heads = dt.shape[1]
    two_n = w.shape[1]
    pay = jax.ShapeDtypeStruct((width // LANES * (two_n + 2), LANES), BF16)
    return pl.pallas_call(
        functools.partial(states_kernel, n_seq),
        name="block_states",
        in_specs=[HBM_SPEC] * 7,
        out_specs=[VMEM_SPEC] * 11,
        out_shape=[
            jax.ShapeDtypeStruct((length, two_n), BF16),
            jax.ShapeDtypeStruct((length, two_n), BF16),
            jax.ShapeDtypeStruct((heads // 2, 8, length), F32),
            jax.ShapeDtypeStruct((8 * heads, length), BF16),
            jax.ShapeDtypeStruct((8 * heads, 4 * width), BF16),
            jax.ShapeDtypeStruct((length, 4 * width), BF16),
            jax.ShapeDtypeStruct((2, two_n, width), F32),
            jax.ShapeDtypeStruct((8, width), F32),
            pay,
            pay,
            pay,
        ],
        scratch_shapes=[
            pltpu.VMEM((length, depth), BF16),
            pltpu.VMEM((length, width), BF16),
            pltpu.VMEM((length, width), BF16),
            pltpu.VMEM((heads, length), F32),
            pltpu.VMEM((depth, two_n), BF16),
            pltpu.SMEM((heads,), F32),
            pltpu.SMEM((heads,), F32),
            pltpu.SemaphoreType.DMA((8,)),
        ],
        compiler_params=LIMIT,
        cost_estimate=pl.CostEstimate(flops=2 * length * depth * two_n, bytes_accessed=5 << 20, transcendentals=0),
    )(*[pltpu.with_memory_space_constraint(a, pltpu.HBM) for a in (tokens, x, g, dt, w, rate, bias)])


def local_kernel(
    x_ref, g_ref, bc_ref, cb_ref, rows_ref, decs_ref, spread_ref, skip_ref,
    y_ref, gv_ref, gbc_ref, queries_ref, gvt_ref, gbt_ref, gc_ref,
):
    length, width = x_ref.shape[1:]
    lanes = 128
    n_pair = width // lanes
    chunk = length // CHUNKS
    tile = 128
    first_half = lax.broadcasted_iota(jnp.int32, (1, lanes), 1) < lanes // 2
    upper = lax.broadcasted_iota(jnp.int32, (lanes, 1), 0) < lanes // 2
    zero = jnp.zeros((), BF16)

    @pl.loop(0, CHUNKS)
    def _(q):
        s0 = pl.multiple_of(q * chunk, chunk)
        bc_s = bc_ref[pl.ds(s0, chunk), :]
        for tb in range(chunk // tile):
            t0 = pl.multiple_of(s0 + tb * tile, tile)
            cb_t = cb_ref[pl.ds(t0, tile), :]
            scores = mm_t(jnp.where(first_half, cb_t, zero), bc_s)
            row = tb * tile + lax.broadcasted_iota(jnp.int32, (tile, chunk), 0)
            col = lax.broadcasted_iota(jnp.int32, (tile, chunk), 1)
            below = col < row
            same = col == row
            total = None
            for p in range(n_pair):
                at = slice(p * lanes, (p + 1) * lanes)
                xp = x_ref[0, pl.ds(s0, chunk), at]
                x1, x2 = jnp.where(first_half, xp, zero), jnp.where(first_half, zero, xp)
                g_t = g_ref[0, pl.ds(t0, tile), at]
                gt = g_t.astype(F32).T.astype(BF16)
                cols = rows_ref[p, :, pl.ds(t0, tile)].T
                mains = []
                for k, xk in ((0, x1), (1, x2)):
                    gram = mm_t(g_t, xk)
                    cum_t, prev_t = cols[:, 2 * k : 2 * k + 1], cols[:, 2 * k + 1 : 2 * k + 2]
                    cum_s = rows_ref[p, 2 * k : 2 * k + 1, pl.ds(s0, chunk)]
                    prev_s = rows_ref[p, 2 * k + 1 : 2 * k + 2, pl.ds(s0, chunk)]
                    diff = jnp.minimum(jnp.where(below, cum_t - cum_s, prev_s - prev_t), 0.0)
                    kern = jnp.where(same, 0.0, jnp.exp(diff))
                    mains.append((scores * kern).astype(BF16))
                    term = gram * kern
                    total = term if total is None else total + term
                sk = jnp.where(first_half, skip_ref[2 * p], skip_ref[2 * p + 1])
                y = mm(mains[0], x1) + mm(mains[1], x2)
                y_ref[pl.ds(t0, tile), at] = y + sk * x_ref[0, pl.ds(t0, tile), at].astype(F32)
                gvt = mm(jnp.where(upper, gt, zero), mains[0]) + mm(jnp.where(upper, zero, gt), mains[1])
                if tb == 0:
                    gvt_ref[p] = gvt
                elif tb < chunk // tile - 1:
                    gvt_ref[p] += gvt
                else:
                    gs = g_ref[0, pl.ds(s0, chunk), at].astype(F32)
                    gv_ref[pl.ds(s0, chunk), at] = (gvt_ref[p] + gvt).T + sk * gs
            total = total.astype(BF16)
            gc_ref[tb * tile : (tb + 1) * tile] = mm(total, cb_ref[pl.ds(s0, chunk), :])
            gbt = mm(cb_t.astype(F32).T.astype(BF16), total)
            if tb == 0:
                gbt_ref[...] = gbt
            else:
                gbt_ref[...] += gbt
        gbc_ref[pl.ds(s0, chunk), :] = jnp.where(first_half, gbt_ref[...].T, gc_ref[...])

        e = mm(decs_ref[:, pl.ds(s0, chunk)].astype(F32).T.astype(BF16), spread_ref[...])
        bc = bc_s.astype(F32)
        cb = cb_ref[pl.ds(s0, chunk), :].astype(F32)
        cc, bb = jnp.where(first_half, cb, bc), jnp.where(first_half, bc, cb)
        for j, (query, kind) in enumerate(((cc, 0), (cc, 1), (bb, 2), (bb, 3))):
            for p in range(n_pair):
                value = query * e[:, kind * width + p * lanes : kind * width + (p + 1) * lanes]
                to = (j // 2) * 2 * width + p * 2 * lanes + (j % 2) * lanes
                queries_ref[pl.ds(s0, chunk), to : to + lanes] = value.astype(BF16)


def inside_chunks(x, g, bc, cb, rows, decs, spread, skip):
    _, length, width = x.shape
    n_pair = width // 128
    chunk = length // CHUNKS
    return pl.pallas_call(
        local_kernel,
        name="inside_chunks",
        in_specs=[VMEM_SPEC] * 7 + [SMEM_SPEC],
        out_specs=[VMEM_SPEC] * 4,
        out_shape=[
            jax.ShapeDtypeStruct((length, width), F32),
            jax.ShapeDtypeStruct((length, width), F32),
            jax.ShapeDtypeStruct((length, 128), F32),
            jax.ShapeDtypeStruct((length, 4 * width), BF16),
        ],
        scratch_shapes=[
            pltpu.VMEM((n_pair, 128, chunk), F32),
            pltpu.VMEM((128, chunk), F32),
            pltpu.VMEM((chunk, 128), F32),
        ],
        compiler_params=LIMIT,
        cost_estimate=pl.CostEstimate(
            flops=6 * length * length * width, bytes_accessed=4 << 20, transcendentals=2 * n_pair * length * length
        ),
    )(x, g, bc, cb, rows, decs, spread, skip)


def combine_received(direct, refs, two_n):
    if not direct:
        return refs[0][...], refs[1][...]
    here = lax.axis_index("seq")
    states, decays = zip(*[unpack(r[...], two_n) for r in refs])
    width = states[0].shape[1]
    before = jnp.zeros((two_n, width), F32)
    after = jnp.zeros((two_n, width), F32)
    for k in (1, 2, 3):
        there = here ^ k
        low, high = jnp.minimum(here, there), jnp.maximum(here, there)
        factor = jnp.ones((1, width), F32)
        for m in (1, 2, 3):
            if m != k:
                mid = here ^ m
                inside = jnp.logical_and(mid > low, mid < high)
                factor = factor * jnp.where(inside, decays[m - 1], 1.0)
        part = states[k - 1]
        earlier = there < here
        before = before + part * jnp.where(earlier, factor, 0.0)
        after = after + part * jnp.where(earlier, 0.0, factor)
    return before, after


def group_kernel(direct, count, *refs):
    received = refs[:count]
    near_ref, coef_ref, scaled_ref, gbc_ref, group_ref, before_ref, after_ref = refs[count:]
    if direct:
        received = [received[ORDER_A.index(k)] for k in (1, 2, 3)]
    length, two_n = group_ref.shape
    width = coef_ref.shape[1]
    chunk = length // CHUNKS
    before, after = combine_received(direct, received, two_n)
    befores = [before.astype(BF16), (near_ref[0] + coef_ref[0:1] * before).astype(BF16)]
    afters = [(near_ref[1] + coef_ref[1:2] * after).astype(BF16), after.astype(BF16)]
    left = lax.broadcasted_iota(jnp.int32, (1, two_n), 1) < two_n // 2
    for q in range(CHUNKS):
        at = slice(q * chunk, (q + 1) * chunk)
        before_ref[q] = befores[q]
        after_ref[q] = afters[q]
        both = jnp.concatenate([befores[q], afters[q]], axis=1)
        from_g = mm_t(scaled_ref[at, : 2 * width], both)
        from_x = mm_t(scaled_ref[at, 2 * width :], both)
        group_ref[at] = (gbc_ref[at] + jnp.where(left, from_x, from_g)).astype(BF16)


def group_sums(direct, received, near, coef, scaled, gbc):
    length, two_n = gbc.shape
    width = coef.shape[1]
    state = jax.ShapeDtypeStruct((CHUNKS, two_n, width), BF16)
    return pl.pallas_call(
        functools.partial(group_kernel, direct, len(received)),
        name="group_sums",
        in_specs=[VMEM_SPEC] * (4 + len(received)),
        out_specs=[VMEM_SPEC] * 3,
        out_shape=[jax.ShapeDtypeStruct((length, two_n), BF16), state, state],
        compiler_params=LIMIT,
        cost_estimate=pl.CostEstimate(flops=8 * length * two_n * width, bytes_accessed=3 << 20, transcendentals=0),
    )(*received, near, coef, scaled, gbc)


def carry_kernel(before_ref, after_ref, queries_ref, y_ref, gv_ref, yo_ref, gvo_ref):
    step = pl.program_id(0)
    _, two_n, width = before_ref.shape
    chunk = yo_ref.shape[0]
    lanes = 128
    half = two_n // 2
    before = before_ref[step]
    after = after_ref[step]
    first_half = lax.broadcasted_iota(jnp.int32, (1, lanes), 1) < lanes // 2
    zero = jnp.zeros((), BF16)
    s0 = pl.multiple_of(step * chunk, chunk)

    def apart(v):
        return [jnp.where(first_half, v, zero), jnp.where(first_half, zero, v)]

    for p in range(width // lanes):
        at = slice(p * lanes, (p + 1) * lanes)
        main = jnp.concatenate(apart(before[half:, at]) + apart(after[half:, at]), axis=0)
        back = jnp.concatenate(apart(before[:half, at]) + apart(after[:half, at]), axis=0)
        wide = slice(2 * p * lanes, 2 * (p + 1) * lanes)
        wide2 = slice(2 * width + 2 * p * lanes, 2 * width + 2 * (p + 1) * lanes)
        yo_ref[:, at] = (y_ref[pl.ds(s0, chunk), at] + mm(queries_ref[pl.ds(s0, chunk), wide], main)).astype(BF16)
        gvo_ref[:, at] = (gv_ref[pl.ds(s0, chunk), at] + mm(queries_ref[pl.ds(s0, chunk), wide2], back)).astype(BF16)


def add_carries(before, after, queries, y, gv):
    length, width = y.shape
    two_n = before.shape[1]
    chunk = length // CHUNKS
    part3 = pl.BlockSpec((None, chunk, width), lambda i: (0, i, 0))
    out = jax.ShapeDtypeStruct((1, length, width), BF16)
    return pl.pallas_call(
        carry_kernel,
        name="add_carries",
        grid=(CHUNKS,),
        in_specs=[VMEM_SPEC] * 5,
        out_specs=[part3, part3],
        out_shape=[out, out],
        compiler_params=LIMIT,
        cost_estimate=pl.CostEstimate(flops=8 * length * two_n * width, bytes_accessed=5 << 20, transcendentals=0),
    )(before, after, queries, y, gv)


def scanned_generic(onward, backward, two_n):
    size, here = lax.axis_size("seq"), lax.axis_index("seq")

    def total(payload, reverse):
        every = lax.all_gather(payload, "seq")

        def step(k, before):
            at = size - 1 - k if reverse else k
            state, decay = unpack(every[at], two_n)
            new = before * decay + state
            return jnp.where(at > here if reverse else at < here, new, before)

        return lax.fori_loop(0, size, step, jnp.zeros((two_n, LANES * (payload.shape[0] // (two_n + 2))), F32))

    return total(onward, False), total(backward, True)


def away_kernel(a0_ref, a1_ref, a2_ref, a3_ref, tokens_ref, grad_ref, grad_t_ref, send_ref):
    total = a0_ref[...].astype(F32) + a1_ref[...].astype(F32) + a2_ref[...].astype(F32) + a3_ref[...].astype(F32)
    grad = total.astype(BF16)
    grad_ref[...] = grad
    grad_t = grad.astype(F32).T.astype(BF16)
    grad_t_ref[...] = grad_t
    here = lax.axis_index("dp")
    n_seq, _, cols = send_ref.shape
    for s in range(n_seq):
        away = pl.multiple_of(((1 - here) * n_seq + s) * cols, cols)
        send_ref[s] = mm(grad_t, tokens_ref[0, :, pl.ds(away, cols)]).astype(BF16)


def home_kernel(grad_t_ref, tokens_ref, keep_ref):
    here = lax.axis_index("dp")
    n_seq, _, cols = keep_ref.shape
    for s in range(n_seq):
        home = pl.multiple_of((here * n_seq + s) * cols, cols)
        keep_ref[s] = mm(grad_t_ref[...], tokens_ref[0, :, pl.ds(home, cols)])


def weight_away(n_seq, groups, tokens):
    _, length, depth = tokens.shape
    two_n = groups[0].shape[1]
    cols = depth // (2 * n_seq)
    return pl.pallas_call(
        away_kernel,
        name="weight_away",
        in_specs=[VMEM_SPEC] * 5,
        out_specs=[VMEM_SPEC] * 3,
        out_shape=[
            jax.ShapeDtypeStruct((length, two_n), BF16),
            jax.ShapeDtypeStruct((two_n, length), BF16),
            jax.ShapeDtypeStruct((n_seq, two_n, cols), BF16),
        ],
        compiler_params=LIMIT,
        cost_estimate=pl.CostEstimate(flops=length * two_n * depth, bytes_accessed=2 << 20, transcendentals=0),
    )(*groups, tokens)


def weight_home(n_seq, grad_t, tokens):
    _, length, depth = tokens.shape
    two_n = grad_t.shape[0]
    cols = depth // (2 * n_seq)
    return pl.pallas_call(
        home_kernel,
        name="weight_home",
        in_specs=[VMEM_SPEC] * 2,
        out_specs=VMEM_SPEC,
        out_shape=jax.ShapeDtypeStruct((n_seq, two_n, cols), F32),
        compiler_params=LIMIT,
        cost_estimate=pl.CostEstimate(flops=length * two_n * depth, bytes_accessed=2 << 20, transcendentals=0),
    )(grad_t, tokens)


def pair_kernel(keep_ref, got_ref, own_ref, s1_ref, s2_ref, s3_ref):
    here = lax.axis_index("seq")
    own_ref[...] = keep_ref[here] + got_ref[here].astype(F32)
    for k, ref in ((1, s1_ref), (2, s2_ref), (3, s3_ref)):
        at = here ^ k
        ref[...] = (keep_ref[at] + got_ref[at].astype(F32)).astype(BF16)


def pair_sum(keep, got):
    _, two_n, cols = keep.shape
    small = jax.ShapeDtypeStruct((two_n, cols), BF16)
    return pl.pallas_call(
        pair_kernel,
        name="pair_sum",
        compiler_params=LIMIT,
        in_specs=[VMEM_SPEC, VMEM_SPEC],
        out_specs=[VMEM_SPEC] * 4,
        out_shape=[jax.ShapeDtypeStruct((two_n, cols), F32), small, small, small],
    )(keep, got)


def final_kernel(scale, own_ref, r3_ref, r2_ref, r1_ref, out_ref):
    total = own_ref[...] + r1_ref[...].astype(F32) + r2_ref[...].astype(F32) + r3_ref[...].astype(F32)
    out_ref[...] = total.T * scale


def final_sum(scale, own, r3, r2, r1):
    two_n, cols = own.shape
    return pl.pallas_call(
        functools.partial(final_kernel, scale),
        name="final_sum",
        compiler_params=LIMIT,
        in_specs=[VMEM_SPEC] * 4,
        out_specs=VMEM_SPEC,
        out_shape=jax.ShapeDtypeStruct((cols, two_n), F32),
    )(own, r3, r2, r1)


def input_kernel(grad_ref, w_ref, out_ref):
    out_ref[...] = mm_t(grad_ref[...], w_ref[...]).astype(BF16)


def input_grad(grad, w):
    length, two_n = grad.shape
    depth = w.shape[0]
    steps = 4
    chunk = length // steps
    return pl.pallas_call(
        input_kernel,
        name="input_grad",
        grid=(steps,),
        in_specs=[pl.BlockSpec((chunk, two_n), lambda i: (i, 0)), pl.BlockSpec((depth, two_n), lambda i: (0, 0))],
        out_specs=pl.BlockSpec((None, chunk, depth), lambda i: (0, i, 0)),
        out_shape=jax.ShapeDtypeStruct((1, length, depth), BF16),
        compiler_params=LIMIT,
        cost_estimate=pl.CostEstimate(flops=2 * length * two_n * depth, bytes_accessed=3 << 20, transcendentals=0),
    )(grad, w)


def swap(value, axis, k):
    return lax.ppermute(value, axis, [(i, i ^ k) for i in range(lax.axis_size(axis))])


def per_device(layer_input, head_values, dt_raw, w_bc, decay_rate, dt_bias, skip_gain, grad_y):
    n_seq, n_head, n_dp = lax.axis_size("seq"), lax.axis_size("head"), lax.axis_size("dp")
    length = layer_input.shape[1]
    two_n = w_bc.shape[1]
    bc, cb, rows, decs, spread, scaled, near, coef, pay1, pay2, pay3 = block_states(
        n_seq, layer_input, head_values, grad_y, dt_raw, w_bc, decay_rate, dt_bias
    )
    direct = n_seq == 4
    if direct:
        received = [swap((pay1, pay2, pay3)[k - 1], "seq", k) for k in ORDER_A]
    else:
        received = scanned_generic(pay1, pay2, two_n)
    y_local, gv_local, gbc_local, queries = inside_chunks(
        head_values, grad_y, bc, cb, rows, decs, spread, skip_gain
    )
    group, before, after = group_sums(direct, received, near, coef, scaled, gbc_local)
    total_tokens = n_dp * n_seq * length
    if direct and n_dp == 2 and n_head == 4:
        others = [swap(group, "head", k) for k in ORDER_B[::-1]]
        y_out, grad_values = add_carries(before, after, queries, y_local, gv_local)
        *others, y_out = lax.optimization_barrier((*others, y_out))
        groups = [group, *others]
        grad_bc, grad_t, send = weight_away(n_seq, groups, layer_input)
        got = swap(send, "dp", 1)
        keep = weight_home(n_seq, grad_t, layer_input)
        own, s1, s2, s3 = pair_sum(keep, got)
        sums = [swap((s1, s2, s3)[k - 1], "seq", k) for k in ORDER_C]
        grad_w_bc = final_sum(1.0 / total_tokens, own, *sums)
    else:
        y_out, grad_values = add_carries(before, after, queries, y_local, gv_local)
        grad_bc = lax.psum(group.astype(F32), "head").astype(BF16)
        part = jnp.einsum("td,tk->dk", layer_input[0], grad_bc, preferred_element_type=F32)
        grad_w_bc = lax.psum_scatter(part, ("dp", "seq"), scatter_dimension=0, tiled=True) / total_tokens
    grad_input = input_grad(grad_bc, w_bc)
    return y_out, grad_values, grad_input, grad_w_bc


def solution(mesh):
    in_specs = (
        P("dp", "seq", None),
        P("dp", "seq", "head"),
        P("dp", "head", "seq"),
        P(),
        P("head"),
        P("head"),
        P("head"),
        P("dp", "seq", "head"),
    )
    out_specs = (
        P("dp", "seq", "head"),
        P("dp", "seq", "head"),
        P("dp", "seq", None),
        P(("dp", "seq"), None),
    )
    return jax.shard_map(per_device, mesh=mesh, in_specs=in_specs, out_specs=out_specs, check_vma=False)
```

```python
import functools

import jax
import jax.numpy as jnp
from jax import lax
from jax.experimental import pallas as pl
from jax.experimental.pallas import tpu as pltpu
from jax.sharding import PartitionSpec as P

F32 = jnp.float32
BF16 = jnp.bfloat16
VMEM_SPEC = pl.BlockSpec(memory_space=pltpu.VMEM)
SMEM_SPEC = pl.BlockSpec(memory_space=pltpu.SMEM)
LANES = 128
ORDER_A = (2, 1, 3)
ORDER_B = (3, 2, 1)
ORDER_C = (3, 2, 1)


def mm(a, b):
    return jnp.dot(a, b, preferred_element_type=F32)


def mm_t(a, b):
    return lax.dot_general(a, b, (((1,), (1,)), ((), ())), preferred_element_type=F32)


LIMIT = pltpu.CompilerParams(vmem_limit_bytes=20 << 20)
HBM_SPEC = pl.BlockSpec(memory_space=pltpu.HBM)
CHUNKS = 2


def log2(n):
    return n.bit_length() - 1


def spread_matrix(heads, width):
    rows = 8 * heads
    row = lax.broadcasted_iota(jnp.int32, (rows, 4 * width), 0)
    col = lax.broadcasted_iota(jnp.int32, (rows, 4 * width), 1)
    kind_ok = (row >> log2(2 * heads)) == (col >> log2(width))
    head_ok = (row & (heads - 1)) == ((col & (width - 1)) >> log2(width // heads))
    return jnp.where(kind_ok & head_ok, 1.0, 0.0).astype(BF16)


def pack(ref, state, decay):
    rows, width = state.shape
    blocks = width // LANES
    high = decay.astype(BF16).astype(F32)
    for p in range(blocks):
        ref[p * rows : (p + 1) * rows] = state[:, p * LANES : (p + 1) * LANES].astype(BF16)
    parts = [v[:, p * LANES : (p + 1) * LANES] for v in (high, decay - high) for p in range(blocks)]
    ref[blocks * rows :] = jnp.concatenate(parts, axis=0).astype(BF16)


def unpack(payload, rows):
    blocks = payload.shape[0] // (rows + 2)
    state = jnp.concatenate([payload[p * rows : (p + 1) * rows] for p in range(blocks)], axis=1).astype(F32)
    tail = payload[blocks * rows :].astype(F32)
    decay = jnp.concatenate([tail[p : p + 1] + tail[blocks + p : blocks + p + 1] for p in range(blocks)], axis=1)
    return state, decay


def states_kernel(
    n_seq, tokens_hbm, x_hbm, g_hbm, dt_hbm, w_hbm, rate_hbm, bias_hbm,
    bc_ref, cb_ref, rows_ref, decs_ref, spread_ref, scaled_ref, near_ref, coef_ref, pay1_ref, pay2_ref, pay3_ref,
    tok_ref, x_ref, g_ref, dt_ref, w_ref, rate_ref, bias_ref, sems,
):
    heads, length = dt_ref.shape
    chunk = length // CHUNKS
    width = x_ref.shape[1]
    copies = [
        pltpu.make_async_copy(dt_hbm.at[0], dt_ref, sems.at[0]),
        pltpu.make_async_copy(rate_hbm, rate_ref, sems.at[1]),
        pltpu.make_async_copy(bias_hbm, bias_ref, sems.at[2]),
        pltpu.make_async_copy(g_hbm.at[0], g_ref, sems.at[3]),
        pltpu.make_async_copy(x_hbm.at[0], x_ref, sems.at[4]),
        pltpu.make_async_copy(w_hbm, w_ref, sems.at[5]),
        pltpu.make_async_copy(tokens_hbm.at[0, :chunk], tok_ref.at[:chunk], sems.at[6]),
        pltpu.make_async_copy(tokens_hbm.at[0, chunk:], tok_ref.at[chunk:], sems.at[7]),
    ]
    for c in copies:
        c.start()
    spread = spread_matrix(heads, width)
    spread_ref[...] = spread
    for c in copies[:3]:
        c.wait()
    sub = lax.broadcasted_iota(jnp.int32, (heads, 1), 0)
    rate = jnp.zeros((heads, 1), F32)
    bias = jnp.zeros((heads, 1), F32)
    for h in range(heads):
        rate = jnp.where(sub == h, rate_ref[h], rate)
        bias = jnp.where(sub == h, bias_ref[h], bias)
    v = dt_ref[...] + bias
    log_step = -rate * (jnp.maximum(v, 0.0) + jnp.log1p(jnp.exp(-jnp.abs(v))))
    lane = lax.broadcasted_iota(jnp.int32, (heads, length), 1)
    cum = log_step
    shift = 1
    while shift < length:
        cum = cum + jnp.where(lane >= shift, pltpu.roll(cum, shift, 1), 0.0)
        shift *= 2
    prev = cum - log_step
    middle = cum[:, chunk - 1 : chunk]
    final = cum[:, length - 1 : length]
    second = lane >= chunk
    begin = jnp.where(second, middle, 0.0)
    end = jnp.where(second, final, middle)
    kinds = (jnp.exp(cum - begin), jnp.exp(end - prev), jnp.exp(jnp.minimum(prev - begin, 0.0)), jnp.exp(end - cum))
    parts = []
    for k in kinds:
        high = k.astype(BF16).astype(F32)
        parts += [high, k - high]
    decs = jnp.concatenate(parts, axis=0)
    decs_ref[...] = decs.astype(BF16)
    for p in range(heads // 2):
        rows_ref[p] = jnp.concatenate(
            [cum[2 * p : 2 * p + 1], prev[2 * p : 2 * p + 1], cum[2 * p + 1 : 2 * p + 2], prev[2 * p + 1 : 2 * p + 2]]
            + [jnp.zeros((4, length), F32)],
            axis=0,
        )
    head_of = lax.broadcasted_iota(jnp.int32, (heads, width), 1) >> log2(width // heads)
    mine = head_of == lax.broadcasted_iota(jnp.int32, (heads, width), 0)
    to_lanes = lambda col: jnp.sum(jnp.where(mine, col, 0.0), axis=0, keepdims=True)
    decay = to_lanes(jnp.exp(final))
    first_decay = to_lanes(jnp.exp(middle))
    second_decay = to_lanes(jnp.exp(final - middle))
    row8 = lax.broadcasted_iota(jnp.int32, (8, width), 0)
    coef_ref[...] = jnp.where(row8 == 0, first_decay, jnp.where(row8 == 1, second_decay, 0.0))
    copies[3].wait()
    copies[4].wait()
    for q in range(CHUNKS):
        at = slice(q * chunk, (q + 1) * chunk)
        spread_decs = decs[:, at].T.astype(BF16)
        for j, (ref, kind) in enumerate(((g_ref, 0), (g_ref, 1), (x_ref, 2), (x_ref, 3))):
            to = slice(j * width, (j + 1) * width)
            scaled_ref[at, to] = (ref[at].astype(F32) * mm(spread_decs, spread[:, to])).astype(BF16)
    copies[5].wait()
    onward, backward = [], []
    for q in range(CHUNKS):
        at = slice(q * chunk, (q + 1) * chunk)
        copies[6 + q].wait()
        projected = mm(tok_ref[at], w_ref[...])
        half = projected.shape[1] // 2
        bc_ref[at] = projected.astype(BF16)
        turned = pltpu.roll(projected, half, 1)
        cb_ref[at] = turned.astype(BF16)
        cb_t = turned.T.astype(BF16)
        parts = [scaled_ref[at, j * width : (j + 1) * width] for j in range(4)]
        onward.append(jnp.concatenate([mm(cb_t[:half], parts[1]), mm(cb_t[half:], parts[3])], axis=0))
        backward.append(jnp.concatenate([mm(cb_t[:half], parts[0]), mm(cb_t[half:], parts[2])], axis=0))

    near_ref[0] = onward[0]
    near_ref[1] = backward[1]
    next_total = onward[0] * second_decay + onward[1]
    prior_total = backward[0] + first_decay * backward[1]
    if n_seq == 4:
        here = lax.axis_index("seq")
        for k, ref in ((1, pay1_ref), (2, pay2_ref), (3, pay3_ref)):
            up = (here ^ k) > here

            @pl.when(up)
            def _():
                pack(ref, next_total, decay)

            @pl.when(jnp.logical_not(up))
            def _():
                pack(ref, prior_total, decay)
    else:
        pack(pay1_ref, next_total, decay)
        pack(pay2_ref, prior_total, decay)
        pack(pay3_ref, prior_total, decay)


def block_states(n_seq, tokens, x, g, dt, w, rate, bias):
    _, length, depth = tokens.shape
    width = x.shape[2]
    heads = dt.shape[1]
    two_n = w.shape[1]
    pay = jax.ShapeDtypeStruct((width // LANES * (two_n + 2), LANES), BF16)
    return pl.pallas_call(
        functools.partial(states_kernel, n_seq),
        name="block_states",
        in_specs=[HBM_SPEC] * 7,
        out_specs=[VMEM_SPEC] * 11,
        out_shape=[
            jax.ShapeDtypeStruct((length, two_n), BF16),
            jax.ShapeDtypeStruct((length, two_n), BF16),
            jax.ShapeDtypeStruct((heads // 2, 8, length), F32),
            jax.ShapeDtypeStruct((8 * heads, length), BF16),
            jax.ShapeDtypeStruct((8 * heads, 4 * width), BF16),
            jax.ShapeDtypeStruct((length, 4 * width), BF16),
            jax.ShapeDtypeStruct((2, two_n, width), F32),
            jax.ShapeDtypeStruct((8, width), F32),
            pay,
            pay,
            pay,
        ],
        scratch_shapes=[
            pltpu.VMEM((length, depth), BF16),
            pltpu.VMEM((length, width), BF16),
            pltpu.VMEM((length, width), BF16),
            pltpu.VMEM((heads, length), F32),
            pltpu.VMEM((depth, two_n), BF16),
            pltpu.SMEM((heads,), F32),
            pltpu.SMEM((heads,), F32),
            pltpu.SemaphoreType.DMA((8,)),
        ],
        compiler_params=LIMIT,
        cost_estimate=pl.CostEstimate(flops=2 * length * depth * two_n, bytes_accessed=5 << 20, transcendentals=0),
    )(*[pltpu.with_memory_space_constraint(a, pltpu.HBM) for a in (tokens, x, g, dt, w, rate, bias)])


def local_kernel(
    x_ref, g_ref, bc_ref, cb_ref, rows_ref, decs_ref, spread_ref, skip_ref,
    y_ref, gv_ref, gbc_ref, queries_ref, gvt_ref, gbt_ref, gc_ref,
):
    length, width = x_ref.shape[1:]
    lanes = 128
    n_pair = width // lanes
    chunk = length // CHUNKS
    tile = 128
    first_half = lax.broadcasted_iota(jnp.int32, (1, lanes), 1) < lanes // 2
    upper = lax.broadcasted_iota(jnp.int32, (lanes, 1), 0) < lanes // 2
    zero = jnp.zeros((), BF16)

    @pl.loop(0, CHUNKS)
    def _(q):
        s0 = pl.multiple_of(q * chunk, chunk)
        bc_s = bc_ref[pl.ds(s0, chunk), :]
        for tb in range(chunk // tile):
            t0 = pl.multiple_of(s0 + tb * tile, tile)
            cb_t = cb_ref[pl.ds(t0, tile), :]
            scores = mm_t(jnp.where(first_half, cb_t, zero), bc_s)
            row = tb * tile + lax.broadcasted_iota(jnp.int32, (tile, chunk), 0)
            col = lax.broadcasted_iota(jnp.int32, (tile, chunk), 1)
            below = col < row
            same = col == row
            total = None
            for p in range(n_pair):
                at = slice(p * lanes, (p + 1) * lanes)
                xp = x_ref[0, pl.ds(s0, chunk), at]
                x1, x2 = jnp.where(first_half, xp, zero), jnp.where(first_half, zero, xp)
                g_t = g_ref[0, pl.ds(t0, tile), at]
                gt = g_t.astype(F32).T.astype(BF16)
                cols = rows_ref[p, :, pl.ds(t0, tile)].T
                mains = []
                for k, xk in ((0, x1), (1, x2)):
                    gram = mm_t(g_t, xk)
                    cum_t, prev_t = cols[:, 2 * k : 2 * k + 1], cols[:, 2 * k + 1 : 2 * k + 2]
                    cum_s = rows_ref[p, 2 * k : 2 * k + 1, pl.ds(s0, chunk)]
                    prev_s = rows_ref[p, 2 * k + 1 : 2 * k + 2, pl.ds(s0, chunk)]
                    diff = jnp.minimum(jnp.where(below, cum_t - cum_s, prev_s - prev_t), 0.0)
                    kern = jnp.where(same, 0.0, jnp.exp(diff))
                    mains.append((scores * kern).astype(BF16))
                    term = gram * kern
                    total = term if total is None else total + term
                sk = jnp.where(first_half, skip_ref[2 * p], skip_ref[2 * p + 1])
                y = mm(mains[0], x1) + mm(mains[1], x2)
                y_ref[pl.ds(t0, tile), at] = y + sk * x_ref[0, pl.ds(t0, tile), at].astype(F32)
                gvt = mm(jnp.where(upper, gt, zero), mains[0]) + mm(jnp.where(upper, zero, gt), mains[1])
                if tb == 0:
                    gvt_ref[p] = gvt
                elif tb < chunk // tile - 1:
                    gvt_ref[p] += gvt
                else:
                    gs = g_ref[0, pl.ds(s0, chunk), at].astype(F32)
                    gv_ref[pl.ds(s0, chunk), at] = (gvt_ref[p] + gvt).T + sk * gs
            total = total.astype(BF16)
            gc_ref[tb * tile : (tb + 1) * tile] = mm(total, cb_ref[pl.ds(s0, chunk), :])
            gbt = mm(cb_t.astype(F32).T.astype(BF16), total)
            if tb == 0:
                gbt_ref[...] = gbt
            else:
                gbt_ref[...] += gbt
        gbc_ref[pl.ds(s0, chunk), :] = jnp.where(first_half, gbt_ref[...].T, gc_ref[...])

        e = mm(decs_ref[:, pl.ds(s0, chunk)].astype(F32).T.astype(BF16), spread_ref[...])
        bc = bc_s.astype(F32)
        cb = cb_ref[pl.ds(s0, chunk), :].astype(F32)
        cc, bb = jnp.where(first_half, cb, bc), jnp.where(first_half, bc, cb)
        for j, (query, kind) in enumerate(((cc, 0), (cc, 1), (bb, 2), (bb, 3))):
            for p in range(n_pair):
                value = query * e[:, kind * width + p * lanes : kind * width + (p + 1) * lanes]
                to = (j // 2) * 2 * width + p * 2 * lanes + (j % 2) * lanes
                queries_ref[pl.ds(s0, chunk), to : to + lanes] = value.astype(BF16)


def inside_chunks(x, g, bc, cb, rows, decs, spread, skip):
    _, length, width = x.shape
    n_pair = width // 128
    chunk = length // CHUNKS
    return pl.pallas_call(
        local_kernel,
        name="inside_chunks",
        in_specs=[VMEM_SPEC] * 7 + [SMEM_SPEC],
        out_specs=[VMEM_SPEC] * 4,
        out_shape=[
            jax.ShapeDtypeStruct((length, width), F32),
            jax.ShapeDtypeStruct((length, width), F32),
            jax.ShapeDtypeStruct((length, 128), F32),
            jax.ShapeDtypeStruct((length, 4 * width), BF16),
        ],
        scratch_shapes=[
            pltpu.VMEM((n_pair, 128, chunk), F32),
            pltpu.VMEM((128, chunk), F32),
            pltpu.VMEM((chunk, 128), F32),
        ],
        compiler_params=LIMIT,
        cost_estimate=pl.CostEstimate(
            flops=6 * length * length * width, bytes_accessed=4 << 20, transcendentals=2 * n_pair * length * length
        ),
    )(x, g, bc, cb, rows, decs, spread, skip)


def combine_received(direct, refs, two_n):
    if not direct:
        return refs[0][...], refs[1][...]
    here = lax.axis_index("seq")
    states, decays = zip(*[unpack(r[...], two_n) for r in refs])
    width = states[0].shape[1]
    before = jnp.zeros((two_n, width), F32)
    after = jnp.zeros((two_n, width), F32)
    for k in (1, 2, 3):
        there = here ^ k
        low, high = jnp.minimum(here, there), jnp.maximum(here, there)
        factor = jnp.ones((1, width), F32)
        for m in (1, 2, 3):
            if m != k:
                mid = here ^ m
                inside = jnp.logical_and(mid > low, mid < high)
                factor = factor * jnp.where(inside, decays[m - 1], 1.0)
        part = states[k - 1]
        earlier = there < here
        before = before + part * jnp.where(earlier, factor, 0.0)
        after = after + part * jnp.where(earlier, 0.0, factor)
    return before, after


def group_kernel(direct, count, *refs):
    received = refs[:count]
    near_ref, coef_ref, scaled_ref, gbc_ref, group_ref, before_ref, after_ref = refs[count:]
    if direct:
        received = [received[ORDER_A.index(k)] for k in (1, 2, 3)]
    length, two_n = group_ref.shape
    width = coef_ref.shape[1]
    chunk = length // CHUNKS
    before, after = combine_received(direct, received, two_n)
    befores = [before.astype(BF16), (near_ref[0] + coef_ref[0:1] * before).astype(BF16)]
    afters = [(near_ref[1] + coef_ref[1:2] * after).astype(BF16), after.astype(BF16)]
    left = lax.broadcasted_iota(jnp.int32, (1, two_n), 1) < two_n // 2
    for q in range(CHUNKS):
        at = slice(q * chunk, (q + 1) * chunk)
        before_ref[q] = befores[q]
        after_ref[q] = afters[q]
        both = jnp.concatenate([befores[q], afters[q]], axis=1)
        from_g = mm_t(scaled_ref[at, : 2 * width], both)
        from_x = mm_t(scaled_ref[at, 2 * width :], both)
        group_ref[at] = (gbc_ref[at] + jnp.where(left, from_x, from_g)).astype(BF16)


def group_sums(direct, received, near, coef, scaled, gbc):
    length, two_n = gbc.shape
    width = coef.shape[1]
    state = jax.ShapeDtypeStruct((CHUNKS, two_n, width), BF16)
    return pl.pallas_call(
        functools.partial(group_kernel, direct, len(received)),
        name="group_sums",
        in_specs=[VMEM_SPEC] * (4 + len(received)),
        out_specs=[VMEM_SPEC] * 3,
        out_shape=[jax.ShapeDtypeStruct((length, two_n), BF16), state, state],
        compiler_params=LIMIT,
        cost_estimate=pl.CostEstimate(flops=8 * length * two_n * width, bytes_accessed=3 << 20, transcendentals=0),
    )(*received, near, coef, scaled, gbc)


def carry_kernel(before_ref, after_ref, queries_ref, y_ref, gv_ref, yo_ref, gvo_ref):
    step = pl.program_id(0)
    _, two_n, width = before_ref.shape
    chunk = yo_ref.shape[0]
    lanes = 128
    half = two_n // 2
    before = before_ref[step]
    after = after_ref[step]
    first_half = lax.broadcasted_iota(jnp.int32, (1, lanes), 1) < lanes // 2
    zero = jnp.zeros((), BF16)
    s0 = pl.multiple_of(step * chunk, chunk)

    def apart(v):
        return [jnp.where(first_half, v, zero), jnp.where(first_half, zero, v)]

    for p in range(width // lanes):
        at = slice(p * lanes, (p + 1) * lanes)
        main = jnp.concatenate(apart(before[half:, at]) + apart(after[half:, at]), axis=0)
        back = jnp.concatenate(apart(before[:half, at]) + apart(after[:half, at]), axis=0)
        wide = slice(2 * p * lanes, 2 * (p + 1) * lanes)
        wide2 = slice(2 * width + 2 * p * lanes, 2 * width + 2 * (p + 1) * lanes)
        yo_ref[:, at] = (y_ref[pl.ds(s0, chunk), at] + mm(queries_ref[pl.ds(s0, chunk), wide], main)).astype(BF16)
        gvo_ref[:, at] = (gv_ref[pl.ds(s0, chunk), at] + mm(queries_ref[pl.ds(s0, chunk), wide2], back)).astype(BF16)


def add_carries(before, after, queries, y, gv):
    length, width = y.shape
    two_n = before.shape[1]
    chunk = length // CHUNKS
    part3 = pl.BlockSpec((None, chunk, width), lambda i: (0, i, 0))
    out = jax.ShapeDtypeStruct((1, length, width), BF16)
    return pl.pallas_call(
        carry_kernel,
        name="add_carries",
        grid=(CHUNKS,),
        in_specs=[VMEM_SPEC] * 5,
        out_specs=[part3, part3],
        out_shape=[out, out],
        compiler_params=LIMIT,
        cost_estimate=pl.CostEstimate(flops=8 * length * two_n * width, bytes_accessed=5 << 20, transcendentals=0),
    )(before, after, queries, y, gv)


def scanned_generic(onward, backward, two_n):
    size, here = lax.axis_size("seq"), lax.axis_index("seq")

    def total(payload, reverse):
        every = lax.all_gather(payload, "seq")

        def step(k, before):
            at = size - 1 - k if reverse else k
            state, decay = unpack(every[at], two_n)
            new = before * decay + state
            return jnp.where(at > here if reverse else at < here, new, before)

        return lax.fori_loop(0, size, step, jnp.zeros((two_n, LANES * (payload.shape[0] // (two_n + 2))), F32))

    return total(onward, False), total(backward, True)


def away_kernel(a0_ref, a1_ref, a2_ref, a3_ref, tokens_ref, grad_ref, grad_t_ref, send_ref):
    total = a0_ref[...].astype(F32) + a1_ref[...].astype(F32) + a2_ref[...].astype(F32) + a3_ref[...].astype(F32)
    grad = total.astype(BF16)
    grad_ref[...] = grad
    grad_t = grad.astype(F32).T.astype(BF16)
    grad_t_ref[...] = grad_t
    here = lax.axis_index("dp")
    n_seq, _, cols = send_ref.shape
    for s in range(n_seq):
        away = pl.multiple_of(((1 - here) * n_seq + s) * cols, cols)
        send_ref[s] = mm(grad_t, tokens_ref[0, :, pl.ds(away, cols)]).astype(BF16)


def home_kernel(grad_t_ref, tokens_ref, keep_ref):
    here = lax.axis_index("dp")
    n_seq, _, cols = keep_ref.shape
    for s in range(n_seq):
        home = pl.multiple_of((here * n_seq + s) * cols, cols)
        keep_ref[s] = mm(grad_t_ref[...], tokens_ref[0, :, pl.ds(home, cols)])


def weight_away(n_seq, groups, tokens):
    _, length, depth = tokens.shape
    two_n = groups[0].shape[1]
    cols = depth // (2 * n_seq)
    return pl.pallas_call(
        away_kernel,
        name="weight_away",
        in_specs=[VMEM_SPEC] * 5,
        out_specs=[VMEM_SPEC] * 3,
        out_shape=[
            jax.ShapeDtypeStruct((length, two_n), BF16),
            jax.ShapeDtypeStruct((two_n, length), BF16),
            jax.ShapeDtypeStruct((n_seq, two_n, cols), BF16),
        ],
        compiler_params=LIMIT,
        cost_estimate=pl.CostEstimate(flops=length * two_n * depth, bytes_accessed=2 << 20, transcendentals=0),
    )(*groups, tokens)


def weight_home(n_seq, grad_t, tokens):
    _, length, depth = tokens.shape
    two_n = grad_t.shape[0]
    cols = depth // (2 * n_seq)
    return pl.pallas_call(
        home_kernel,
        name="weight_home",
        in_specs=[VMEM_SPEC] * 2,
        out_specs=VMEM_SPEC,
        out_shape=jax.ShapeDtypeStruct((n_seq, two_n, cols), F32),
        compiler_params=LIMIT,
        cost_estimate=pl.CostEstimate(flops=length * two_n * depth, bytes_accessed=2 << 20, transcendentals=0),
    )(grad_t, tokens)


def pair_kernel(keep_ref, got_ref, own_ref, s1_ref, s2_ref, s3_ref):
    here = lax.axis_index("seq")
    own_ref[...] = keep_ref[here] + got_ref[here].astype(F32)
    for k, ref in ((1, s1_ref), (2, s2_ref), (3, s3_ref)):
        at = here ^ k
        ref[...] = (keep_ref[at] + got_ref[at].astype(F32)).astype(BF16)


def pair_sum(keep, got):
    _, two_n, cols = keep.shape
    small = jax.ShapeDtypeStruct((two_n, cols), BF16)
    return pl.pallas_call(
        pair_kernel,
        name="pair_sum",
        compiler_params=LIMIT,
        in_specs=[VMEM_SPEC, VMEM_SPEC],
        out_specs=[VMEM_SPEC] * 4,
        out_shape=[jax.ShapeDtypeStruct((two_n, cols), F32), small, small, small],
    )(keep, got)


def final_kernel(scale, own_ref, r3_ref, r2_ref, r1_ref, out_ref):
    total = own_ref[...] + r1_ref[...].astype(F32) + r2_ref[...].astype(F32) + r3_ref[...].astype(F32)
    out_ref[...] = total.T * scale


def final_sum(scale, own, r3, r2, r1):
    two_n, cols = own.shape
    return pl.pallas_call(
        functools.partial(final_kernel, scale),
        name="final_sum",
        compiler_params=LIMIT,
        in_specs=[VMEM_SPEC] * 4,
        out_specs=VMEM_SPEC,
        out_shape=jax.ShapeDtypeStruct((cols, two_n), F32),
    )(own, r3, r2, r1)


def input_kernel(grad_ref, w_ref, out_ref):
    out_ref[...] = mm_t(grad_ref[...], w_ref[...]).astype(BF16)


def input_grad(grad, w):
    length, two_n = grad.shape
    depth = w.shape[0]
    steps = 4
    chunk = length // steps
    return pl.pallas_call(
        input_kernel,
        name="input_grad",
        grid=(steps,),
        in_specs=[pl.BlockSpec((chunk, two_n), lambda i: (i, 0)), pl.BlockSpec((depth, two_n), lambda i: (0, 0))],
        out_specs=pl.BlockSpec((None, chunk, depth), lambda i: (0, i, 0)),
        out_shape=jax.ShapeDtypeStruct((1, length, depth), BF16),
        compiler_params=LIMIT,
        cost_estimate=pl.CostEstimate(flops=2 * length * two_n * depth, bytes_accessed=3 << 20, transcendentals=0),
    )(grad, w)


def swap(value, axis, k):
    return lax.ppermute(value, axis, [(i, i ^ k) for i in range(lax.axis_size(axis))])


def per_device(layer_input, head_values, dt_raw, w_bc, decay_rate, dt_bias, skip_gain, grad_y):
    n_seq, n_head, n_dp = lax.axis_size("seq"), lax.axis_size("head"), lax.axis_size("dp")
    length = layer_input.shape[1]
    two_n = w_bc.shape[1]
    bc, cb, rows, decs, spread, scaled, near, coef, pay1, pay2, pay3 = block_states(
        n_seq, layer_input, head_values, grad_y, dt_raw, w_bc, decay_rate, dt_bias
    )
    direct = n_seq == 4
    if direct:
        received = [swap((pay1, pay2, pay3)[k - 1], "seq", k) for k in ORDER_A]
    else:
        received = scanned_generic(pay1, pay2, two_n)
    y_local, gv_local, gbc_local, queries = inside_chunks(
        head_values, grad_y, bc, cb, rows, decs, spread, skip_gain
    )
    group, before, after = group_sums(direct, received, near, coef, scaled, gbc_local)
    total_tokens = n_dp * n_seq * length
    if direct and n_dp == 2 and n_head == 4:
        others = [swap(group, "head", k) for k in ORDER_B[::-1]]
        y_out, grad_values = add_carries(before, after, queries, y_local, gv_local)
        *others, y_out = lax.optimization_barrier((*others, y_out))
        groups = [group, *others]
        grad_bc, grad_t, send = weight_away(n_seq, groups, layer_input)
        got = swap(send, "dp", 1)
        keep = weight_home(n_seq, grad_t, layer_input)
        own, s1, s2, s3 = pair_sum(keep, got)
        sums = [swap((s1, s2, s3)[k - 1], "seq", k) for k in ORDER_C]
        grad_w_bc = final_sum(1.0 / total_tokens, own, *sums)
    else:
        y_out, grad_values = add_carries(before, after, queries, y_local, gv_local)
        grad_bc = lax.psum(group.astype(F32), "head").astype(BF16)
        part = jnp.einsum("td,tk->dk", layer_input[0], grad_bc, preferred_element_type=F32)
        grad_w_bc = lax.psum_scatter(part, ("dp", "seq"), scatter_dimension=0, tiled=True) / total_tokens
    grad_input = input_grad(grad_bc, w_bc)
    return y_out, grad_values, grad_input, grad_w_bc


def solution(mesh):
    in_specs = (
        P("dp", "seq", None),
        P("dp", "seq", "head"),
        P("dp", "head", "seq"),
        P(),
        P("head"),
        P("head"),
        P("head"),
        P("dp", "seq", "head"),
    )
    out_specs = (
        P("dp", "seq", "head"),
        P("dp", "seq", "head"),
        P("dp", "seq", None),
        P(("dp", "seq"), None),
    )
    return jax.shard_map(per_device, mesh=mesh, in_specs=in_specs, out_specs=out_specs, check_vma=False)
```

```python
import functools

import jax
import jax.numpy as jnp
from jax import lax
from jax.experimental import pallas as pl
from jax.experimental.pallas import tpu as pltpu
from jax.sharding import PartitionSpec as P

F32 = jnp.float32
BF16 = jnp.bfloat16
VMEM_SPEC = pl.BlockSpec(memory_space=pltpu.VMEM)
SMEM_SPEC = pl.BlockSpec(memory_space=pltpu.SMEM)
LANES = 128
ORDER_A = (2, 1, 3)
ORDER_B = (3, 2, 1)
ORDER_C = (3, 2, 1)


def mm(a, b):
    return jnp.dot(a, b, preferred_element_type=F32)


def mm_t(a, b):
    return lax.dot_general(a, b, (((1,), (1,)), ((), ())), preferred_element_type=F32)


LIMIT = pltpu.CompilerParams(vmem_limit_bytes=20 << 20)
HBM_SPEC = pl.BlockSpec(memory_space=pltpu.HBM)
CHUNKS = 2


def log2(n):
    return n.bit_length() - 1


def spread_matrix(heads, width):
    rows = 8 * heads
    row = lax.broadcasted_iota(jnp.int32, (rows, 4 * width), 0)
    col = lax.broadcasted_iota(jnp.int32, (rows, 4 * width), 1)
    kind_ok = (row >> log2(2 * heads)) == (col >> log2(width))
    head_ok = (row & (heads - 1)) == ((col & (width - 1)) >> log2(width // heads))
    return jnp.where(kind_ok & head_ok, 1.0, 0.0).astype(BF16)


def pack(ref, state, decay):
    rows, width = state.shape
    blocks = width // LANES
    high = decay.astype(BF16).astype(F32)
    for p in range(blocks):
        ref[p * rows : (p + 1) * rows] = state[:, p * LANES : (p + 1) * LANES].astype(BF16)
    parts = [v[:, p * LANES : (p + 1) * LANES] for v in (high, decay - high) for p in range(blocks)]
    ref[blocks * rows :] = jnp.concatenate(parts, axis=0).astype(BF16)


def unpack(payload, rows):
    blocks = payload.shape[0] // (rows + 2)
    state = jnp.concatenate([payload[p * rows : (p + 1) * rows] for p in range(blocks)], axis=1).astype(F32)
    tail = payload[blocks * rows :].astype(F32)
    decay = jnp.concatenate([tail[p : p + 1] + tail[blocks + p : blocks + p + 1] for p in range(blocks)], axis=1)
    return state, decay


def states_kernel(
    n_seq, tokens_hbm, x_hbm, g_hbm, dt_hbm, w_hbm, rate_hbm, bias_hbm,
    bc_ref, cb_ref, rows_ref, decs_ref, spread_ref, scaled_ref, near_ref, coef_ref, pay1_ref, pay2_ref, pay3_ref,
    x_ref, g_ref, tok_ref, w_ref, dt_ref, rate_ref, bias_ref, sems,
):
    heads, length = dt_ref.shape
    chunk = length // CHUNKS
    width = x_ref.shape[1]
    copies = [
        pltpu.make_async_copy(dt_hbm.at[0], dt_ref, sems.at[0]),
        pltpu.make_async_copy(rate_hbm, rate_ref, sems.at[1]),
        pltpu.make_async_copy(bias_hbm, bias_ref, sems.at[2]),
        pltpu.make_async_copy(g_hbm.at[0], g_ref, sems.at[3]),
        pltpu.make_async_copy(x_hbm.at[0], x_ref, sems.at[4]),
        pltpu.make_async_copy(w_hbm, w_ref, sems.at[5]),
        pltpu.make_async_copy(tokens_hbm.at[0, :chunk], tok_ref.at[:chunk], sems.at[6]),
        pltpu.make_async_copy(tokens_hbm.at[0, chunk:], tok_ref.at[chunk:], sems.at[7]),
    ]
    for c in copies:
        c.start()
    spread = spread_matrix(heads, width)
    spread_ref[...] = spread
    for c in copies[:3]:
        c.wait()
    sub = lax.broadcasted_iota(jnp.int32, (heads, 1), 0)
    rate = jnp.zeros((heads, 1), F32)
    bias = jnp.zeros((heads, 1), F32)
    for h in range(heads):
        rate = jnp.where(sub == h, rate_ref[h], rate)
        bias = jnp.where(sub == h, bias_ref[h], bias)
    v = dt_ref[...] + bias
    log_step = -rate * (jnp.maximum(v, 0.0) + jnp.log1p(jnp.exp(-jnp.abs(v))))
    lane = lax.broadcasted_iota(jnp.int32, (heads, length), 1)
    cum = log_step
    shift = 1
    while shift < length:
        cum = cum + jnp.where(lane >= shift, pltpu.roll(cum, shift, 1), 0.0)
        shift *= 2
    prev = cum - log_step
    middle = cum[:, chunk - 1 : chunk]
    final = cum[:, length - 1 : length]
    second = lane >= chunk
    begin = jnp.where(second, middle, 0.0)
    end = jnp.where(second, final, middle)
    kinds = (jnp.exp(cum - begin), jnp.exp(end - prev), jnp.exp(jnp.minimum(prev - begin, 0.0)), jnp.exp(end - cum))
    parts = []
    for k in kinds:
        high = k.astype(BF16).astype(F32)
        parts += [high, k - high]
    decs = jnp.concatenate(parts, axis=0)
    decs_ref[...] = decs.astype(BF16)
    for p in range(heads // 2):
        rows_ref[p] = jnp.concatenate(
            [cum[2 * p : 2 * p + 1], prev[2 * p : 2 * p + 1], cum[2 * p + 1 : 2 * p + 2], prev[2 * p + 1 : 2 * p + 2]]
            + [jnp.zeros((4, length), F32)],
            axis=0,
        )
    head_of = lax.broadcasted_iota(jnp.int32, (heads, width), 1) >> log2(width // heads)
    mine = head_of == lax.broadcasted_iota(jnp.int32, (heads, width), 0)
    to_lanes = lambda col: jnp.sum(jnp.where(mine, col, 0.0), axis=0, keepdims=True)
    decay = to_lanes(jnp.exp(final))
    first_decay = to_lanes(jnp.exp(middle))
    second_decay = to_lanes(jnp.exp(final - middle))
    row8 = lax.broadcasted_iota(jnp.int32, (8, width), 0)
    coef_ref[...] = jnp.where(row8 == 0, first_decay, jnp.where(row8 == 1, second_decay, 0.0))
    copies[3].wait()
    copies[4].wait()
    for q in range(CHUNKS):
        at = slice(q * chunk, (q + 1) * chunk)
        spread_decs = decs[:, at].T.astype(BF16)
        for j, (ref, kind) in enumerate(((g_ref, 0), (g_ref, 1), (x_ref, 2), (x_ref, 3))):
            to = slice(j * width, (j + 1) * width)
            scaled_ref[at, to] = (ref[at].astype(F32) * mm(spread_decs, spread[:, to])).astype(BF16)
    copies[5].wait()
    onward, backward = [], []
    for q in range(CHUNKS):
        at = slice(q * chunk, (q + 1) * chunk)
        copies[6 + q].wait()
        projected = mm(tok_ref[at], w_ref[...])
        half = projected.shape[1] // 2
        bc_ref[at] = projected.astype(BF16)
        turned = pltpu.roll(projected, half, 1)
        cb_ref[at] = turned.astype(BF16)
        cb_t = turned.T.astype(BF16)
        parts = [scaled_ref[at, j * width : (j + 1) * width] for j in range(4)]
        onward.append(jnp.concatenate([mm(cb_t[:half], parts[1]), mm(cb_t[half:], parts[3])], axis=0))
        backward.append(jnp.concatenate([mm(cb_t[:half], parts[0]), mm(cb_t[half:], parts[2])], axis=0))

    near_ref[0] = onward[0]
    near_ref[1] = backward[1]
    next_total = onward[0] * second_decay + onward[1]
    prior_total = backward[0] + first_decay * backward[1]
    if n_seq == 4:
        here = lax.axis_index("seq")
        for k, ref in ((1, pay1_ref), (2, pay2_ref), (3, pay3_ref)):
            up = (here ^ k) > here

            @pl.when(up)
            def _():
                pack(ref, next_total, decay)

            @pl.when(jnp.logical_not(up))
            def _():
                pack(ref, prior_total, decay)
    else:
        pack(pay1_ref, next_total, decay)
        pack(pay2_ref, prior_total, decay)
        pack(pay3_ref, prior_total, decay)


def block_states(n_seq, tokens, x, g, dt, w, rate, bias):
    _, length, depth = tokens.shape
    width = x.shape[2]
    heads = dt.shape[1]
    two_n = w.shape[1]
    pay = jax.ShapeDtypeStruct((width // LANES * (two_n + 2), LANES), BF16)
    return pl.pallas_call(
        functools.partial(states_kernel, n_seq),
        name="block_states",
        in_specs=[HBM_SPEC] * 7,
        out_specs=[VMEM_SPEC] * 15,
        out_shape=[
            jax.ShapeDtypeStruct((length, two_n), BF16),
            jax.ShapeDtypeStruct((length, two_n), BF16),
            jax.ShapeDtypeStruct((heads // 2, 8, length), F32),
            jax.ShapeDtypeStruct((8 * heads, length), BF16),
            jax.ShapeDtypeStruct((8 * heads, 4 * width), BF16),
            jax.ShapeDtypeStruct((length, 4 * width), BF16),
            jax.ShapeDtypeStruct((2, two_n, width), F32),
            jax.ShapeDtypeStruct((8, width), F32),
            pay,
            pay,
            pay,
            jax.ShapeDtypeStruct((length, width), BF16),
            jax.ShapeDtypeStruct((length, width), BF16),
            jax.ShapeDtypeStruct((length, depth), BF16),
            jax.ShapeDtypeStruct((depth, two_n), BF16),
        ],
        scratch_shapes=[
            pltpu.VMEM((heads, length), F32),
            pltpu.SMEM((heads,), F32),
            pltpu.SMEM((heads,), F32),
            pltpu.SemaphoreType.DMA((8,)),
        ],
        compiler_params=LIMIT,
        cost_estimate=pl.CostEstimate(flops=2 * length * depth * two_n, bytes_accessed=5 << 20, transcendentals=0),
    )(*[pltpu.with_memory_space_constraint(a, pltpu.HBM) for a in (tokens, x, g, dt, w, rate, bias)])


def local_kernel(
    x_ref, g_ref, bc_ref, cb_ref, rows_ref, decs_ref, spread_ref, skip_ref,
    y_ref, gv_ref, gbc_ref, queries_ref, gvt_ref, gbt_ref, gc_ref,
):
    length, width = x_ref.shape
    lanes = 128
    n_pair = width // lanes
    chunk = length // CHUNKS
    tile = 128
    first_half = lax.broadcasted_iota(jnp.int32, (1, lanes), 1) < lanes // 2
    upper = lax.broadcasted_iota(jnp.int32, (lanes, 1), 0) < lanes // 2
    zero = jnp.zeros((), BF16)

    @pl.loop(0, CHUNKS)
    def _(q):
        s0 = pl.multiple_of(q * chunk, chunk)
        bc_s = bc_ref[pl.ds(s0, chunk), :]
        for tb in range(chunk // tile):
            t0 = pl.multiple_of(s0 + tb * tile, tile)
            cb_t = cb_ref[pl.ds(t0, tile), :]
            scores = mm_t(jnp.where(first_half, cb_t, zero), bc_s)
            row = tb * tile + lax.broadcasted_iota(jnp.int32, (tile, chunk), 0)
            col = lax.broadcasted_iota(jnp.int32, (tile, chunk), 1)
            below = col < row
            same = col == row
            total = None
            for p in range(n_pair):
                at = slice(p * lanes, (p + 1) * lanes)
                xp = x_ref[pl.ds(s0, chunk), at]
                x1, x2 = jnp.where(first_half, xp, zero), jnp.where(first_half, zero, xp)
                g_t = g_ref[pl.ds(t0, tile), at]
                gt = g_t.astype(F32).T.astype(BF16)
                cols = rows_ref[p, :, pl.ds(t0, tile)].T
                mains = []
                for k, xk in ((0, x1), (1, x2)):
                    gram = mm_t(g_t, xk)
                    cum_t, prev_t = cols[:, 2 * k : 2 * k + 1], cols[:, 2 * k + 1 : 2 * k + 2]
                    cum_s = rows_ref[p, 2 * k : 2 * k + 1, pl.ds(s0, chunk)]
                    prev_s = rows_ref[p, 2 * k + 1 : 2 * k + 2, pl.ds(s0, chunk)]
                    diff = jnp.minimum(jnp.where(below, cum_t - cum_s, prev_s - prev_t), 0.0)
                    kern = jnp.where(same, 0.0, jnp.exp(diff))
                    mains.append((scores * kern).astype(BF16))
                    term = gram * kern
                    total = term if total is None else total + term
                sk = jnp.where(first_half, skip_ref[2 * p], skip_ref[2 * p + 1])
                y = mm(mains[0], x1) + mm(mains[1], x2)
                y_ref[pl.ds(t0, tile), at] = y + sk * x_ref[pl.ds(t0, tile), at].astype(F32)
                gvt = mm(jnp.where(upper, gt, zero), mains[0]) + mm(jnp.where(upper, zero, gt), mains[1])
                if tb == 0:
                    gvt_ref[p] = gvt
                elif tb < chunk // tile - 1:
                    gvt_ref[p] += gvt
                else:
                    gs = g_ref[pl.ds(s0, chunk), at].astype(F32)
                    gv_ref[pl.ds(s0, chunk), at] = (gvt_ref[p] + gvt).T + sk * gs
            total = total.astype(BF16)
            gc_ref[tb * tile : (tb + 1) * tile] = mm(total, cb_ref[pl.ds(s0, chunk), :])
            gbt = mm(cb_t.astype(F32).T.astype(BF16), total)
            if tb == 0:
                gbt_ref[...] = gbt
            else:
                gbt_ref[...] += gbt
        gbc_ref[pl.ds(s0, chunk), :] = jnp.where(first_half, gbt_ref[...].T, gc_ref[...])

        e = mm(decs_ref[:, pl.ds(s0, chunk)].astype(F32).T.astype(BF16), spread_ref[...])
        bc = bc_s.astype(F32)
        cb = cb_ref[pl.ds(s0, chunk), :].astype(F32)
        cc, bb = jnp.where(first_half, cb, bc), jnp.where(first_half, bc, cb)
        for j, (query, kind) in enumerate(((cc, 0), (cc, 1), (bb, 2), (bb, 3))):
            for p in range(n_pair):
                value = query * e[:, kind * width + p * lanes : kind * width + (p + 1) * lanes]
                to = (j // 2) * 2 * width + p * 2 * lanes + (j % 2) * lanes
                queries_ref[pl.ds(s0, chunk), to : to + lanes] = value.astype(BF16)


def inside_chunks(x, g, bc, cb, rows, decs, spread, skip):
    length, width = x.shape
    n_pair = width // 128
    chunk = length // CHUNKS
    return pl.pallas_call(
        local_kernel,
        name="inside_chunks",
        in_specs=[VMEM_SPEC] * 7 + [SMEM_SPEC],
        out_specs=[VMEM_SPEC] * 4,
        out_shape=[
            jax.ShapeDtypeStruct((length, width), F32),
            jax.ShapeDtypeStruct((length, width), F32),
            jax.ShapeDtypeStruct((length, 128), F32),
            jax.ShapeDtypeStruct((length, 4 * width), BF16),
        ],
        scratch_shapes=[
            pltpu.VMEM((n_pair, 128, chunk), F32),
            pltpu.VMEM((128, chunk), F32),
            pltpu.VMEM((chunk, 128), F32),
        ],
        compiler_params=LIMIT,
        cost_estimate=pl.CostEstimate(
            flops=6 * length * length * width, bytes_accessed=4 << 20, transcendentals=2 * n_pair * length * length
        ),
    )(x, g, bc, cb, rows, decs, spread, skip)


def combine_received(direct, refs, two_n):
    if not direct:
        return refs[0][...], refs[1][...]
    here = lax.axis_index("seq")
    states, decays = zip(*[unpack(r[...], two_n) for r in refs])
    width = states[0].shape[1]
    before = jnp.zeros((two_n, width), F32)
    after = jnp.zeros((two_n, width), F32)
    for k in (1, 2, 3):
        there = here ^ k
        low, high = jnp.minimum(here, there), jnp.maximum(here, there)
        factor = jnp.ones((1, width), F32)
        for m in (1, 2, 3):
            if m != k:
                mid = here ^ m
                inside = jnp.logical_and(mid > low, mid < high)
                factor = factor * jnp.where(inside, decays[m - 1], 1.0)
        part = states[k - 1]
        earlier = there < here
        before = before + part * jnp.where(earlier, factor, 0.0)
        after = after + part * jnp.where(earlier, 0.0, factor)
    return before, after


def group_kernel(direct, count, *refs):
    received = refs[:count]
    near_ref, coef_ref, scaled_ref, gbc_ref, group_ref, before_ref, after_ref = refs[count:]
    if direct:
        received = [received[ORDER_A.index(k)] for k in (1, 2, 3)]
    length, two_n = group_ref.shape
    width = coef_ref.shape[1]
    chunk = length // CHUNKS
    before, after = combine_received(direct, received, two_n)
    befores = [before.astype(BF16), (near_ref[0] + coef_ref[0:1] * before).astype(BF16)]
    afters = [(near_ref[1] + coef_ref[1:2] * after).astype(BF16), after.astype(BF16)]
    left = lax.broadcasted_iota(jnp.int32, (1, two_n), 1) < two_n // 2
    for q in range(CHUNKS):
        at = slice(q * chunk, (q + 1) * chunk)
        before_ref[q] = befores[q]
        after_ref[q] = afters[q]
        both = jnp.concatenate([befores[q], afters[q]], axis=1)
        from_g = mm_t(scaled_ref[at, : 2 * width], both)
        from_x = mm_t(scaled_ref[at, 2 * width :], both)
        group_ref[at] = (gbc_ref[at] + jnp.where(left, from_x, from_g)).astype(BF16)


def group_sums(direct, received, near, coef, scaled, gbc):
    length, two_n = gbc.shape
    width = coef.shape[1]
    state = jax.ShapeDtypeStruct((CHUNKS, two_n, width), BF16)
    return pl.pallas_call(
        functools.partial(group_kernel, direct, len(received)),
        name="group_sums",
        in_specs=[VMEM_SPEC] * (4 + len(received)),
        out_specs=[VMEM_SPEC] * 3,
        out_shape=[jax.ShapeDtypeStruct((length, two_n), BF16), state, state],
        compiler_params=LIMIT,
        cost_estimate=pl.CostEstimate(flops=8 * length * two_n * width, bytes_accessed=3 << 20, transcendentals=0),
    )(*received, near, coef, scaled, gbc)


def carry_kernel(before_ref, after_ref, queries_ref, y_ref, gv_ref, yo_ref, gvo_ref):
    step = pl.program_id(0)
    _, two_n, width = before_ref.shape
    chunk = yo_ref.shape[0]
    lanes = 128
    half = two_n // 2
    before = before_ref[step]
    after = after_ref[step]
    first_half = lax.broadcasted_iota(jnp.int32, (1, lanes), 1) < lanes // 2
    zero = jnp.zeros((), BF16)
    s0 = pl.multiple_of(step * chunk, chunk)

    def apart(v):
        return [jnp.where(first_half, v, zero), jnp.where(first_half, zero, v)]

    for p in range(width // lanes):
        at = slice(p * lanes, (p + 1) * lanes)
        main = jnp.concatenate(apart(before[half:, at]) + apart(after[half:, at]), axis=0)
        back = jnp.concatenate(apart(before[:half, at]) + apart(after[:half, at]), axis=0)
        wide = slice(2 * p * lanes, 2 * (p + 1) * lanes)
        wide2 = slice(2 * width + 2 * p * lanes, 2 * width + 2 * (p + 1) * lanes)
        yo_ref[:, at] = (y_ref[pl.ds(s0, chunk), at] + mm(queries_ref[pl.ds(s0, chunk), wide], main)).astype(BF16)
        gvo_ref[:, at] = (gv_ref[pl.ds(s0, chunk), at] + mm(queries_ref[pl.ds(s0, chunk), wide2], back)).astype(BF16)


def add_carries(before, after, queries, y, gv):
    length, width = y.shape
    two_n = before.shape[1]
    chunk = length // CHUNKS
    part3 = pl.BlockSpec((None, chunk, width), lambda i: (0, i, 0))
    out = jax.ShapeDtypeStruct((1, length, width), BF16)
    return pl.pallas_call(
        carry_kernel,
        name="add_carries",
        grid=(CHUNKS,),
        in_specs=[VMEM_SPEC] * 5,
        out_specs=[part3, part3],
        out_shape=[out, out],
        compiler_params=LIMIT,
        cost_estimate=pl.CostEstimate(flops=8 * length * two_n * width, bytes_accessed=5 << 20, transcendentals=0),
    )(before, after, queries, y, gv)


def scanned_generic(onward, backward, two_n):
    size, here = lax.axis_size("seq"), lax.axis_index("seq")

    def total(payload, reverse):
        every = lax.all_gather(payload, "seq")

        def step(k, before):
            at = size - 1 - k if reverse else k
            state, decay = unpack(every[at], two_n)
            new = before * decay + state
            return jnp.where(at > here if reverse else at < here, new, before)

        return lax.fori_loop(0, size, step, jnp.zeros((two_n, LANES * (payload.shape[0] // (two_n + 2))), F32))

    return total(onward, False), total(backward, True)


def away_kernel(a0_ref, a1_ref, a2_ref, a3_ref, tokens_ref, grad_ref, grad_t_ref, send_ref):
    total = a0_ref[...].astype(F32) + a1_ref[...].astype(F32) + a2_ref[...].astype(F32) + a3_ref[...].astype(F32)
    grad = total.astype(BF16)
    grad_ref[...] = grad
    grad_t = grad.astype(F32).T.astype(BF16)
    grad_t_ref[...] = grad_t
    here = lax.axis_index("dp")
    n_seq, _, cols = send_ref.shape
    for s in range(n_seq):
        away = pl.multiple_of(((1 - here) * n_seq + s) * cols, cols)
        send_ref[s] = mm(grad_t, tokens_ref[:, pl.ds(away, cols)]).astype(BF16)


def home_kernel(grad_t_ref, tokens_ref, keep_ref):
    here = lax.axis_index("dp")
    n_seq, _, cols = keep_ref.shape
    for s in range(n_seq):
        home = pl.multiple_of((here * n_seq + s) * cols, cols)
        keep_ref[s] = mm(grad_t_ref[...], tokens_ref[:, pl.ds(home, cols)])


def weight_away(n_seq, groups, tokens):
    length, depth = tokens.shape
    two_n = groups[0].shape[1]
    cols = depth // (2 * n_seq)
    return pl.pallas_call(
        away_kernel,
        name="weight_away",
        in_specs=[VMEM_SPEC] * 5,
        out_specs=[VMEM_SPEC] * 3,
        out_shape=[
            jax.ShapeDtypeStruct((length, two_n), BF16),
            jax.ShapeDtypeStruct((two_n, length), BF16),
            jax.ShapeDtypeStruct((n_seq, two_n, cols), BF16),
        ],
        compiler_params=LIMIT,
        cost_estimate=pl.CostEstimate(flops=length * two_n * depth, bytes_accessed=2 << 20, transcendentals=0),
    )(*groups, tokens)


def weight_home(n_seq, grad_t, tokens):
    length, depth = tokens.shape
    two_n = grad_t.shape[0]
    cols = depth // (2 * n_seq)
    return pl.pallas_call(
        home_kernel,
        name="weight_home",
        in_specs=[VMEM_SPEC] * 2,
        out_specs=VMEM_SPEC,
        out_shape=jax.ShapeDtypeStruct((n_seq, two_n, cols), F32),
        compiler_params=LIMIT,
        cost_estimate=pl.CostEstimate(flops=length * two_n * depth, bytes_accessed=2 << 20, transcendentals=0),
    )(grad_t, tokens)


def pair_kernel(keep_ref, got_ref, own_ref, s1_ref, s2_ref, s3_ref):
    here = lax.axis_index("seq")
    own_ref[...] = keep_ref[here] + got_ref[here].astype(F32)
    for k, ref in ((1, s1_ref), (2, s2_ref), (3, s3_ref)):
        at = here ^ k
        ref[...] = (keep_ref[at] + got_ref[at].astype(F32)).astype(BF16)


def pair_sum(keep, got):
    _, two_n, cols = keep.shape
    small = jax.ShapeDtypeStruct((two_n, cols), BF16)
    return pl.pallas_call(
        pair_kernel,
        name="pair_sum",
        compiler_params=LIMIT,
        in_specs=[VMEM_SPEC, VMEM_SPEC],
        out_specs=[VMEM_SPEC] * 4,
        out_shape=[jax.ShapeDtypeStruct((two_n, cols), F32), small, small, small],
    )(keep, got)


def final_kernel(scale, own_ref, r3_ref, r2_ref, r1_ref, out_ref):
    total = own_ref[...] + r1_ref[...].astype(F32) + r2_ref[...].astype(F32) + r3_ref[...].astype(F32)
    out_ref[...] = total.T * scale


def final_sum(scale, own, r3, r2, r1):
    two_n, cols = own.shape
    return pl.pallas_call(
        functools.partial(final_kernel, scale),
        name="final_sum",
        compiler_params=LIMIT,
        in_specs=[VMEM_SPEC] * 4,
        out_specs=VMEM_SPEC,
        out_shape=jax.ShapeDtypeStruct((cols, two_n), F32),
    )(own, r3, r2, r1)


def input_kernel(grad_ref, w_ref, out_ref):
    out_ref[...] = mm_t(grad_ref[...], w_ref[...]).astype(BF16)


def input_grad(grad, w):
    length, two_n = grad.shape
    depth = w.shape[0]
    steps = 4
    chunk = length // steps
    return pl.pallas_call(
        input_kernel,
        name="input_grad",
        grid=(steps,),
        in_specs=[pl.BlockSpec((chunk, two_n), lambda i: (i, 0)), pl.BlockSpec((depth, two_n), lambda i: (0, 0))],
        out_specs=pl.BlockSpec((None, chunk, depth), lambda i: (0, i, 0)),
        out_shape=jax.ShapeDtypeStruct((1, length, depth), BF16),
        compiler_params=LIMIT,
        cost_estimate=pl.CostEstimate(flops=2 * length * two_n * depth, bytes_accessed=3 << 20, transcendentals=0),
    )(grad, w)


def swap(value, axis, k):
    return lax.ppermute(value, axis, [(i, i ^ k) for i in range(lax.axis_size(axis))])


def per_device(layer_input, head_values, dt_raw, w_bc, decay_rate, dt_bias, skip_gain, grad_y):
    n_seq, n_head, n_dp = lax.axis_size("seq"), lax.axis_size("head"), lax.axis_size("dp")
    length = layer_input.shape[1]
    two_n = w_bc.shape[1]
    bc, cb, rows, decs, spread, scaled, near, coef, pay1, pay2, pay3, x, g, tokens, w = block_states(
        n_seq, layer_input, head_values, grad_y, dt_raw, w_bc, decay_rate, dt_bias
    )
    direct = n_seq == 4
    if direct:
        received = [swap((pay1, pay2, pay3)[k - 1], "seq", k) for k in ORDER_A]
    else:
        received = scanned_generic(pay1, pay2, two_n)
    y_local, gv_local, gbc_local, queries = inside_chunks(
        x, g, bc, cb, rows, decs, spread, skip_gain
    )
    group, before, after = group_sums(direct, received, near, coef, scaled, gbc_local)
    total_tokens = n_dp * n_seq * length
    if direct and n_dp == 2 and n_head == 4:
        others = [swap(group, "head", k) for k in ORDER_B[::-1]]
        y_out, grad_values = add_carries(before, after, queries, y_local, gv_local)
        *others, y_out = lax.optimization_barrier((*others, y_out))
        groups = [group, *others]
        grad_bc, grad_t, send = weight_away(n_seq, groups, tokens)
        got = swap(send, "dp", 1)
        keep = weight_home(n_seq, grad_t, tokens)
        own, s1, s2, s3 = pair_sum(keep, got)
        sums = [swap((s1, s2, s3)[k - 1], "seq", k) for k in ORDER_C]
        grad_w_bc = final_sum(1.0 / total_tokens, own, *sums)
    else:
        y_out, grad_values = add_carries(before, after, queries, y_local, gv_local)
        grad_bc = lax.psum(group.astype(F32), "head").astype(BF16)
        part = jnp.einsum("td,tk->dk", tokens, grad_bc, preferred_element_type=F32)
        grad_w_bc = lax.psum_scatter(part, ("dp", "seq"), scatter_dimension=0, tiled=True) / total_tokens
    grad_input = input_grad(grad_bc, w)
    return y_out, grad_values, grad_input, grad_w_bc


def solution(mesh):
    in_specs = (
        P("dp", "seq", None),
        P("dp", "seq", "head"),
        P("dp", "head", "seq"),
        P(),
        P("head"),
        P("head"),
        P("head"),
        P("dp", "seq", "head"),
    )
    out_specs = (
        P("dp", "seq", "head"),
        P("dp", "seq", "head"),
        P("dp", "seq", None),
        P(("dp", "seq"), None),
    )
    return jax.shard_map(per_device, mesh=mesh, in_specs=in_specs, out_specs=out_specs, check_vma=False)
```

```python
import functools

import jax
import jax.numpy as jnp
from jax import lax
from jax.experimental import pallas as pl
from jax.experimental.pallas import tpu as pltpu
from jax.sharding import PartitionSpec as P

F32 = jnp.float32
BF16 = jnp.bfloat16
VMEM_SPEC = pl.BlockSpec(memory_space=pltpu.VMEM)
SMEM_SPEC = pl.BlockSpec(memory_space=pltpu.SMEM)
LANES = 128
ORDER_A = (2, 1, 3)
ORDER_B = (3, 2, 1)
ORDER_C = (3, 2, 1)


def mm(a, b):
    return jnp.dot(a, b, preferred_element_type=F32)


def mm_t(a, b):
    return lax.dot_general(a, b, (((1,), (1,)), ((), ())), preferred_element_type=F32)


LIMIT = pltpu.CompilerParams(vmem_limit_bytes=20 << 20)
HBM_SPEC = pl.BlockSpec(memory_space=pltpu.HBM)
CHUNKS = 2


def log2(n):
    return n.bit_length() - 1


def spread_matrix(heads, width):
    rows = 8 * heads
    row = lax.broadcasted_iota(jnp.int32, (rows, 4 * width), 0)
    col = lax.broadcasted_iota(jnp.int32, (rows, 4 * width), 1)
    kind_ok = (row >> log2(2 * heads)) == (col >> log2(width))
    head_ok = (row & (heads - 1)) == ((col & (width - 1)) >> log2(width // heads))
    return jnp.where(kind_ok & head_ok, 1.0, 0.0).astype(BF16)


def pack(ref, state, decay):
    rows, width = state.shape
    blocks = width // LANES
    high = decay.astype(BF16).astype(F32)
    for p in range(blocks):
        ref[p * rows : (p + 1) * rows] = state[:, p * LANES : (p + 1) * LANES].astype(BF16)
    parts = [v[:, p * LANES : (p + 1) * LANES] for v in (high, decay - high) for p in range(blocks)]
    ref[blocks * rows :] = jnp.concatenate(parts, axis=0).astype(BF16)


def unpack(payload, rows):
    blocks = payload.shape[0] // (rows + 2)
    state = jnp.concatenate([payload[p * rows : (p + 1) * rows] for p in range(blocks)], axis=1).astype(F32)
    tail = payload[blocks * rows :].astype(F32)
    decay = jnp.concatenate([tail[p : p + 1] + tail[blocks + p : blocks + p + 1] for p in range(blocks)], axis=1)
    return state, decay


def mm_rows(a, b):
    return lax.dot_general(a, b, (((0,), (0,)), ((), ())), preferred_element_type=F32)


def states_kernel(
    n_seq, tokens_hbm, x_hbm, g_hbm, dt_hbm, w_hbm, rate_hbm, bias_hbm,
    bc_ref, cb_ref, rows_ref, decs_ref, spread_ref, scaled_ref, near_ref, coef_ref, pay1_ref, pay2_ref, pay3_ref,
    x_ref, g_ref, tok_ref, w_ref, dt_ref, rate_ref, bias_ref, sems,
):
    heads, length = dt_ref.shape
    chunk = length // CHUNKS
    width = x_ref.shape[1]
    copies = [
        pltpu.make_async_copy(dt_hbm.at[0], dt_ref, sems.at[0]),
        pltpu.make_async_copy(rate_hbm, rate_ref, sems.at[1]),
        pltpu.make_async_copy(bias_hbm, bias_ref, sems.at[2]),
        pltpu.make_async_copy(g_hbm.at[0], g_ref, sems.at[3]),
        pltpu.make_async_copy(x_hbm.at[0], x_ref, sems.at[4]),
        pltpu.make_async_copy(w_hbm, w_ref, sems.at[5]),
        pltpu.make_async_copy(tokens_hbm.at[0, :chunk], tok_ref.at[:chunk], sems.at[6]),
        pltpu.make_async_copy(tokens_hbm.at[0, chunk:], tok_ref.at[chunk:], sems.at[7]),
    ]
    for c in copies:
        c.start()
    spread = spread_matrix(heads, width)
    spread_ref[...] = spread
    for c in copies[:3]:
        c.wait()
    sub = lax.broadcasted_iota(jnp.int32, (heads, 1), 0)
    rate = jnp.zeros((heads, 1), F32)
    bias = jnp.zeros((heads, 1), F32)
    for h in range(heads):
        rate = jnp.where(sub == h, rate_ref[h], rate)
        bias = jnp.where(sub == h, bias_ref[h], bias)
    v = dt_ref[...] + bias
    log_step = -rate * (jnp.maximum(v, 0.0) + jnp.log1p(jnp.exp(-jnp.abs(v))))
    lane = lax.broadcasted_iota(jnp.int32, (heads, length), 1)
    cum = log_step
    shift = 1
    while shift < length:
        cum = cum + jnp.where(lane >= shift, pltpu.roll(cum, shift, 1), 0.0)
        shift *= 2
    prev = cum - log_step
    middle = cum[:, chunk - 1 : chunk]
    final = cum[:, length - 1 : length]
    second = lane >= chunk
    begin = jnp.where(second, middle, 0.0)
    end = jnp.where(second, final, middle)
    kinds = (jnp.exp(cum - begin), jnp.exp(end - prev), jnp.exp(jnp.minimum(prev - begin, 0.0)), jnp.exp(end - cum))
    parts = []
    for k in kinds:
        high = k.astype(BF16).astype(F32)
        parts += [high, k - high]
    decs = jnp.concatenate(parts, axis=0)
    decs_ref[...] = decs.astype(BF16)
    for p in range(heads // 2):
        rows_ref[p] = jnp.concatenate(
            [cum[2 * p : 2 * p + 1], prev[2 * p : 2 * p + 1], cum[2 * p + 1 : 2 * p + 2], prev[2 * p + 1 : 2 * p + 2]]
            + [jnp.zeros((4, length), F32)],
            axis=0,
        )
    head_of = lax.broadcasted_iota(jnp.int32, (heads, width), 1) >> log2(width // heads)
    mine = head_of == lax.broadcasted_iota(jnp.int32, (heads, width), 0)
    to_lanes = lambda col: jnp.sum(jnp.where(mine, col, 0.0), axis=0, keepdims=True)
    decay = to_lanes(jnp.exp(final))
    first_decay = to_lanes(jnp.exp(middle))
    second_decay = to_lanes(jnp.exp(final - middle))
    row8 = lax.broadcasted_iota(jnp.int32, (8, width), 0)
    coef_ref[...] = jnp.where(row8 == 0, first_decay, jnp.where(row8 == 1, second_decay, 0.0))
    copies[3].wait()
    copies[4].wait()
    for q in range(CHUNKS):
        at = slice(q * chunk, (q + 1) * chunk)
        chunk_decs = decs[:, at].astype(BF16)
        for j, (ref, kind) in enumerate(((g_ref, 0), (g_ref, 1), (x_ref, 2), (x_ref, 3))):
            to = slice(j * width, (j + 1) * width)
            scaled_ref[at, to] = (ref[at].astype(F32) * mm_rows(chunk_decs, spread[:, to])).astype(BF16)
    copies[5].wait()
    onward, backward = [], []
    for q in range(CHUNKS):
        at = slice(q * chunk, (q + 1) * chunk)
        copies[6 + q].wait()
        projected = mm(tok_ref[at], w_ref[...])
        half = projected.shape[1] // 2
        bc_ref[at] = projected.astype(BF16)
        turned = pltpu.roll(projected, half, 1)
        cb_ref[at] = turned.astype(BF16)
        cb_t = turned.astype(BF16).T
        parts = [scaled_ref[at, j * width : (j + 1) * width] for j in range(4)]
        onward.append(jnp.concatenate([mm(cb_t[:half], parts[1]), mm(cb_t[half:], parts[3])], axis=0))
        backward.append(jnp.concatenate([mm(cb_t[:half], parts[0]), mm(cb_t[half:], parts[2])], axis=0))

    near_ref[0] = onward[0]
    near_ref[1] = backward[1]
    next_total = onward[0] * second_decay + onward[1]
    prior_total = backward[0] + first_decay * backward[1]
    if n_seq == 4:
        here = lax.axis_index("seq")
        for k, ref in ((1, pay1_ref), (2, pay2_ref), (3, pay3_ref)):
            up = (here ^ k) > here

            @pl.when(up)
            def _():
                pack(ref, next_total, decay)

            @pl.when(jnp.logical_not(up))
            def _():
                pack(ref, prior_total, decay)
    else:
        pack(pay1_ref, next_total, decay)
        pack(pay2_ref, prior_total, decay)
        pack(pay3_ref, prior_total, decay)


def block_states(n_seq, tokens, x, g, dt, w, rate, bias):
    _, length, depth = tokens.shape
    width = x.shape[2]
    heads = dt.shape[1]
    two_n = w.shape[1]
    pay = jax.ShapeDtypeStruct((width // LANES * (two_n + 2), LANES), BF16)
    return pl.pallas_call(
        functools.partial(states_kernel, n_seq),
        name="block_states",
        in_specs=[HBM_SPEC] * 7,
        out_specs=[VMEM_SPEC] * 15,
        out_shape=[
            jax.ShapeDtypeStruct((length, two_n), BF16),
            jax.ShapeDtypeStruct((length, two_n), BF16),
            jax.ShapeDtypeStruct((heads // 2, 8, length), F32),
            jax.ShapeDtypeStruct((8 * heads, length), BF16),
            jax.ShapeDtypeStruct((8 * heads, 4 * width), BF16),
            jax.ShapeDtypeStruct((length, 4 * width), BF16),
            jax.ShapeDtypeStruct((2, two_n, width), F32),
            jax.ShapeDtypeStruct((8, width), F32),
            pay,
            pay,
            pay,
            jax.ShapeDtypeStruct((length, width), BF16),
            jax.ShapeDtypeStruct((length, width), BF16),
            jax.ShapeDtypeStruct((length, depth), BF16),
            jax.ShapeDtypeStruct((depth, two_n), BF16),
        ],
        scratch_shapes=[
            pltpu.VMEM((heads, length), F32),
            pltpu.SMEM((heads,), F32),
            pltpu.SMEM((heads,), F32),
            pltpu.SemaphoreType.DMA((8,)),
        ],
        compiler_params=LIMIT,
        cost_estimate=pl.CostEstimate(flops=2 * length * depth * two_n, bytes_accessed=5 << 20, transcendentals=0),
    )(*[pltpu.with_memory_space_constraint(a, pltpu.HBM) for a in (tokens, x, g, dt, w, rate, bias)])


def local_kernel(
    x_ref, g_ref, bc_ref, cb_ref, rows_ref, decs_ref, spread_ref, skip_ref,
    y_ref, gv_ref, gbc_ref, queries_ref, gvt_ref, gbt_ref, gc_ref,
):
    length, width = x_ref.shape
    lanes = 128
    n_pair = width // lanes
    chunk = length // CHUNKS
    tile = 128
    first_half = lax.broadcasted_iota(jnp.int32, (1, lanes), 1) < lanes // 2
    upper = lax.broadcasted_iota(jnp.int32, (lanes, 1), 0) < lanes // 2
    zero = jnp.zeros((), BF16)

    @pl.loop(0, CHUNKS)
    def _(q):
        s0 = pl.multiple_of(q * chunk, chunk)
        bc_s = bc_ref[pl.ds(s0, chunk), :]
        for tb in range(chunk // tile):
            t0 = pl.multiple_of(s0 + tb * tile, tile)
            cb_t = cb_ref[pl.ds(t0, tile), :]
            scores = mm_t(jnp.where(first_half, cb_t, zero), bc_s)
            row = tb * tile + lax.broadcasted_iota(jnp.int32, (tile, chunk), 0)
            col = lax.broadcasted_iota(jnp.int32, (tile, chunk), 1)
            below = col < row
            same = col == row
            total = None
            for p in range(n_pair):
                at = slice(p * lanes, (p + 1) * lanes)
                xp = x_ref[pl.ds(s0, chunk), at]
                x1, x2 = jnp.where(first_half, xp, zero), jnp.where(first_half, zero, xp)
                g_t = g_ref[pl.ds(t0, tile), at]
                gt = g_t.astype(F32).T.astype(BF16)
                cols = rows_ref[p, :, pl.ds(t0, tile)].T
                mains = []
                for k, xk in ((0, x1), (1, x2)):
                    gram = mm_t(g_t, xk)
                    cum_t, prev_t = cols[:, 2 * k : 2 * k + 1], cols[:, 2 * k + 1 : 2 * k + 2]
                    cum_s = rows_ref[p, 2 * k : 2 * k + 1, pl.ds(s0, chunk)]
                    prev_s = rows_ref[p, 2 * k + 1 : 2 * k + 2, pl.ds(s0, chunk)]
                    diff = jnp.minimum(jnp.where(below, cum_t - cum_s, prev_s - prev_t), 0.0)
                    kern = jnp.where(same, 0.0, jnp.exp(diff))
                    mains.append((scores * kern).astype(BF16))
                    term = gram * kern
                    total = term if total is None else total + term
                sk = jnp.where(first_half, skip_ref[2 * p], skip_ref[2 * p + 1])
                y = mm(mains[0], x1) + mm(mains[1], x2)
                y_ref[pl.ds(t0, tile), at] = y + sk * x_ref[pl.ds(t0, tile), at].astype(F32)
                gvt = mm(jnp.where(upper, gt, zero), mains[0]) + mm(jnp.where(upper, zero, gt), mains[1])
                if tb == 0:
                    gvt_ref[p] = gvt
                elif tb < chunk // tile - 1:
                    gvt_ref[p] += gvt
                else:
                    gs = g_ref[pl.ds(s0, chunk), at].astype(F32)
                    gv_ref[pl.ds(s0, chunk), at] = (gvt_ref[p] + gvt).T + sk * gs
            total = total.astype(BF16)
            gc_ref[tb * tile : (tb + 1) * tile] = mm(total, cb_ref[pl.ds(s0, chunk), :])
            gbt = mm(cb_t.astype(F32).T.astype(BF16), total)
            if tb == 0:
                gbt_ref[...] = gbt
            else:
                gbt_ref[...] += gbt
        gbc_ref[pl.ds(s0, chunk), :] = jnp.where(first_half, gbt_ref[...].T, gc_ref[...])

        e = mm(decs_ref[:, pl.ds(s0, chunk)].astype(F32).T.astype(BF16), spread_ref[...])
        bc = bc_s.astype(F32)
        cb = cb_ref[pl.ds(s0, chunk), :].astype(F32)
        cc, bb = jnp.where(first_half, cb, bc), jnp.where(first_half, bc, cb)
        for j, (query, kind) in enumerate(((cc, 0), (cc, 1), (bb, 2), (bb, 3))):
            for p in range(n_pair):
                value = query * e[:, kind * width + p * lanes : kind * width + (p + 1) * lanes]
                to = (j // 2) * 2 * width + p * 2 * lanes + (j % 2) * lanes
                queries_ref[pl.ds(s0, chunk), to : to + lanes] = value.astype(BF16)


def inside_chunks(x, g, bc, cb, rows, decs, spread, skip):
    length, width = x.shape
    n_pair = width // 128
    chunk = length // CHUNKS
    return pl.pallas_call(
        local_kernel,
        name="inside_chunks",
        in_specs=[VMEM_SPEC] * 7 + [SMEM_SPEC],
        out_specs=[VMEM_SPEC] * 4,
        out_shape=[
            jax.ShapeDtypeStruct((length, width), F32),
            jax.ShapeDtypeStruct((length, width), F32),
            jax.ShapeDtypeStruct((length, 128), F32),
            jax.ShapeDtypeStruct((length, 4 * width), BF16),
        ],
        scratch_shapes=[
            pltpu.VMEM((n_pair, 128, chunk), F32),
            pltpu.VMEM((128, chunk), F32),
            pltpu.VMEM((chunk, 128), F32),
        ],
        compiler_params=LIMIT,
        cost_estimate=pl.CostEstimate(
            flops=6 * length * length * width, bytes_accessed=4 << 20, transcendentals=2 * n_pair * length * length
        ),
    )(x, g, bc, cb, rows, decs, spread, skip)


def combine_received(direct, refs, two_n):
    if not direct:
        return refs[0][...], refs[1][...]
    here = lax.axis_index("seq")
    states, decays = zip(*[unpack(r[...], two_n) for r in refs])
    width = states[0].shape[1]
    before = jnp.zeros((two_n, width), F32)
    after = jnp.zeros((two_n, width), F32)
    for k in (1, 2, 3):
        there = here ^ k
        low, high = jnp.minimum(here, there), jnp.maximum(here, there)
        factor = jnp.ones((1, width), F32)
        for m in (1, 2, 3):
            if m != k:
                mid = here ^ m
                inside = jnp.logical_and(mid > low, mid < high)
                factor = factor * jnp.where(inside, decays[m - 1], 1.0)
        part = states[k - 1]
        earlier = there < here
        before = before + part * jnp.where(earlier, factor, 0.0)
        after = after + part * jnp.where(earlier, 0.0, factor)
    return before, after


def group_kernel(direct, count, *refs):
    received = refs[:count]
    near_ref, coef_ref, scaled_ref, gbc_ref, group_ref, before_ref, after_ref = refs[count:]
    if direct:
        received = [received[ORDER_A.index(k)] for k in (1, 2, 3)]
    length, two_n = group_ref.shape
    width = coef_ref.shape[1]
    chunk = length // CHUNKS
    before, after = combine_received(direct, received, two_n)
    befores = [before.astype(BF16), (near_ref[0] + coef_ref[0:1] * before).astype(BF16)]
    afters = [(near_ref[1] + coef_ref[1:2] * after).astype(BF16), after.astype(BF16)]
    left = lax.broadcasted_iota(jnp.int32, (1, two_n), 1) < two_n // 2
    for q in range(CHUNKS):
        at = slice(q * chunk, (q + 1) * chunk)
        before_ref[q] = befores[q]
        after_ref[q] = afters[q]
        both = jnp.concatenate([befores[q], afters[q]], axis=1)
        from_g = mm_t(scaled_ref[at, : 2 * width], both)
        from_x = mm_t(scaled_ref[at, 2 * width :], both)
        group_ref[at] = (gbc_ref[at] + jnp.where(left, from_x, from_g)).astype(BF16)


def group_sums(direct, received, near, coef, scaled, gbc):
    length, two_n = gbc.shape
    width = coef.shape[1]
    state = jax.ShapeDtypeStruct((CHUNKS, two_n, width), BF16)
    return pl.pallas_call(
        functools.partial(group_kernel, direct, len(received)),
        name="group_sums",
        in_specs=[VMEM_SPEC] * (4 + len(received)),
        out_specs=[VMEM_SPEC] * 3,
        out_shape=[jax.ShapeDtypeStruct((length, two_n), BF16), state, state],
        compiler_params=LIMIT,
        cost_estimate=pl.CostEstimate(flops=8 * length * two_n * width, bytes_accessed=3 << 20, transcendentals=0),
    )(*received, near, coef, scaled, gbc)


def carry_kernel(before_ref, after_ref, queries_ref, y_ref, gv_ref, yo_ref, gvo_ref):
    step = pl.program_id(0)
    _, two_n, width = before_ref.shape
    chunk = yo_ref.shape[0]
    lanes = 128
    half = two_n // 2
    before = before_ref[step]
    after = after_ref[step]
    first_half = lax.broadcasted_iota(jnp.int32, (1, lanes), 1) < lanes // 2
    zero = jnp.zeros((), BF16)
    s0 = pl.multiple_of(step * chunk, chunk)

    def apart(v):
        return [jnp.where(first_half, v, zero), jnp.where(first_half, zero, v)]

    for p in range(width // lanes):
        at = slice(p * lanes, (p + 1) * lanes)
        main = jnp.concatenate(apart(before[half:, at]) + apart(after[half:, at]), axis=0)
        back = jnp.concatenate(apart(before[:half, at]) + apart(after[:half, at]), axis=0)
        wide = slice(2 * p * lanes, 2 * (p + 1) * lanes)
        wide2 = slice(2 * width + 2 * p * lanes, 2 * width + 2 * (p + 1) * lanes)
        yo_ref[:, at] = (y_ref[pl.ds(s0, chunk), at] + mm(queries_ref[pl.ds(s0, chunk), wide], main)).astype(BF16)
        gvo_ref[:, at] = (gv_ref[pl.ds(s0, chunk), at] + mm(queries_ref[pl.ds(s0, chunk), wide2], back)).astype(BF16)


def add_carries(before, after, queries, y, gv):
    length, width = y.shape
    two_n = before.shape[1]
    chunk = length // CHUNKS
    part3 = pl.BlockSpec((None, chunk, width), lambda i: (0, i, 0))
    out = jax.ShapeDtypeStruct((1, length, width), BF16)
    return pl.pallas_call(
        carry_kernel,
        name="add_carries",
        grid=(CHUNKS,),
        in_specs=[VMEM_SPEC] * 5,
        out_specs=[part3, part3],
        out_shape=[out, out],
        compiler_params=LIMIT,
        cost_estimate=pl.CostEstimate(flops=8 * length * two_n * width, bytes_accessed=5 << 20, transcendentals=0),
    )(before, after, queries, y, gv)


def scanned_generic(onward, backward, two_n):
    size, here = lax.axis_size("seq"), lax.axis_index("seq")

    def total(payload, reverse):
        every = lax.all_gather(payload, "seq")

        def step(k, before):
            at = size - 1 - k if reverse else k
            state, decay = unpack(every[at], two_n)
            new = before * decay + state
            return jnp.where(at > here if reverse else at < here, new, before)

        return lax.fori_loop(0, size, step, jnp.zeros((two_n, LANES * (payload.shape[0] // (two_n + 2))), F32))

    return total(onward, False), total(backward, True)


def away_kernel(a0_ref, a1_ref, a2_ref, a3_ref, tokens_ref, grad_ref, grad_t_ref, send_ref):
    total = a0_ref[...].astype(F32) + a1_ref[...].astype(F32) + a2_ref[...].astype(F32) + a3_ref[...].astype(F32)
    grad = total.astype(BF16)
    grad_ref[...] = grad
    grad_t = grad.astype(F32).T.astype(BF16)
    grad_t_ref[...] = grad_t
    here = lax.axis_index("dp")
    n_seq, _, cols = send_ref.shape
    for s in range(n_seq):
        away = pl.multiple_of(((1 - here) * n_seq + s) * cols, cols)
        send_ref[s] = mm(grad_t, tokens_ref[:, pl.ds(away, cols)]).astype(BF16)


def home_kernel(grad_t_ref, tokens_ref, keep_ref):
    here = lax.axis_index("dp")
    n_seq, _, cols = keep_ref.shape
    for s in range(n_seq):
        home = pl.multiple_of((here * n_seq + s) * cols, cols)
        keep_ref[s] = mm(grad_t_ref[...], tokens_ref[:, pl.ds(home, cols)])


def weight_away(n_seq, groups, tokens):
    length, depth = tokens.shape
    two_n = groups[0].shape[1]
    cols = depth // (2 * n_seq)
    return pl.pallas_call(
        away_kernel,
        name="weight_away",
        in_specs=[VMEM_SPEC] * 5,
        out_specs=[VMEM_SPEC] * 3,
        out_shape=[
            jax.ShapeDtypeStruct((length, two_n), BF16),
            jax.ShapeDtypeStruct((two_n, length), BF16),
            jax.ShapeDtypeStruct((n_seq, two_n, cols), BF16),
        ],
        compiler_params=LIMIT,
        cost_estimate=pl.CostEstimate(flops=length * two_n * depth, bytes_accessed=2 << 20, transcendentals=0),
    )(*groups, tokens)


def weight_home(n_seq, grad_t, tokens):
    length, depth = tokens.shape
    two_n = grad_t.shape[0]
    cols = depth // (2 * n_seq)
    return pl.pallas_call(
        home_kernel,
        name="weight_home",
        in_specs=[VMEM_SPEC] * 2,
        out_specs=VMEM_SPEC,
        out_shape=jax.ShapeDtypeStruct((n_seq, two_n, cols), F32),
        compiler_params=LIMIT,
        cost_estimate=pl.CostEstimate(flops=length * two_n * depth, bytes_accessed=2 << 20, transcendentals=0),
    )(grad_t, tokens)


def pair_kernel(keep_ref, got_ref, own_ref, s1_ref, s2_ref, s3_ref):
    here = lax.axis_index("seq")
    own_ref[...] = keep_ref[here] + got_ref[here].astype(F32)
    for k, ref in ((1, s1_ref), (2, s2_ref), (3, s3_ref)):
        at = here ^ k
        ref[...] = (keep_ref[at] + got_ref[at].astype(F32)).astype(BF16)


def pair_sum(keep, got):
    _, two_n, cols = keep.shape
    small = jax.ShapeDtypeStruct((two_n, cols), BF16)
    return pl.pallas_call(
        pair_kernel,
        name="pair_sum",
        compiler_params=LIMIT,
        in_specs=[VMEM_SPEC, VMEM_SPEC],
        out_specs=[VMEM_SPEC] * 4,
        out_shape=[jax.ShapeDtypeStruct((two_n, cols), F32), small, small, small],
    )(keep, got)


def final_kernel(scale, own_ref, r3_ref, r2_ref, r1_ref, out_ref):
    total = own_ref[...] + r1_ref[...].astype(F32) + r2_ref[...].astype(F32) + r3_ref[...].astype(F32)
    out_ref[...] = total.T * scale


def final_sum(scale, own, r3, r2, r1):
    two_n, cols = own.shape
    return pl.pallas_call(
        functools.partial(final_kernel, scale),
        name="final_sum",
        compiler_params=LIMIT,
        in_specs=[VMEM_SPEC] * 4,
        out_specs=VMEM_SPEC,
        out_shape=jax.ShapeDtypeStruct((cols, two_n), F32),
    )(own, r3, r2, r1)


def input_kernel(grad_ref, w_ref, out_ref):
    out_ref[...] = mm_t(grad_ref[...], w_ref[...]).astype(BF16)


def input_grad(grad, w):
    length, two_n = grad.shape
    depth = w.shape[0]
    steps = 4
    chunk = length // steps
    return pl.pallas_call(
        input_kernel,
        name="input_grad",
        grid=(steps,),
        in_specs=[pl.BlockSpec((chunk, two_n), lambda i: (i, 0)), pl.BlockSpec((depth, two_n), lambda i: (0, 0))],
        out_specs=pl.BlockSpec((None, chunk, depth), lambda i: (0, i, 0)),
        out_shape=jax.ShapeDtypeStruct((1, length, depth), BF16),
        compiler_params=LIMIT,
        cost_estimate=pl.CostEstimate(flops=2 * length * two_n * depth, bytes_accessed=3 << 20, transcendentals=0),
    )(grad, w)


def swap(value, axis, k):
    return lax.ppermute(value, axis, [(i, i ^ k) for i in range(lax.axis_size(axis))])


def per_device(layer_input, head_values, dt_raw, w_bc, decay_rate, dt_bias, skip_gain, grad_y):
    n_seq, n_head, n_dp = lax.axis_size("seq"), lax.axis_size("head"), lax.axis_size("dp")
    length = layer_input.shape[1]
    two_n = w_bc.shape[1]
    bc, cb, rows, decs, spread, scaled, near, coef, pay1, pay2, pay3, x, g, tokens, w = block_states(
        n_seq, layer_input, head_values, grad_y, dt_raw, w_bc, decay_rate, dt_bias
    )
    direct = n_seq == 4
    if direct:
        received = [swap((pay1, pay2, pay3)[k - 1], "seq", k) for k in ORDER_A]
    else:
        received = scanned_generic(pay1, pay2, two_n)
    y_local, gv_local, gbc_local, queries = inside_chunks(
        x, g, bc, cb, rows, decs, spread, skip_gain
    )
    group, before, after = group_sums(direct, received, near, coef, scaled, gbc_local)
    total_tokens = n_dp * n_seq * length
    if direct and n_dp == 2 and n_head == 4:
        others = [swap(group, "head", k) for k in ORDER_B[::-1]]
        y_out, grad_values = add_carries(before, after, queries, y_local, gv_local)
        *others, y_out = lax.optimization_barrier((*others, y_out))
        groups = [group, *others]
        grad_bc, grad_t, send = weight_away(n_seq, groups, tokens)
        got = swap(send, "dp", 1)
        keep = weight_home(n_seq, grad_t, tokens)
        own, s1, s2, s3 = pair_sum(keep, got)
        sums = [swap((s1, s2, s3)[k - 1], "seq", k) for k in ORDER_C]
        grad_w_bc = final_sum(1.0 / total_tokens, own, *sums)
    else:
        y_out, grad_values = add_carries(before, after, queries, y_local, gv_local)
        grad_bc = lax.psum(group.astype(F32), "head").astype(BF16)
        part = jnp.einsum("td,tk->dk", tokens, grad_bc, preferred_element_type=F32)
        grad_w_bc = lax.psum_scatter(part, ("dp", "seq"), scatter_dimension=0, tiled=True) / total_tokens
    grad_input = input_grad(grad_bc, w)
    return y_out, grad_values, grad_input, grad_w_bc


def solution(mesh):
    in_specs = (
        P("dp", "seq", None),
        P("dp", "seq", "head"),
        P("dp", "head", "seq"),
        P(),
        P("head"),
        P("head"),
        P("head"),
        P("dp", "seq", "head"),
    )
    out_specs = (
        P("dp", "seq", "head"),
        P("dp", "seq", "head"),
        P("dp", "seq", None),
        P(("dp", "seq"), None),
    )
    return jax.shard_map(per_device, mesh=mesh, in_specs=in_specs, out_specs=out_specs, check_vma=False)
```
